32 devices in a mesh: dp: 8 (over z, x), head: 4 (over y, core).
Axes of the slice: x: 2, y: 2, z: 4, core: 2. Of those that a mesh axis runs over, the one named last changes fastest.
Arguments:
- tokens: bfloat16 [8192, 768], P(('dp', 'head')), may hold values from -6 to 6
- cotangent: bfloat16 [8192, 768], P(('dp', 'head')), may hold values from -6 to 6
- segments: int32 [8, 1024], P('dp'), may hold values from -1 to 169, as said below
- attention_master: float32 [768, 3072], P('dp')
- feedforward_master: float32 [768, 6144], P('dp'), may hold values from -0.21875 to 0.21875
- vector_master: float32 [12, 768], P(None, 'dp')
- attention_moment: float32 [768, 3072], P('dp'), may hold values from -0.0024414062 to 0.0024414062
- feedforward_moment: float32 [768, 6144], P('dp'), may hold values from -0.0024414062 to 0.0024414062
- vector_moment: float32 [12, 768], P(None, 'dp'), may hold values from -0.0024414062 to 0.0024414062
- attention_second: float32 [768, 3072], P('dp'), may hold values from 1.4110135e-07 to 5.644054e-07
- feedforward_second: float32 [768, 6144], P('dp'), may hold values from 1.4110135e-07 to 5.644054e-07
- vector_second: float32 [12, 768], P(None, 'dp'), may hold values from 1.4110135e-07 to 5.644054e-07
- attention_teacher: float32 [768, 3072], P('dp'), may hold values from -0.21875 to 0.21875
- feedforward_teacher: float32 [768, 6144], P('dp'), may hold values from -0.21875 to 0.21875
- vector_teacher: float32 [12, 768], P(None, 'dp')
Outputs:
- block_output: bfloat16 [8192, 768], P(('dp', 'head'))
- input_gradient: float32 [8192, 768], P(('dp', 'head'))
- gradient_norm: float32 [], replicated
- new_attention_master: float32 [768, 3072], P('dp')
- new_feedforward_master: float32 [768, 6144], P('dp')
- new_vector_master: float32 [12, 768], P(None, 'dp')
- new_attention_moment: float32 [768, 3072], P('dp')
- new_feedforward_moment: float32 [768, 6144], P('dp')
- new_vector_moment: float32 [12, 768], P(None, 'dp')
- new_attention_second: float32 [768, 3072], P('dp')
- new_feedforward_second: float32 [768, 6144], P('dp')
- new_vector_second: float32 [12, 768], P(None, 'dp')
- new_attention_teacher: float32 [768, 3072], P('dp')
- new_feedforward_teacher: float32 [768, 6144], P('dp')
- new_vector_teacher: float32 [12, 768], P(None, 'dp')
- attention_copy: bfloat16 [768, 3072], P('dp')
- feedforward_copy: bfloat16 [768, 6144], P('dp')
- vector_copy: bfloat16 [12, 768], P(None, 'dp')
The draws below stay inside these ranges and needn't reach their ends.
Inputs may be any that keep to these rules, and one draw needn't show every extreme that they name: `segments`: in each pack, segment numbers start at 0 and rise by one from image to image; an image holds 2 + p * p tokens for some p from 2 to 12; -1 marks padding at the end of the pack, one token of it or more. In every draw one pack holds only images of 2 x 2 patches, as many as fit, so that its last image number is the largest possible.
All inputs are finite; a program needn't handle non-finite values.
Results may differ from the reference program's by a relative error of at most 0.012.
The reference program's roundings to bfloat16 on the way count: a program that leaves them out, or rounds other values in their place, can miss the bound.
Values may be sent and summed in bfloat16 or wider, within the bound.
No kernel may reach another device: no remote copies, remote signals or barrier semaphores. Data moves between devices by JAX's collectives and lax.ppermute only.
A program may use at most 192 MiB of HBM per device.

```python
import math
import jax
import jax.numpy as jnp
from jax import lax

D = 768
HEADS = 12
HEAD_DIM = 64
FF = 3072
LEN = 1024
PMAX = 12
ADAM_STEP = 3
SEQS = 8
TOKENS = 8192
PARAMS = 7087104


def draw_segments(key, part):
    most_images = LEN // 6 + 1
    key_sizes = jax.random.fold_in(key, 5)
    key_pick = jax.random.fold_in(key, 7)
    patches = jax.random.randint(key_sizes, (SEQS, most_images), 2, PMAX + 1)
    chosen = jax.random.randint(key_pick, (), 0, SEQS)
    rows = jnp.arange(SEQS, dtype=jnp.int32)
    patches = jnp.where((rows == chosen)[:, None], 2, patches)
    lengths = patches * patches + 2
    bounds = jnp.cumsum(lengths, axis=1)
    fitting = bounds <= LEN - 1
    filled = jnp.max(jnp.where(fitting, bounds, 0), axis=1)
    places = jnp.arange(LEN, dtype=jnp.int32)
    numbers = jnp.sum((bounds[:, None, :] <= places[None, :, None]).astype(jnp.int32), axis=2)
    return jnp.where(places[None, :] < filled[:, None], numbers, -1).astype(jnp.int32)


def draw_attention_master(key, part):
    base = jax.random.normal(key, (D, 4 * D), jnp.float32) * (1.0 / math.sqrt(D))
    columns = jnp.arange(4 * D)
    return base * jnp.where(columns >= 3 * D, 4.0, 1.0)


def vector_rows(key, noise_salt, gain_salt):
    key_noise = jax.random.fold_in(key, noise_salt)
    key_gain = jax.random.fold_in(key, gain_salt)
    noise = jax.random.normal(key_noise, (12, D), jnp.float32) * 0.2
    gains = jax.random.uniform(key_gain, (12, D), jnp.float32, minval=0.6, maxval=1.4)
    row_numbers = jnp.arange(12)[:, None]
    gain_rows = (row_numbers == 0) | (row_numbers == 5)
    return jnp.where(gain_rows, gains, noise)


def draw_vector_master(key, part):
    return vector_rows(key, 11, 23)


def draw_vector_teacher(key, part):
    return vector_rows(key, 31, 43)


def level_of(key, dims, pieces, low, top_value):
    def one(dim, blocks):
        steps = jax.random.uniform(jax.random.fold_in(jax.random.fold_in(key, 6), dim), (blocks,), jnp.float32, low / len(pieces), top_value / len(pieces))
        return jnp.repeat(jnp.exp(steps), dims[dim] // blocks).reshape((-1,) + (1,) * (len(dims) - dim - 1))

    loudness = one(*pieces[0])
    for cut in pieces[1:]:
        loudness = loudness * one(*cut)
    return loudness


def centred(stream_key, extent, scale, reach, split=(), kind=jnp.bfloat16):
    result = scale * jax.random.normal(stream_key, extent, jnp.float32)
    if split:
        result = result * level_of(stream_key, extent, split, -0.22, 0.18)
    return jnp.clip(result, -reach, reach).astype(kind)


def setup_inputs(seed: int = 0) -> dict:
    arg_keys = jax.random.split(jax.random.key(seed), 16)
    return {
        "tokens": centred(arg_keys[0], (TOKENS, D), 1.0, 6.0, ((0, 32),)),
        "cotangent": centred(arg_keys[1], (TOKENS, D), 1.0, 6.0, ((0, 32),)),
        "segments": draw_segments(jax.random.fold_in(arg_keys[15], 71), 0),
        "attention_master": draw_attention_master(jax.random.fold_in(arg_keys[15], 71), 0),
        "feedforward_master": centred(arg_keys[4], (D, 2 * FF), D ** -0.5, 0.21875, ((0, 8),), jnp.float32),
        "vector_master": draw_vector_master(jax.random.fold_in(arg_keys[15], 71), 0),
        "attention_moment": centred(arg_keys[6], (D, 4 * D), PARAMS ** -0.5, 0.0024414062, ((0, 8),), jnp.float32),
        "feedforward_moment": centred(arg_keys[7], (D, 2 * FF), PARAMS ** -0.5, 0.0024414062, ((0, 8),), jnp.float32),
        "vector_moment": centred(arg_keys[8], (12, D), PARAMS ** -0.5, 0.0024414062, ((1, 8),), jnp.float32),
        "attention_second": jnp.clip(jnp.exp(math.log(5.644054112963204e-07) - 1.3862944 * jax.random.uniform(arg_keys[9], (D, 4 * D), jnp.float32) ** level_of(arg_keys[9], (D, 4 * D), ((0, 8),), -0.2, 0.2)), 1.411013528240801e-07, 5.644054112963204e-07),
        "feedforward_second": jnp.clip(jnp.exp(math.log(5.644054112963204e-07) - 1.3862944 * jax.random.uniform(arg_keys[10], (D, 2 * FF), jnp.float32) ** level_of(arg_keys[10], (D, 2 * FF), ((0, 8),), -0.2, 0.2)), 1.411013528240801e-07, 5.644054112963204e-07),
        "vector_second": jnp.clip(jnp.exp(math.log(5.644054112963204e-07) - 1.3862944 * jax.random.uniform(arg_keys[11], (12, D), jnp.float32) ** level_of(arg_keys[11], (12, D), ((1, 8),), -0.2, 0.2)), 1.411013528240801e-07, 5.644054112963204e-07),
        "attention_teacher": centred(arg_keys[12], (D, 4 * D), D ** -0.5, 0.21875, ((0, 8),), jnp.float32),
        "feedforward_teacher": centred(arg_keys[13], (D, 2 * FF), D ** -0.5, 0.21875, ((0, 8),), jnp.float32),
        "vector_teacher": draw_vector_teacher(jax.random.fold_in(arg_keys[15], 71), 0),
    }


norm_epsilon = 1e-06
beta_one = 0.5
beta_two = 0.5
adam_epsilon = 1e-08
learn_rate = 0.05
weight_decay = 0.05
teacher_keep = 0.8
clip_limit = 1.0
masked_score = -1e+30

@jax.custom_vjp
def low(v):
    return lax.optimization_barrier(v.astype(jnp.bfloat16)).astype(jnp.float32)

@jax.custom_vjp
def low_back(v):
    return v

def low_keep(v):
    return (low(v), None)

def low_pass(kept, grad):
    return (grad,)

def back_keep(v):
    return (v, None)

def back_low(kept, grad):
    return (low(grad),)
low.defvjp(low_keep, low_pass)
low_back.defvjp(back_keep, back_low)

def layer_norm(values, gain, shift):
    center = lax.optimization_barrier(jnp.mean(values, axis=-1, keepdims=True))
    deviate = values - center
    spread = lax.optimization_barrier(jnp.mean(deviate * deviate, axis=-1, keepdims=True))
    return deviate * lax.rsqrt(spread + norm_epsilon) * gain + shift

def gelu_exact(values):
    return 0.5 * values * (1.0 + lax.erf(values * 0.7071067811865476))

def product(left, right):
    return jnp.dot(left, right, precision=lax.Precision.HIGHEST, preferred_element_type=jnp.float32)

def adam_update(master, moment, second, teacher, gradient, factor, decay_rate):
    clipped = gradient * factor
    moment_new = beta_one * moment + (1.0 - beta_one) * clipped
    second_new = beta_two * second + (1.0 - beta_two) * clipped * clipped
    scale_one = 1.0 - beta_one ** ADAM_STEP
    scale_two = 1.0 - beta_two ** ADAM_STEP
    update = moment_new / scale_one / (jnp.sqrt(second_new / scale_two) + adam_epsilon)
    master_new = master * (1.0 - learn_rate * decay_rate) - learn_rate * update
    teacher_new = teacher_keep * teacher + (1.0 - teacher_keep) * master_new
    return (master_new, moment_new, second_new, teacher_new)

def layer_block(attention_weight, forward_weight, vector_weight, inputs, segment_ids):
    norm_gain = vector_weight[0]
    norm_shift = vector_weight[1]
    query_bias = vector_weight[2]
    value_bias = vector_weight[3]
    output_bias = vector_weight[4]
    second_gain = vector_weight[5]
    second_shift = vector_weight[6]
    down_bias = vector_weight[7]
    up_bias = vector_weight[8:12].reshape(-1)
    w_qkv = attention_weight[:, :3 * D]
    w_out = attention_weight[:, 3 * D:]
    w_up = forward_weight[:, :FF]
    w_down = forward_weight[:, FF:]
    normed = low(layer_norm(inputs, norm_gain, norm_shift))
    qkv_bias = jnp.concatenate([query_bias, jnp.zeros_like(query_bias), value_bias])
    projected = low_back(low(product(normed, w_qkv) + qkv_bias))
    queries = projected[:, :D].reshape(LEN, HEADS, HEAD_DIM)
    key_rows = projected[:, D:2 * D].reshape(LEN, HEADS, HEAD_DIM)
    value_rows = projected[:, 2 * D:].reshape(LEN, HEADS, HEAD_DIM)
    raw_score = jnp.einsum('qhd,khd->hqk', queries, key_rows, precision=lax.Precision.HIGHEST) * HEAD_DIM ** (-0.5)
    same_image = segment_ids[:, None] == segment_ids[None, :]
    scores = jnp.where(same_image[None], low_back(raw_score), masked_score)
    largest = lax.optimization_barrier(jnp.max(scores, axis=-1, keepdims=True))
    powered = jnp.exp(scores - largest)
    attention = powered / lax.optimization_barrier(jnp.sum(powered, axis=-1, keepdims=True))
    attended = jnp.einsum('hqk,khd->qhd', low(attention), value_rows, precision=lax.Precision.HIGHEST).reshape(LEN, D)
    attended = low_back(low(attended))
    resid = inputs + low_back(product(attended, w_out) + output_bias)
    normed_two = low(layer_norm(resid, second_gain, second_shift))
    pre_act = low_back(product(normed_two, w_up) + up_bias)
    activated = low(gelu_exact(pre_act))
    branch_out = low_back(jnp.dot(activated, w_down.T, precision=lax.Precision.HIGHEST) + down_bias)
    return resid + branch_out

def reference(tokens, cotangent, segments, attention_master, feedforward_master, vector_master, attention_moment, feedforward_moment, vector_moment, attention_second, feedforward_second, vector_second, attention_teacher, feedforward_teacher, vector_teacher):
    sequences = tokens.astype(jnp.float32).reshape(SEQS, LEN, D)

    def network(attention_weight, forward_weight, vector_weight, packs):
        attention_low = low(attention_weight)
        forward_low = low(forward_weight)
        vector_low = low(vector_weight)
        rerun_block = jax.checkpoint(layer_block)

        def scan_step(carry, packed):
            return (carry, rerun_block(attention_low, forward_low, vector_low, packed[0], packed[1]))
        _, results = lax.scan(scan_step, jnp.zeros((), jnp.float32), (packs, segments))
        return results
    results, pull_back = jax.vjp(network, attention_master, feedforward_master, vector_master, sequences)
    grad_attention, grad_forward, grad_vector, grad_inputs = pull_back(cotangent.astype(jnp.float32).reshape(SEQS, LEN, D))
    total = jnp.sum(grad_attention * grad_attention) + jnp.sum(grad_forward * grad_forward) + jnp.sum(grad_vector * grad_vector)
    gradient_norm = jnp.sqrt(total)
    factor = jnp.minimum(1.0, clip_limit / (gradient_norm + 1e-06))
    attention_new = adam_update(attention_master, attention_moment, attention_second, attention_teacher, grad_attention, factor, weight_decay)
    forward_new = adam_update(feedforward_master, feedforward_moment, feedforward_second, feedforward_teacher, grad_forward, factor, weight_decay)
    vector_new = adam_update(vector_master, vector_moment, vector_second, vector_teacher, grad_vector, factor, 0.0)
    return (results.reshape(TOKENS, D).astype(jnp.bfloat16), grad_inputs.reshape(TOKENS, D), gradient_norm, attention_new[0], forward_new[0], vector_new[0], attention_new[1], forward_new[1], vector_new[1], attention_new[2], forward_new[2], vector_new[2], attention_new[3], forward_new[3], vector_new[3], attention_new[0].astype(jnp.bfloat16), forward_new[0].astype(jnp.bfloat16), vector_new[0].astype(jnp.bfloat16))
```

```python
import functools

import jax
import jax.numpy as jnp
from jax import lax
from jax.experimental import pallas as pl
from jax.experimental.pallas import tpu as pltpu
from jax.sharding import PartitionSpec as P

HEADS = 12
HEAD_DIM = 64
ADAM_STEP = 3

norm_epsilon = 1e-06
beta_one = 0.5
beta_two = 0.5
adam_epsilon = 1e-08
learn_rate = 0.05
weight_decay = 0.05
teacher_keep = 0.8
clip_limit = 1.0
masked_score = -1e30

BF = jnp.bfloat16
F32 = jnp.float32


def dot_rows(left, right):
    return lax.dot_general(left, right, (((0,), (0,)), ((), ())), preferred_element_type=F32)


def dot_cols(left, right):
    return lax.dot_general(left, right, (((1,), (1,)), ((), ())), preferred_element_type=F32)


def dot(left, right):
    return jnp.dot(left, right, preferred_element_type=F32)


def normalize(values):
    center = jnp.mean(values, axis=-1, keepdims=True)
    deviate = values - center
    spread = jnp.mean(deviate * deviate, axis=-1, keepdims=True)
    inverse = lax.rsqrt(spread + norm_epsilon)
    return deviate * inverse, inverse


def norm_back(hat, inverse, gain, grad):
    scaled = grad * gain
    mean_one = jnp.mean(scaled, axis=-1, keepdims=True)
    mean_two = jnp.mean(scaled * hat, axis=-1, keepdims=True)
    return inverse * (scaled - mean_one - hat * mean_two)


def head_lanes(index, shape):
    lane = lax.broadcasted_iota(jnp.int32, shape, 1)
    return (lane >= index * HEAD_DIM) & (lane < (index + 1) * HEAD_DIM)


def attend_kernel(per, q_ref, k_ref, v_ref, seg_q_ref, seg_k_ref, out_ref):
    same = seg_q_ref[...] == seg_k_ref[...]
    queries = q_ref[...] * jnp.asarray(HEAD_DIM**-0.5, BF)
    keys = k_ref[...]
    values = v_ref[...]
    result = jnp.zeros(out_ref.shape, F32)
    for head in range(per):
        lanes = head_lanes(head, queries.shape)
        score = dot_cols(jnp.where(lanes, queries, jnp.zeros_like(queries)), keys)
        score = jnp.where(same, score, masked_score)
        largest = jnp.max(score, axis=1, keepdims=True)
        power = jnp.exp(score - largest)
        total = jnp.sum(power, axis=1, keepdims=True)
        chance = (power * (1.0 / total)).astype(BF)
        result = jnp.where(lanes, dot(chance, values), result)
    out_ref[...] = result.astype(BF)


def attend(qkv, segments, per):
    length = qkv.shape[0]
    cols = per * HEAD_DIM
    block = 256
    queries, keys, values = qkv[:, :cols], qkv[:, cols : 2 * cols], qkv[:, 2 * cols :]
    return pl.pallas_call(
        functools.partial(attend_kernel, per),
        out_shape=jax.ShapeDtypeStruct((length, cols), BF),
        grid=(length // block,),
        in_specs=[
            pl.BlockSpec((block, cols), lambda i: (i, 0)),
            pl.BlockSpec((length, cols), lambda i: (0, 0)),
            pl.BlockSpec((length, cols), lambda i: (0, 0)),
            pl.BlockSpec((block, 1), lambda i: (i, 0)),
            pl.BlockSpec((1, length), lambda i: (0, 0)),
        ],
        out_specs=pl.BlockSpec((block, cols), lambda i: (i, 0)),
        compiler_params=pltpu.CompilerParams(vmem_limit_bytes=48 * 2**20),
        name="attend",
    )(queries, keys, values, segments.reshape(length, 1), segments)


def attend_back_kernel(
    per, q_ref, k_ref, v_ref, do_ref, seg_q_ref, seg_k_ref, dq_ref, dk_ref, dv_ref, k_acc, v_acc
):
    step = pl.program_id(0)

    @pl.when(step == 0)
    def _():
        k_acc[...] = jnp.zeros_like(k_acc)
        v_acc[...] = jnp.zeros_like(v_acc)

    same = seg_k_ref[...] == seg_q_ref[...]
    queries = q_ref[...] * jnp.asarray(HEAD_DIM**-0.5, BF)
    grads = do_ref[...]
    keys = k_ref[...]
    values = v_ref[...]
    grad_query = jnp.zeros(dq_ref.shape, F32)
    for head in range(per):
        lanes = head_lanes(head, queries.shape)
        query = jnp.where(lanes, queries, jnp.zeros_like(queries))
        grad = jnp.where(lanes, grads, jnp.zeros_like(grads))
        score = jnp.where(same, dot_cols(keys, query), masked_score)
        largest = jnp.max(score, axis=0, keepdims=True)
        power = jnp.exp(score - largest)
        total = jnp.sum(power, axis=0, keepdims=True)
        chance = power * (1.0 / total)
        grad_chance = dot_cols(values, grad)
        inner = jnp.sum(chance * grad_chance, axis=0, keepdims=True)
        grad_score = (chance * (grad_chance - inner)).astype(BF)
        k_acc[...] += dot(grad_score, query)
        v_acc[...] += dot(chance.astype(BF), grad)
        grad_query = jnp.where(lanes, dot_rows(grad_score, keys), grad_query)
    dq_ref[...] = (grad_query * HEAD_DIM**-0.5).astype(BF)

    @pl.when(step == pl.num_programs(0) - 1)
    def _():
        dk_ref[...] = k_acc[...].astype(BF)
        dv_ref[...] = v_acc[...].astype(BF)


def attend_back(qkv, grad_out, segments, per):
    length = qkv.shape[0]
    cols = per * HEAD_DIM
    block = 256
    queries, keys, values = qkv[:, :cols], qkv[:, cols : 2 * cols], qkv[:, 2 * cols :]
    whole = pl.BlockSpec((length, cols), lambda i: (0, 0))
    part = pl.BlockSpec((block, cols), lambda i: (i, 0))
    shape = jax.ShapeDtypeStruct((length, cols), BF)
    return pl.pallas_call(
        functools.partial(attend_back_kernel, per),
        out_shape=(shape, shape, shape),
        grid=(length // block,),
        in_specs=[
            part,
            whole,
            whole,
            part,
            pl.BlockSpec((1, block), lambda i: (0, i)),
            pl.BlockSpec((length, 1), lambda i: (0, 0)),
        ],
        out_specs=(part, whole, whole),
        scratch_shapes=[pltpu.VMEM((length, cols), F32), pltpu.VMEM((length, cols), F32)],
        compiler_params=pltpu.CompilerParams(vmem_limit_bytes=48 * 2**20),
        name="attend_back",
    )(queries, keys, values, grad_out, segments, segments.reshape(length, 1))


def adam_update(master, moment, second, teacher, gradient, factor, decay_rate):
    clipped = gradient * factor
    moment_new = beta_one * moment + (1.0 - beta_one) * clipped
    second_new = beta_two * second + (1.0 - beta_two) * clipped * clipped
    scale_one = 1.0 - beta_one**ADAM_STEP
    scale_two = 1.0 - beta_two**ADAM_STEP
    update = moment_new / scale_one / (jnp.sqrt(second_new / scale_two) + adam_epsilon)
    master_new = master * (1.0 - learn_rate * decay_rate) - learn_rate * update
    teacher_new = teacher_keep * teacher + (1.0 - teacher_keep) * master_new
    return (master_new, moment_new, second_new, teacher_new)


PAIR_ROW = [[0, 2], [1, 3]]
PAIR_CORE = [[0, 1], [2, 3]]


def gather_head(part):
    rows = lax.all_gather(part, "head", axis=0, axis_index_groups=PAIR_ROW)
    both = lax.all_gather(rows, "head", axis=0, axis_index_groups=PAIR_CORE)
    return [both[0, 0], both[1, 0], both[0, 1], both[1, 1]]


def swap(part, bit):
    return lax.ppermute(part, "head", [(i, i ^ bit) for i in range(4)])


def scatter_head(partial, member):
    rows, width = partial.shape
    row, core = member // 2, member % 2
    blocks = partial.reshape(2, 2, rows // 4, width)
    keep = lax.dynamic_index_in_dim(blocks, core, 1, keepdims=False)
    send = lax.dynamic_index_in_dim(blocks, 1 - core, 1, keepdims=False).astype(BF)
    half = keep + swap(send, 1).astype(F32)
    keep = lax.dynamic_index_in_dim(half, row, 0, keepdims=False)
    send = lax.dynamic_index_in_dim(half, 1 - row, 0, keepdims=False).astype(BF)
    return keep + swap(send, 2).astype(F32)


def local(
    tokens,
    cotangent,
    segments,
    attention_master,
    feedforward_master,
    vector_master,
    attention_moment,
    feedforward_moment,
    vector_moment,
    attention_second,
    feedforward_second,
    vector_second,
    attention_teacher,
    feedforward_teacher,
    vector_teacher,
):
    width = tokens.shape[1]
    rows = tokens.shape[0]
    owners = lax.axis_size("dp")
    groups = lax.axis_size("head")
    member = lax.axis_index("head")
    hidden = feedforward_master.shape[1] // 2
    per = HEADS // groups
    cols = per * HEAD_DIM
    part = hidden // groups
    owned = attention_master.shape[0]

    def own_cols(array, start, size):
        return lax.dynamic_slice_in_dim(array, start + member * size, size, axis=1)

    low_qkv = jnp.concatenate(
        [own_cols(attention_master, i * width, cols) for i in range(3)], axis=1
    ).astype(BF)
    w_qkv = lax.all_gather(low_qkv, "dp", axis=0, tiled=True)
    vector_low = lax.all_gather(vector_master.astype(BF), "dp", axis=1, tiled=True)
    low_rest = jnp.concatenate(
        [
            attention_master[:, 3 * width :],
            own_cols(feedforward_master, 0, part),
            own_cols(feedforward_master, hidden, part),
        ],
        axis=1,
    ).astype(BF)
    w_rest = lax.all_gather(low_rest, "dp", axis=0, tiled=True)
    w_out = w_rest[:, :width]
    w_up = w_rest[:, width : width + part]
    w_down = w_rest[:, width + part :]

    vector_full = vector_low.astype(F32)
    gain_one, shift_one = vector_full[0], vector_full[1]
    output_bias, gain_two, shift_two, down_bias = (vector_full[i] for i in (4, 5, 6, 7))
    query_bias = lax.dynamic_slice_in_dim(vector_full[2], member * cols, cols)
    value_bias = lax.dynamic_slice_in_dim(vector_full[3], member * cols, cols)
    up_bias = lax.dynamic_index_in_dim(vector_full[8:12], member, 0, keepdims=False)

    inputs = jnp.concatenate(gather_head(tokens), axis=0).astype(F32)
    grads = jnp.concatenate(gather_head(cotangent), axis=0)

    hat_one, inverse_one = normalize(inputs)
    normed = (hat_one * gain_one + shift_one).astype(BF)
    qkv_bias = jnp.concatenate([query_bias, jnp.zeros_like(query_bias), value_bias])
    qkv = (dot(normed, w_qkv) + qkv_bias).astype(BF)
    attended = attend(qkv, segments, per)
    mixed = jnp.concatenate(gather_head(attended), axis=1)
    resid = inputs + dot(mixed, w_out) + output_bias
    hat_two, inverse_two = normalize(resid)
    normed_two = (hat_two * gain_two + shift_two).astype(BF)
    pre_act = dot(normed_two, w_up) + up_bias
    phi = 0.5 * (1.0 + lax.erf(pre_act * 0.7071067811865476))
    activated = (pre_act * phi).astype(BF)
    slope = phi + pre_act * (jnp.exp(-0.5 * pre_act * pre_act) * 0.3989422804014327)
    grad_pre = (dot(grads, w_down) * slope).astype(BF)
    branch = scatter_head(dot_cols(activated, w_down), member)

    def own_rows(array):
        return lax.dynamic_slice_in_dim(array, member * rows, rows, axis=0)

    resid_own = own_rows(resid)
    block_output = (resid_own + branch + down_bias).astype(BF)

    grad_down = dot_rows(grads, activated)
    grad_up = dot_rows(normed_two, grad_pre)
    grad_up_bias = jnp.sum(grad_pre.astype(F32), axis=0)
    grad_normed_two = dot_cols(grad_pre, w_up)
    grad_gain_two = jnp.sum(grad_normed_two * hat_two, axis=0)
    grad_shift_two = jnp.sum(grad_normed_two, axis=0)
    grad_two = scatter_head(grad_normed_two, member)
    grad_resid = cotangent.astype(F32) + norm_back(
        own_rows(hat_two), own_rows(inverse_two), gain_two, grad_two
    )
    grad_branch = grad_resid.astype(BF)
    grad_down_bias = jnp.sum(cotangent.astype(F32), axis=0)
    grad_out_bias = jnp.sum(grad_branch.astype(F32), axis=0)
    branch_all = jnp.concatenate(gather_head(grad_branch), axis=0)
    grad_out = dot_rows(mixed, lax.dynamic_slice_in_dim(branch_all, member * cols, cols, axis=1))
    w_out_own = lax.dynamic_slice_in_dim(w_out, member * cols, cols, axis=0)
    grad_mixed = dot_cols(branch_all, w_out_own).astype(BF)
    grad_query, grad_key, grad_value = attend_back(qkv, grad_mixed, segments, per)
    grad_qkv = jnp.concatenate([grad_query, grad_key, grad_value], axis=1)
    grad_qkv_weight = dot_rows(normed, grad_qkv)
    grad_query_bias = jnp.sum(grad_query.astype(F32), axis=0)
    grad_value_bias = jnp.sum(grad_value.astype(F32), axis=0)
    grad_normed = dot_cols(grad_qkv, w_qkv)
    grad_gain_one = jnp.sum(grad_normed * hat_one, axis=0)
    grad_shift_one = jnp.sum(grad_normed, axis=0)
    grad_one = scatter_head(grad_normed, member)
    input_gradient = grad_resid + norm_back(
        own_rows(hat_one), own_rows(inverse_one), gain_one, grad_one
    )

    def place(piece):
        return lax.dynamic_update_slice_in_dim(jnp.zeros((width,), F32), piece, member * cols, 0)

    up_rows = lax.dynamic_update_slice_in_dim(
        jnp.zeros((groups, part), F32), grad_up_bias[None], member, 0
    )
    grad_vector = jnp.concatenate(
        [
            jnp.stack(
                [
                    grad_gain_one,
                    grad_shift_one,
                    place(grad_query_bias),
                    place(grad_value_bias),
                    grad_out_bias,
                    grad_gain_two,
                    grad_shift_two,
                    grad_down_bias,
                ]
            ),
            up_rows,
        ],
        axis=0,
    )

    sum_ff = lax.psum_scatter(
        jnp.concatenate([grad_up, grad_down], axis=1).astype(BF),
        "dp",
        scatter_dimension=0,
        tiled=True,
    )
    vector_high = grad_vector.astype(BF)
    vector_rest = (grad_vector - vector_high.astype(F32)).astype(BF)
    vector_pack = jnp.concatenate([vector_high, vector_rest], axis=0).T
    attention_pack = jnp.concatenate(
        [grad_qkv_weight.astype(BF), grad_out.astype(BF), vector_pack], axis=1
    )
    pieces = lax.all_to_all(
        attention_pack.reshape(owners, owned, -1), "dp", split_axis=0, concat_axis=0
    )
    sum_pack = jnp.sum(pieces.astype(F32), axis=0)
    sum_attention = sum_pack[:, : 4 * cols].astype(BF)
    sum_vector = sum_pack[:, 4 * cols : 4 * cols + 12] + sum_pack[:, 4 * cols + 12 :]

    vectors = gather_head(sum_vector)
    vector_grad = (vectors[0] + vectors[1] + vectors[2] + vectors[3]).T
    attention_parts = gather_head(sum_attention)
    attention_grad = jnp.concatenate(
        [item[:, i * cols : (i + 1) * cols] for i in range(4) for item in attention_parts], axis=1
    ).astype(F32)
    forward_parts = gather_head(sum_ff)
    forward_grad = jnp.concatenate(
        [item[:, i * part : (i + 1) * part] for i in range(2) for item in forward_parts], axis=1
    ).astype(F32)
    squares = (
        jnp.sum(attention_grad * attention_grad)
        + jnp.sum(forward_grad * forward_grad)
        + jnp.sum(vector_grad * vector_grad)
    )
    total = jnp.sum(
        lax.all_to_all(
            jnp.broadcast_to(squares, (owners, 8, 128)), "dp", split_axis=0, concat_axis=0
        )[:, 0, 0]
    )
    gradient_norm = jnp.sqrt(total)
    factor = jnp.minimum(1.0, clip_limit / (gradient_norm + 1e-06))
    attention_new = adam_update(
        attention_master,
        attention_moment,
        attention_second,
        attention_teacher,
        attention_grad,
        factor,
        weight_decay,
    )
    forward_new = adam_update(
        feedforward_master,
        feedforward_moment,
        feedforward_second,
        feedforward_teacher,
        forward_grad,
        factor,
        weight_decay,
    )
    vector_new = adam_update(
        vector_master, vector_moment, vector_second, vector_teacher, vector_grad, factor, 0.0
    )
    states = []
    for state in range(4):
        states += [attention_new[state], forward_new[state], vector_new[state]]
    return (
        block_output,
        input_gradient,
        gradient_norm,
        *states,
        attention_new[0].astype(BF),
        forward_new[0].astype(BF),
        vector_new[0].astype(BF),
    )


def solution(mesh):
    rows = P(("dp", "head"), None)
    shard = P("dp", None)
    vector = P(None, "dp")
    return jax.shard_map(
        local,
        mesh=mesh,
        in_specs=(rows, rows, shard) + (shard, shard, vector) * 4,
        out_specs=(rows, rows, P()) + (shard, shard, vector) * 5,
        check_vma=False,
    )
```

```python
import functools

import jax
import jax.numpy as jnp
import numpy as np
from jax import lax
from jax.experimental import pallas as pl
from jax.experimental.pallas import tpu as pltpu
from jax.sharding import PartitionSpec as P

HEADS = 12
HEAD_DIM = 64
ADAM_STEP = 3

norm_epsilon = 1e-06
beta_one = 0.5
beta_two = 0.5
adam_epsilon = 1e-08
learn_rate = 0.05
weight_decay = 0.05
teacher_keep = 0.8
clip_limit = 1.0
masked_score = -1e30

BF = jnp.bfloat16
F32 = jnp.float32


def dot_rows(left, right):
    return lax.dot_general(left, right, (((0,), (0,)), ((), ())), preferred_element_type=F32)


def dot_cols(left, right):
    return lax.dot_general(left, right, (((1,), (1,)), ((), ())), preferred_element_type=F32)


def dot(left, right):
    return jnp.dot(left, right, preferred_element_type=F32)


def normalize(values):
    center = jnp.mean(values, axis=-1, keepdims=True)
    deviate = values - center
    spread = jnp.mean(deviate * deviate, axis=-1, keepdims=True)
    inverse = lax.rsqrt(spread + norm_epsilon)
    return deviate * inverse, inverse


def norm_back(hat, inverse, gain, grad):
    scaled = grad * gain
    mean_one = jnp.mean(scaled, axis=-1, keepdims=True)
    mean_two = jnp.mean(scaled * hat, axis=-1, keepdims=True)
    return inverse * (scaled - mean_one - hat * mean_two)


def head_lanes(index, shape):
    lane = lax.broadcasted_iota(jnp.int32, shape, 1)
    return (lane >= index * HEAD_DIM) & (lane < (index + 1) * HEAD_DIM)


def unit_rows(rows, columns):
    row = lax.broadcasted_iota(jnp.int32, (rows, columns), 0)
    column = lax.broadcasted_iota(jnp.int32, (rows, columns), 1)
    return jnp.where(row == column, 1.0, 0.0).astype(BF)


def smem():
    return pl.BlockSpec(memory_space=pltpu.SMEM)


def vmem():
    return pl.BlockSpec(memory_space=pltpu.VMEM)


def whole(*shape):
    return pl.BlockSpec(shape, lambda *index: (0,) * len(shape))


def shaped(shape, kind):
    return jax.ShapeDtypeStruct(shape, kind)


def params(mebibytes):
    return pltpu.CompilerParams(vmem_limit_bytes=mebibytes * 2**20)


COST_SCALE = 1.0


def cost(microseconds):
    return pl.CostEstimate(
        flops=0, transcendentals=0, bytes_accessed=int(microseconds * COST_SCALE * 3.6e6)
    )


def pin(array):
    return pltpu.with_memory_space_constraint(array, pltpu.HBM)


def far_space():
    return pl.BlockSpec(memory_space=pltpu.HBM)


def run(
    kernel, name, outputs, inputs, microseconds, scratch=(), mebibytes=16, lazy=(), save=(), far=()
):
    single = not isinstance(outputs, tuple)
    outputs = [outputs] if single else list(outputs)
    lazy, save, far = list(lazy), list(save), list(far)
    count, produced, own = len(inputs), len(outputs), len(scratch)
    buffers = [pltpu.VMEM(inputs[i].shape, inputs[i].dtype) for i in lazy]
    buffers += [pltpu.VMEM(outputs[i].shape, outputs[i].dtype) for i in far]
    moves = len(lazy) + len(save) + len(far)
    if moves:
        buffers.append(pltpu.SemaphoreType.DMA((moves,)))

    def body(*refs):
        items = list(refs[: count + produced])
        saved = refs[count + produced : count + produced + len(save)]
        rest = refs[count + produced + len(save) :]
        inner, extra = rest[:own], rest[own:]
        copies, number = [], 0
        for j, i in enumerate(lazy):
            copies.append(pltpu.make_async_copy(refs[i], extra[j], extra[-1].at[number]))
            items[i] = extra[j]
            number += 1
        stores = []
        for j, i in enumerate(save):
            stores.append(pltpu.make_async_copy(refs[i], saved[j], extra[-1].at[number]))
            number += 1
        last = []
        for j, i in enumerate(far):
            buffer = extra[len(lazy) + j]
            last.append(pltpu.make_async_copy(buffer, refs[count + i], extra[-1].at[number]))
            items[count + i] = buffer
            number += 1
        for copy in copies + stores:
            copy.start()
        for copy in copies:
            copy.wait()
        kernel(*items, *inner)
        for copy in last:
            copy.start()
        for copy in stores + last:
            copy.wait()

    shapes = [pltpu.HBM(item.shape, item.dtype) if i in far else item for i, item in enumerate(outputs)]
    results = pl.pallas_call(
        body,
        out_shape=shapes + [pltpu.HBM(inputs[i].shape, inputs[i].dtype) for i in save],
        in_specs=[smem()] + [far_space() if i in lazy else vmem() for i in range(1, count)],
        out_specs=[far_space() if i in far else vmem() for i in range(produced)]
        + [far_space()] * len(save),
        scratch_shapes=list(scratch) + buffers,
        compiler_params=params(mebibytes),
        cost_estimate=cost(microseconds),
        name=name,
    )(*[pin(item) if i in lazy else item for i, item in enumerate(inputs)])
    return results[0] if single and not save else tuple(results)


GROUPS = 4


def pack_kernel(cols, scal, *refs):
    vector_ref, out_ref = refs[4:6]
    for side in range(2):

        @pl.when(scal[0] % 2 == side)
        def _():
            for i in range(4):
                out_ref[:, i * cols : (i + 1) * cols] = refs[i][
                    :, side * cols : (side + 1) * cols
                ].astype(BF)

    vector = vector_ref[...].astype(BF)
    out_ref[:, 4 * cols :] = dot_rows(vector, unit_rows(vector.shape[0], 128)).astype(BF)


def pack_attention(scal, attention, vector, cols):
    rows = attention.shape[0]

    def pair(i):
        return pl.BlockSpec((rows, 2 * cols), lambda step, scal: (0, 2 * i + scal[0] // 2))

    return pl.pallas_call(
        functools.partial(pack_kernel, cols),
        out_shape=shaped((rows, 4 * cols + 128), BF),
        grid_spec=pltpu.PrefetchScalarGridSpec(
            num_scalar_prefetch=1,
            grid=(1,),
            in_specs=[pair(i) for i in range(4)] + [whole(*vector.shape)],
            out_specs=whole(rows, 4 * cols + 128),
        ),
        compiler_params=params(8),
        cost_estimate=cost(1.5),
        name="pack_attention",
    )(scal, *[attention] * 4, vector)


def cast_kernel(scal, in_ref, out_ref):
    out_ref[...] = in_ref[...].astype(BF)


def pack_forward(scal, forward, part):
    rows = forward.shape[0]
    return pl.pallas_call(
        cast_kernel,
        out_shape=shaped((rows, 2 * part), BF),
        grid_spec=pltpu.PrefetchScalarGridSpec(
            num_scalar_prefetch=1,
            grid=(2,),
            in_specs=[pl.BlockSpec((rows, part), lambda i, scal: (0, GROUPS * i + scal[0]))],
            out_specs=pl.BlockSpec((rows, part), lambda i, scal: (0, i)),
        ),
        compiler_params=params(8),
        cost_estimate=cost(1.5),
        name="pack_forward",
    )(scal, forward)


def place_rows(scal, pieces, target):
    rows = pieces[0].shape[0]
    if len(pieces) == 1:
        target[...] = pieces[0][...]
        return
    for i, piece in enumerate(pieces):
        start = pl.multiple_of(scal[1 + i] * rows, rows)
        target[pl.ds(start, rows), :] = piece[...]


def place_members(scal, pieces, target):
    rows = pieces[0].shape[0]
    for i, piece in enumerate(pieces):
        start = pl.multiple_of((scal[0] ^ i) * rows, rows)
        target[pl.ds(start, rows), :] = piece[...]


def place_kernel(scal, *refs):
    place_members(scal, refs[0:4], refs[4])


def place_blocks(scal, blocks):
    rows, width = blocks[0].shape
    wide = shaped((GROUPS * rows, width), BF)
    return run(place_kernel, "place_blocks", wide, (scal, *blocks), 0.5, mebibytes=2)


def project_kernel(count, cols, scal, seg_ref, x_ref, *refs):
    pieces = refs[:count]
    q_ref, k_ref, v_ref, wq_ref, wk_ref, wv_ref, wo_ref, vec_ref, col_ref = refs[count : 9 + count]
    weights = refs[9 + count]
    place_rows(scal, pieces, weights)
    for i, ref in enumerate((wq_ref, wk_ref, wv_ref, wo_ref)):
        ref[...] = weights[:, i * cols : (i + 1) * cols]
    unit = unit_rows(16, 128)
    vec_ref[...] = dot_cols(unit, weights[:, 4 * cols :])
    start = pl.multiple_of(scal[0] * cols, cols)
    own = dot_cols(unit, weights[pl.ds(start, cols), 4 * cols :])
    query_bias, value_bias = own[2:3, :], own[3:4, :]
    gain, shift = vec_ref[0:1, :], vec_ref[1:2, :]
    numbers = jnp.broadcast_to(seg_ref[...].astype(F32), (8, seg_ref.shape[1])).astype(BF)
    col_ref[...] = dot_rows(numbers, unit_rows(8, 128))[:, 0:1].astype(jnp.int32)
    block = 256

    def step(i, carry):
        rows = pl.ds(pl.multiple_of(i * block, block), block)
        hat, _ = normalize(x_ref[rows, :].astype(F32))
        normed = (hat * gain + shift).astype(BF)
        q_ref[rows, :] = (dot(normed, wq_ref[...]) + query_bias).astype(BF)
        k_ref[rows, :] = dot(normed, wk_ref[...]).astype(BF)
        v_ref[rows, :] = (dot(normed, wv_ref[...]) + value_bias).astype(BF)
        return carry

    lax.fori_loop(0, x_ref.shape[0] // block, step, 0)


def project(scal, segments, x_all, pieces, cols):
    length, width = x_all.shape
    outputs = (
        (shaped((length, cols), BF),) * 3
        + (shaped((width, cols), BF),) * 4
        + (shaped((16, width), F32), shaped((length, 1), jnp.int32))
    )
    return run(
        functools.partial(project_kernel, len(pieces), cols),
        "project",
        outputs,
        (scal, segments, x_all, *pieces),
        4.5,
        [pltpu.VMEM((width, 4 * cols + 128), BF)],
    )


def attend_kernel(per, first, scal, q_ref, k_ref, v_ref, seg_row_ref, seg_col_ref, *refs):
    out_ref = refs[-1]
    block = 256
    keys = k_ref[...]
    values = v_ref[...]

    def step(i, carry):
        start = pl.multiple_of(first + i * block, block)
        same = seg_col_ref[pl.ds(start, block), :] == seg_row_ref[...]
        queries = q_ref[pl.ds(start, block), :] * jnp.asarray(HEAD_DIM**-0.5, BF)
        result = jnp.zeros(queries.shape, F32)
        for head in range(per):
            lanes = head_lanes(head, queries.shape)
            score = dot_cols(jnp.where(lanes, queries, jnp.zeros_like(queries)), keys)
            score = jnp.where(same, score, masked_score)
            largest = jnp.max(score, axis=1, keepdims=True)
            power = jnp.exp(score - largest)
            total = jnp.sum(power, axis=1, keepdims=True)
            chance = (power * (1.0 / total)).astype(BF)
            result = jnp.where(lanes, dot(chance, values), result)
        out_ref[pl.ds(pl.multiple_of(i * block, block), block), :] = result.astype(BF)
        return carry

    lax.fori_loop(0, out_ref.shape[0] // block, step, 0)


def attend(scal, queries, keys, values, seg_row, seg_col, per, first, count, kept=()):
    inputs = (scal, queries, keys, values, seg_row, seg_col, *kept)
    return run(
        functools.partial(attend_kernel, per, first),
        "attend",
        shaped((count, queries.shape[1]), BF),
        inputs,
        7.0 * count / queries.shape[0],
        save=(1, 2, 3, 5, *range(6, len(inputs))) if kept else (),
    )


def forward_kernel(count, cols, parts, scal, x_ref, dy_ref, *refs):
    mixed, w_out = [refs[k * parts : (k + 1) * parts] for k in range(4)], refs[4 * parts :][:4]
    refs = refs[4 * parts + 4 :]
    pieces = refs[:count]
    vec_ref = refs[count]
    c_ref, u_ref, df_ref, keep_ref, send_ref, h_ref, w_ref, rows_ref, sums_ref = refs[
        1 + count : 10 + count
    ]
    out_weight = refs[10 + count]
    member = scal[0]
    part = w_ref.shape[1] // 2
    block = x_ref.shape[0] // GROUPS
    place_rows(scal, pieces, w_ref)
    for index in range(GROUPS):

        @pl.when(member == index)
        def _():
            for k in range(GROUPS):
                start = (index ^ k) * cols
                out_weight[:, start : start + cols] = w_out[k][...]

    rows_ref[...] = out_weight[pl.ds(pl.multiple_of(member * cols, cols), cols), :]
    zero = jnp.zeros((1, x_ref.shape[1]), F32)
    up_bias = vec_ref[pl.ds(8 + member, 1), :]

    def run_block(step, half, inner, carry):
        rows = pl.ds(pl.multiple_of(step * block, block), block)
        near = pl.ds(pl.multiple_of(inner * block, block), block)
        resid = x_ref[rows, :].astype(F32) + vec_ref[4:5, :]
        for k in range(GROUPS):
            start = pl.multiple_of((member ^ k) * cols, cols)
            resid += dot(mixed[k][half][near, :], out_weight[pl.ds(start, cols), :])

        @pl.when(step == member)
        def _():
            h_ref[...] = resid

        hat, _ = normalize(resid)
        normed = (hat * vec_ref[5:6, :] + vec_ref[6:7, :]).astype(BF)
        c_ref[rows, :] = normed
        pre = dot(normed, w_ref[:, :part]) + up_bias
        phi = 0.5 * (1.0 + lax.erf(pre * 0.7071067811865476))
        u_ref[rows, :] = (pre * phi).astype(BF)
        slope = phi + pre * (jnp.exp(-0.5 * pre * pre) * 0.3989422804014327)
        grad_pre = (dot(dy_ref[rows, :], w_ref[:, part:]) * slope).astype(BF)
        df_ref[rows, :] = grad_pre
        grad_normed = dot_cols(grad_pre, w_ref[:, :part])
        split_store(member, step, grad_normed, keep_ref, send_ref)
        return (
            carry[0] + jnp.sum(grad_normed * hat, axis=0, keepdims=True),
            carry[1] + jnp.sum(grad_normed, axis=0, keepdims=True),
            carry[2] + jnp.sum(grad_pre.astype(F32), axis=0, keepdims=True),
        )

    carry = (zero, zero, zero)
    inside = GROUPS // parts
    for half in range(parts):
        carry = lax.fori_loop(
            0,
            inside,
            lambda i, carry, half=half: run_block(half * inside + i, half, i, carry),
            carry,
        )
    sums_ref[...] = jnp.zeros_like(sums_ref)
    for i in range(3):
        sums_ref[i : i + 1, :] = carry[i]


def split_store(member, index, value, keep_ref, send_ref):
    mine = (index % 2) == (member % 2)

    @pl.when(mine)
    def _():
        keep_ref[index // 2] = value

    @pl.when(jnp.logical_not(mine))
    def _():
        send_ref[index // 2] = value.astype(BF)


def forward_back(scal, x_all, dy_all, mixed, w_out, pieces, vec, cols):
    length, width = x_all.shape
    part = pieces[0].shape[1] // 2
    rows = length // GROUPS
    outputs = (
        shaped((length, width), BF),
        shaped((length, part), BF),
        shaped((length, part), BF),
        shaped((2, rows, width), F32),
        shaped((2, rows, width), BF),
        shaped((rows, width), F32),
        shaped((width, 2 * part), BF),
        shaped((cols, width), BF),
        shaped((8, width), F32),
    )
    flat = [item for items in mixed for item in items]
    return run(
        functools.partial(forward_kernel, len(pieces), cols, len(mixed[0])),
        "forward_back",
        outputs,
        (scal, x_all, dy_all, *flat, *w_out, *pieces, vec),
        13.0,
        [pltpu.VMEM((width, width), BF)],
    )


def forward_grads_kernel(scal, c_ref, u_ref, df_ref, dy_ref, w_ref, *refs):
    own_ref, g_ref, keep_ref, send_ref = refs[-4:]
    part = u_ref.shape[1]
    block = u_ref.shape[0] // GROUPS
    third = c_ref.shape[1] // 3
    own_ref[...] = dy_ref[pl.ds(pl.multiple_of(scal[0] * block, block), block), :]

    def branch(i, carry):
        rows = pl.ds(pl.multiple_of(i * block, block), block)
        split_store(scal[0], i, dot_cols(u_ref[rows, :], w_ref[:, part:]), keep_ref, send_ref)
        return carry

    lax.fori_loop(0, GROUPS, branch, 0)

    def weight(i, carry):
        lanes = pl.ds(pl.multiple_of(i * third, third), third)
        g_ref[lanes, :part] = dot_rows(c_ref[:, lanes], df_ref[...]).astype(BF)
        g_ref[lanes, part:] = dot_rows(dy_ref[:, lanes], u_ref[...]).astype(BF)
        return carry

    lax.fori_loop(0, 3, weight, 0)


def forward_grads(scal, normed, active, grad_pre, dy_all, weights, kept):
    length, width = normed.shape
    part = active.shape[1]
    rows = length // GROUPS
    outputs = (
        shaped((rows, width), BF),
        shaped((width, 2 * part), BF),
        shaped((2, rows, width), F32),
        shaped((2, rows, width), BF),
    )
    inputs = (scal, normed, active, grad_pre, dy_all, weights, *kept)
    return run(
        forward_grads_kernel,
        "forward_grads",
        outputs,
        inputs,
        6.0,
        save=range(6, len(inputs)),
        far=(2,),
    )


def merge_kernel(scal, keep_ref, got_ref, mine_ref, send_ref):
    row = scal[0] // 2
    mine_ref[...] = keep_ref[row] + got_ref[row].astype(F32)
    send_ref[...] = (keep_ref[1 - row] + got_ref[1 - row].astype(F32)).astype(BF)


def merge(scal, keep, got, lazy=()):
    _, rows, width = keep.shape
    outputs = (shaped((rows, width), F32), shaped((rows, width), BF))
    return run(merge_kernel, "merge", outputs, (scal, keep, got), 0.7, mebibytes=8, lazy=lazy)


def resid_kernel(scal, mine_ref, got_ref, h_ref, dy_ref, vec_ref, dh_ref, dp_ref, sums_ref):
    grad = mine_ref[...] + got_ref[...].astype(F32)
    hat, inverse = normalize(h_ref[...])
    dy = dy_ref[...].astype(F32)
    grad_resid = dy + norm_back(hat, inverse, vec_ref[5:6, :], grad)
    dh_ref[...] = grad_resid
    low = grad_resid.astype(BF)
    dp_ref[...] = low
    sums_ref[...] = jnp.zeros_like(sums_ref)
    sums_ref[0:1, :] = jnp.sum(low.astype(F32), axis=0, keepdims=True)
    sums_ref[1:2, :] = jnp.sum(dy, axis=0, keepdims=True)


def resid_back(scal, mine, got, resid, cotangent, vec):
    rows, width = mine.shape
    outputs = (shaped((rows, width), F32), shaped((rows, width), BF), shaped((8, width), F32))
    return run(resid_kernel, "resid_back", outputs, (scal, mine, got, resid, cotangent, vec), 0.8)


def mixed_kernel(cols, parts, scal, *refs):
    grads, mixed = refs[0:4], [refs[4 + k * parts : 4 + (k + 1) * parts] for k in range(4)]
    rows_ref, do_ref, g_ref, all_ref, own_ref = refs[4 + 4 * parts :]
    share = all_ref.shape[0] // parts
    member = scal[0]
    place_members(scal, grads, all_ref)
    do_ref[...] = dot_cols(all_ref[...], rows_ref[...]).astype(BF)
    for index in range(GROUPS):

        @pl.when(member == index)
        def _():
            own_ref[...] = all_ref[:, index * cols : (index + 1) * cols]

    for k in range(GROUPS):
        start = pl.multiple_of((member ^ k) * cols, cols)
        total = dot_rows(mixed[k][0][...], own_ref[:share, :])
        for half in range(1, parts):
            total += dot_rows(mixed[k][half][...], own_ref[half * share : (half + 1) * share, :])
        g_ref[pl.ds(start, cols), :] = total.astype(BF)


def mixed_back(scal, grads, mixed, w_rows):
    rows, width = grads[0].shape
    cols = w_rows.shape[0]
    length = GROUPS * rows
    flat = [item for items in mixed for item in items]
    return run(
        functools.partial(mixed_kernel, cols, len(mixed[0])),
        "mixed_back",
        (shaped((length, cols), BF), shaped((width, cols), BF)),
        (scal, *grads, *flat, w_rows),
        2.5,
        [pltpu.VMEM((length, width), BF), pltpu.VMEM((length, cols), BF)],
        lazy=range(1 + GROUPS, 2 + GROUPS + len(flat)),
    )


def attend_back_kernel(
    per,
    scal,
    q_ref,
    k_ref,
    v_ref,
    do_ref,
    seg_row_ref,
    seg_col_ref,
    *refs,
):
    dq_ref, dk_ref, dv_ref, k_acc, v_acc = refs[-5:]
    block = 256
    k_acc[...] = jnp.zeros_like(k_acc)
    v_acc[...] = jnp.zeros_like(v_acc)
    keys = k_ref[...]
    values = v_ref[...]

    def step(i, carry):
        rows = pl.ds(pl.multiple_of(i * block, block), block)
        same = seg_col_ref[...] == seg_row_ref[:, rows]
        queries = q_ref[rows, :] * jnp.asarray(HEAD_DIM**-0.5, BF)
        grads = do_ref[rows, :]
        grad_query = jnp.zeros(queries.shape, F32)
        for head in range(per):
            lanes = head_lanes(head, queries.shape)
            query = jnp.where(lanes, queries, jnp.zeros_like(queries))
            grad = jnp.where(lanes, grads, jnp.zeros_like(grads))
            score = jnp.where(same, dot_cols(keys, query), masked_score)
            largest = jnp.max(score, axis=0, keepdims=True)
            power = jnp.exp(score - largest)
            total = jnp.sum(power, axis=0, keepdims=True)
            chance = power * (1.0 / total)
            grad_chance = dot_cols(values, grad)
            inner = jnp.sum(chance * grad_chance, axis=0, keepdims=True)
            grad_score = (chance * (grad_chance - inner)).astype(BF)
            k_acc[...] += dot(grad_score, query)
            v_acc[...] += dot(chance.astype(BF), grad)
            grad_query = jnp.where(lanes, dot_rows(grad_score, keys), grad_query)
        dq_ref[rows, :] = (grad_query * HEAD_DIM**-0.5).astype(BF)
        return carry

    lax.fori_loop(0, q_ref.shape[0] // block, step, 0)
    dk_ref[...] = k_acc[...].astype(BF)
    dv_ref[...] = v_acc[...].astype(BF)


def attend_back(scal, queries, keys, values, grad_out, seg_row, seg_col, per, kept):
    shape = shaped(queries.shape, BF)
    wide = pltpu.VMEM(queries.shape, F32)
    inputs = (scal, queries, keys, values, grad_out, seg_row, seg_col, *kept)
    return run(
        functools.partial(attend_back_kernel, per),
        "attend_back",
        (shape, shape, shape),
        inputs,
        16.0,
        [wide, wide],
        lazy=(1, 2, 3, 6),
        save=range(7, len(inputs)),
    )


def project_back_kernel(cols, scal, *refs):
    x_ref = refs[0]
    grads, weights = refs[1:4], refs[4:7]
    vec_ref, forward_ref, resid_ref, out_ref = refs[7:11]
    g_ref, keep_ref, send_ref, rows_ref, a_ref = refs[11:16]
    member = scal[0]
    block = 256
    width = x_ref.shape[1]
    zero = jnp.zeros((1, width), F32)

    g_ref[:, 3 * cols : 4 * cols] = out_ref[...]

    def step(i, carry):
        rows = pl.ds(pl.multiple_of(i * block, block), block)
        hat, _ = normalize(x_ref[rows, :].astype(F32))
        a_ref[rows, :] = (hat * vec_ref[0:1, :] + vec_ref[1:2, :]).astype(BF)
        grad = dot_cols(grads[0][rows, :], weights[0][...])
        grad += dot_cols(grads[1][rows, :], weights[1][...])
        grad += dot_cols(grads[2][rows, :], weights[2][...])
        split_store(member, i, grad, keep_ref, send_ref)
        return (
            carry[0] + jnp.sum(grad * hat, axis=0, keepdims=True),
            carry[1] + jnp.sum(grad, axis=0, keepdims=True),
        )

    gain, shift = lax.fori_loop(0, GROUPS, step, (zero, zero))
    for i in range(3):
        g_ref[:, i * cols : (i + 1) * cols] = dot_rows(a_ref[...], grads[i][...]).astype(BF)
    rows_ref[...] = jnp.zeros_like(rows_ref)
    listed = (gain, shift, None, None, resid_ref[0:1, :], forward_ref[0:1, :], forward_ref[1:2, :])
    listed += (resid_ref[1:2, :],)
    for i, row in enumerate(listed):
        if row is not None:
            rows_ref[i : i + 1, :] = row
    rows_ref[pl.ds(8 + member, 1), :] = forward_ref[2:3, :]
    rows = rows_ref[...]
    high = rows.astype(BF)
    low = (rows - high.astype(F32)).astype(BF)
    unit = unit_rows(16, 128)
    shifted = jnp.where(
        lax.broadcasted_iota(jnp.int32, (16, 128), 1)
        == lax.broadcasted_iota(jnp.int32, (16, 128), 0) + 16,
        1.0,
        0.0,
    ).astype(BF)
    table = dot_rows(high, unit) + dot_rows(low, shifted)
    lane = lax.broadcasted_iota(jnp.int32, (cols, 128), 1)
    bias = jnp.zeros((cols, 128), F32)
    ones = jnp.ones((grads[0].shape[0], 8), BF)
    for i, column in ((0, 2), (2, 3)):
        total = dot_rows(grads[i][...], ones)[:, 0:1]
        top = total.astype(BF).astype(F32)
        bias = jnp.where(lane == column, top, bias)
        bias = jnp.where(lane == column + 16, total - top, bias)
    g_ref[:, 4 * cols :] = table.astype(BF)
    own = pl.ds(pl.multiple_of(member * cols, cols), cols)
    g_ref[own, 4 * cols :] = (g_ref[own, 4 * cols :].astype(F32) + bias).astype(BF)


def project_back(scal, x_all, grads, weights, vec, sums_forward, sums_resid, grad_out):
    length, width = x_all.shape
    cols = grads[0].shape[1]
    rows = length // GROUPS
    return run(
        functools.partial(project_back_kernel, cols),
        "project_back",
        (
            shaped((width, 4 * cols + 128), BF),
            shaped((2, rows, width), F32),
            shaped((2, rows, width), BF),
        ),
        (scal, x_all, *grads, *weights, vec, sums_forward, sums_resid, grad_out),
        5.0,
        [pltpu.VMEM((16, width), F32), pltpu.VMEM((length, width), BF)],
        lazy=(1, *range(5, 12)),
    )


def input_kernel(scal, mine_ref, got_ref, x_ref, dh_ref, vec_ref, out_ref):
    grad = mine_ref[...] + got_ref[...].astype(F32)
    hat, inverse = normalize(x_ref[...].astype(F32))
    out_ref[...] = dh_ref[...] + norm_back(hat, inverse, vec_ref[0:1, :], grad)


def input_back(scal, mine, got, tokens, grad_resid, vec):
    inputs = (scal, mine, got, tokens, grad_resid, vec)
    return run(input_kernel, "input_back", shaped(mine.shape, F32), inputs, 1.0, lazy=(3, 4, 5))


def output_kernel(scal, mine_ref, got_ref, h_ref, vec_ref, out_ref):
    branch = mine_ref[...] + got_ref[...].astype(F32) + vec_ref[7:8, :]
    out_ref[...] = (h_ref[...] + branch).astype(BF)


def output_sum(scal, mine, got, resid, vec):
    inputs = (scal, mine, got, resid, vec)
    return run(output_kernel, "output_sum", shaped(mine.shape, BF), inputs, 0.8, lazy=(3, 4))


def owned_kernel(scal, in_ref, low_ref, squares_ref):
    total = in_ref[0].astype(F32)
    for i in range(1, in_ref.shape[0]):
        total += in_ref[i].astype(F32)
    low = total.astype(BF)
    low_ref[...] = low
    wide = low.astype(F32)
    squares_ref[...] = jnp.full(squares_ref.shape, jnp.sum(wide * wide), F32)


def owned_sum(scal, pieces):
    outputs = (shaped(pieces.shape[1:], BF), shaped((8, 128), F32))
    return run(owned_kernel, "owned_sum", outputs, (scal, pieces), 1.5, lazy=(1,))


def owned_vector_kernel(cols, scal, in_ref, low_ref):
    total = in_ref[0].astype(F32)
    for i in range(1, in_ref.shape[0]):
        total += in_ref[i].astype(F32)
    low_ref[:, : 4 * cols] = total[:, : 4 * cols].astype(BF)
    vector = total[:, 4 * cols :]
    low_ref[:, 4 * cols : 4 * cols + 128] = vector.astype(BF)
    low_ref[:, 4 * cols + 128 :] = (vector - vector.astype(BF).astype(F32)).astype(BF)


def owned_vector(scal, pieces, cols):
    _, rows, width = pieces.shape
    return run(
        functools.partial(owned_vector_kernel, cols),
        "owned_vector",
        shaped((rows, width + 128), BF),
        (scal, pieces),
        1.5,
    )


def join_kernel(cols, count, scal, *refs):
    pieces, squares = refs[0:4], refs[4:8]
    gradient_ref, vector_ref, squares_ref = refs[8:11]
    width = gradient_ref.shape[1] // 4
    for member in range(GROUPS):

        @pl.when(scal[0] == member)
        def _():
            for i in range(4):
                for k in range(GROUPS):
                    start = i * width + (member ^ k) * cols
                    gradient_ref[:, start : start + cols] = pieces[k][
                        :, i * cols : (i + 1) * cols
                    ].astype(F32)

    def vector_of(piece):
        high = piece[:, 4 * cols : 4 * cols + 128].astype(F32)
        return high + piece[:, 4 * cols + 128 :].astype(F32)

    halves = [vector_of(piece) for piece in pieces]
    table = (halves[0] + halves[1]) + (halves[2] + halves[3])
    rows = lax.broadcasted_iota(jnp.int32, (16, 128), 0)
    lanes = lax.broadcasted_iota(jnp.int32, (16, 128), 1)
    unit = jnp.where((lanes == rows) | (lanes == rows + 16), 1.0, 0.0)
    vector = lax.dot_general(
        unit,
        table,
        (((1,), (1,)), ((), ())),
        preferred_element_type=F32,
        precision=lax.Precision.HIGHEST,
    )[:count]
    vector_ref[...] = vector
    gradient = gradient_ref[...]
    total = jnp.sum(gradient * gradient) + jnp.sum(vector * vector)
    forward = (squares[0][...] + squares[1][...]) + (squares[2][...] + squares[3][...])
    squares_ref[...] = forward + total


def join(scal, pieces, squares, width, count, cols):
    rows = pieces[0].shape[0]
    return run(
        functools.partial(join_kernel, cols, count),
        "join",
        (shaped((rows, 4 * width), F32), shaped((count, rows), F32), shaped((8, 128), F32)),
        (scal, *pieces, *squares),
        1.5,
    )


def clip_factor(total_ref):
    total = total_ref[0]
    for i in range(1, total_ref.shape[0]):
        total += total_ref[i]
    norm = jnp.sqrt(total[0:1, 0:1])
    return jnp.minimum(1.0, clip_limit / (norm + 1e-06))


def adam_kernel(counts, scal, total_ref, attention_ref, vector_ref, *refs):
    grads = refs[0:4]
    sources, targets = refs[4:16], refs[16:31]
    held, copies = refs[31:43], refs[43:46]
    loads, stores = refs[46:49], refs[49:52]
    factor = clip_factor(total_ref)
    decays = (weight_decay, weight_decay, 0.0)

    def chunk(kind, i):
        if counts[kind] == 1:
            return (slice(None), slice(None))
        size = held[4 * kind].shape[1] // counts[kind]
        return (slice(None), pl.ds(pl.multiple_of(i * size, size), size))

    def load(kind, i, state):
        place = chunk(kind, i)
        number = 4 * kind + state
        return pltpu.make_async_copy(
            sources[number].at[place], held[number].at[place], loads[kind].at[i, state]
        )

    def store(kind, i, state):
        place = chunk(kind, i)
        source = held[4 * kind + state] if state < 4 else copies[kind]
        return pltpu.make_async_copy(
            source.at[place], targets[3 * state + kind].at[place], stores[kind].at[i, state]
        )

    def every(kind, action):
        def step(i, carry):
            action(kind, i)
            return carry

        lax.fori_loop(0, counts[kind], step, 0)

    def start(kind, i):
        for state in range(4):
            load(kind, i, state).start()

    def work(kind, i):
        for state in range(4):
            load(kind, i, state).wait()
        place = chunk(kind, i)
        if kind == 0:
            gradient = attention_ref[place]
        elif kind == 2:
            gradient = vector_ref[...]
        else:
            size = held[4].shape[1] // counts[1]
            half = pl.ds(pl.multiple_of((i // GROUPS) * size, size), size)
            source = scal[0] ^ (i % GROUPS)
            gradient = grads[0][:, half]
            for k in range(1, GROUPS):
                gradient = jnp.where(source == k, grads[k][:, half], gradient)
            gradient = gradient.astype(F32)
        results = adam_update(
            *[held[4 * kind + state][place] for state in range(4)], gradient, factor, decays[kind]
        )
        for state, value in zip((0, 1, 2, 3), results):
            held[4 * kind + state][place] = value
        copies[kind][place] = results[0].astype(BF)
        for state in range(5):
            store(kind, i, state).start()

    def finish(kind, i):
        for state in range(5):
            store(kind, i, state).wait()

    for kind in (1, 0, 2):
        every(kind, start)
    for kind in (1, 0, 2):
        every(kind, work)
    for kind in (1, 0, 2):
        every(kind, finish)


def adam(scal, totals, attention_grad, vector_grad, forward_grads_by_member, states):
    counts = (4, 2 * GROUPS, 1)
    kinds = [states[4 * kind].shape for kind in range(3)]
    out_shape = [pltpu.HBM(shape, F32) for _ in range(4) for shape in kinds]
    out_shape += [pltpu.HBM(shape, BF) for shape in kinds]
    return pl.pallas_call(
        functools.partial(adam_kernel, counts),
        out_shape=out_shape,
        in_specs=[smem()] + [vmem()] * 7 + [far_space()] * 12,
        out_specs=[far_space()] * 15,
        scratch_shapes=[pltpu.VMEM(kinds[kind], F32) for kind in range(3) for _ in range(4)]
        + [pltpu.VMEM(shape, BF) for shape in kinds]
        + [pltpu.SemaphoreType.DMA((count, 4)) for count in counts]
        + [pltpu.SemaphoreType.DMA((count, 5)) for count in counts],
        compiler_params=params(32),
        cost_estimate=cost(9.0),
        name="adam",
    )(scal, totals, attention_grad, vector_grad, *forward_grads_by_member, *map(pin, states))


def adam_update(master, moment, second, teacher, gradient, factor, decay_rate):
    clipped = gradient * factor
    moment_new = beta_one * moment + (1.0 - beta_one) * clipped
    second_new = beta_two * second + (1.0 - beta_two) * clipped * clipped
    scale_one = 1.0 - beta_one**ADAM_STEP
    scale_two = 1.0 - beta_two**ADAM_STEP
    update = (moment_new * (1.0 / scale_one)) / (
        jnp.sqrt(second_new * (1.0 / scale_two)) + adam_epsilon
    )
    master_new = master * (1.0 - learn_rate * decay_rate) - learn_rate * update
    teacher_new = teacher_keep * teacher + (1.0 - teacher_keep) * master_new
    return (master_new, moment_new, second_new, teacher_new)


def swap(part, bit):
    return lax.ppermute(part, "head", [(i, i ^ bit) for i in range(4)])


def spread(part, *others):
    across = swap(part, 2)
    if others:
        return [
            part,
            swap(after(part, *others), 1),
            across,
            swap(after(across, *others), 1),
        ]
    return [part, swap(part, 1), across, swap(across, 1)]


RING = (0, 2, 4, 6, 7, 5, 3, 1)


def ring_owners(count):
    if count != len(RING):
        return np.zeros((count, 1), np.int32)
    table = []
    for device in range(count):
        place = RING.index(device)
        owners = [device]
        for hop in range(1, count // 2 + 1):
            owners.append(RING[(place - hop) % count])
            if hop < count // 2:
                owners.append(RING[(place + hop) % count])
        table.append(owners)
    return np.asarray(table, np.int32)


def after(value, *others):
    return lax.optimization_barrier((value, *others))[0]


class Ring:
    def __init__(self, block, count):
        self.count = count
        self.hops = count // 2 if count == len(RING) else 1
        self.front = self.rear = block
        self.pieces = [block]
        self.done = 0

    def hop(self, *others):
        self.done += 1
        if self.count != len(RING):
            self.pieces = [lax.all_gather(after(self.front, *others), "dp", axis=0, tiled=True)]
            return self
        ahead = [(RING[i], RING[(i + 1) % self.count]) for i in range(self.count)]
        back = [(target, source) for source, target in ahead]
        last = self.done == self.hops
        if self.done > 1 or others:
            self.front, self.rear = lax.optimization_barrier((self.front, self.rear, *others))[:2]
        self.front = lax.ppermute(self.front, "dp", ahead)
        self.pieces.append(self.front)
        if not last:
            self.rear = lax.ppermute(self.rear, "dp", back)
            self.pieces.append(self.rear)
        return self

    def rest(self):
        while self.done < self.hops:
            self.hop()
        return self.pieces


def exchange_owned(grads, count):
    blocks = grads.reshape(count, -1, grads.shape[1])
    return lax.all_to_all(blocks, "dp", split_axis=0, concat_axis=0)


def local(
    tokens,
    cotangent,
    segments,
    attention_master,
    feedforward_master,
    vector_master,
    attention_moment,
    feedforward_moment,
    vector_moment,
    attention_second,
    feedforward_second,
    vector_second,
    attention_teacher,
    feedforward_teacher,
    vector_teacher,
):
    width = tokens.shape[1]
    owners = lax.axis_size("dp")
    groups = lax.axis_size("head")
    hidden = feedforward_master.shape[1] // 2
    per = HEADS // groups
    cols = per * HEAD_DIM
    part = hidden // groups

    owner_table = ring_owners(owners)
    table = np.concatenate(
        [
            np.tile(np.arange(groups, dtype=np.int32), owners)[:, None],
            np.repeat(owner_table, groups, axis=0),
        ],
        axis=1,
    )
    place = lax.axis_index("dp") * groups + lax.axis_index("head")
    scal = lax.dynamic_index_in_dim(jnp.asarray(table), place, 0, keepdims=False)
    first = Ring(pack_attention(scal, attention_master, vector_master, cols), owners)
    first.rest()
    early = first.pieces[-2] if owners == len(RING) else first.pieces[0]
    middle = first.pieces[3] if owners == len(RING) else first.pieces[0]
    x_all = place_blocks(scal, spread(tokens, early))
    second = Ring(pack_forward(scal, feedforward_master, part), owners)
    second.hop(early)
    across = swap(after(cotangent, middle), 2)

    queries, keys, values, w_q, w_k, w_v, w_o, vec, seg_col = project(
        scal, segments, x_all, first.pieces, cols
    )
    if second.done < second.hops:
        second.hop(queries)
    half = x_all.shape[0] // 2
    w_across = swap(w_o, 2)
    mixed_low, *kept = attend(
        scal,
        queries,
        keys,
        values,
        segments,
        seg_col,
        per,
        0,
        half,
        (x_all, w_q, w_k, w_v, vec),
    )
    far_q, far_k, far_v, far_col, far_x, far_wq, far_wk, far_wv, far_vec = kept
    low_across = swap(mixed_low, 2)
    w_across = after(w_across, mixed_low)
    if second.done < second.hops:
        second.hop(mixed_low)
    mixed_high = attend(
        scal, after(queries, w_across), keys, values, segments, seg_col, per, half, half
    )
    high_across = swap(mixed_high, 2)
    across, w_across, low_across, w_o, mixed_low, cot = lax.optimization_barrier(
        (across, w_across, low_across, w_o, mixed_low, cotangent, high_across)
    )[:6]
    dy_all = place_blocks(scal, [cot, swap(cot, 1), across, swap(across, 1)])
    w_out = [w_o, swap(w_o, 1), w_across, swap(w_across, 1)]
    mixed = [
        (mixed_low, mixed_high),
        (swap(mixed_low, 1), swap(mixed_high, 1)),
        (low_across, high_across),
        (swap(low_across, 1), swap(high_across, 1)),
    ]
    normed_two, active, grad_pre, keep, send, resid, w_ff, w_rows, sums_forward = forward_back(
        scal, x_all, dy_all, mixed, w_out, second.rest(), vec, cols
    )
    mine, send = merge(scal, keep, swap(send, 1))
    flat = [item for items in mixed for item in items]
    cot_own, grad_ff, keep_branch, send_branch, *kept = forward_grads(
        scal,
        after(normed_two, send),
        active,
        grad_pre,
        dy_all,
        w_ff,
        (resid, sums_forward, w_rows, *flat),
    )
    far_resid, far_sums, far_rows = kept[:3]
    far_mixed = [tuple(kept[3 + 2 * k : 5 + 2 * k]) for k in range(GROUPS)]
    grad_resid, grad_low, sums_resid = resid_back(scal, mine, swap(send, 2), resid, cot_own, vec)
    low_blocks = spread(grad_low)
    owned_ff = exchange_owned(after(grad_ff, low_blocks[1]), owners)
    grad_mixed, grad_out = mixed_back(scal, low_blocks, far_mixed, far_rows)
    mine, send = merge(
        scal, keep_branch, swap(after(send_branch, low_blocks[1]), 1), lazy=(1,)
    )
    *grad_qkv, far_dh, far_sums_resid, far_grad_out = attend_back(
        scal,
        far_q,
        far_k,
        far_v,
        grad_mixed,
        segments,
        far_col,
        per,
        (grad_resid, sums_resid, grad_out),
    )
    block_output = output_sum(scal, mine, swap(send, 2), far_resid, far_vec)
    pack, keep, send = project_back(
        scal,
        far_x,
        grad_qkv,
        (far_wq, far_wk, far_wv),
        far_vec,
        far_sums,
        far_sums_resid,
        far_grad_out,
    )
    owned_pack = exchange_owned(pack, owners)
    mine, send = merge(scal, keep, swap(send, 1))
    input_gradient = input_back(scal, mine, swap(send, 2), tokens, far_dh, far_vec)
    sum_ff, squares_ff = owned_sum(scal, after(owned_ff, pack))
    forward_parts = spread(sum_ff)
    forward_squares = spread(squares_ff)
    owned_pack = after(
        owned_pack, input_gradient, block_output, *forward_parts, *forward_squares
    )
    attention_parts = spread(owned_vector(scal, owned_pack, cols))
    attention_grad, vector_grad, squares = join(
        scal, attention_parts, forward_squares, width, vector_master.shape[0], cols
    )
    totals = lax.all_to_all(
        jnp.broadcast_to(squares, (owners, 8, 128)), "dp", split_axis=0, concat_axis=0
    )
    gradient_norm = jnp.sqrt(jnp.sum(totals[:, 0, 0]))
    results = adam(
        scal,
        totals,
        attention_grad,
        vector_grad,
        forward_parts,
        (
            attention_master,
            attention_moment,
            attention_second,
            attention_teacher,
            feedforward_master,
            feedforward_moment,
            feedforward_second,
            feedforward_teacher,
            vector_master,
            vector_moment,
            vector_second,
            vector_teacher,
        ),
    )
    return (block_output, input_gradient, gradient_norm, *results)


def solution(mesh):
    rows = P(("dp", "head"), None)
    shard = P("dp", None)
    vector = P(None, "dp")
    return jax.shard_map(
        local,
        mesh=mesh,
        in_specs=(rows, rows, shard) + (shard, shard, vector) * 4,
        out_specs=(rows, rows, P()) + (shard, shard, vector) * 5,
        check_vma=False,
    )
```

```python
import functools

import jax
import jax.numpy as jnp
import numpy as np
from jax import lax
from jax.experimental import pallas as pl
from jax.experimental.pallas import tpu as pltpu
from jax.sharding import PartitionSpec as P

HEADS = 12
HEAD_DIM = 64
ADAM_STEP = 3

norm_epsilon = 1e-06
beta_one = 0.5
beta_two = 0.5
adam_epsilon = 1e-08
learn_rate = 0.05
weight_decay = 0.05
teacher_keep = 0.8
clip_limit = 1.0
masked_score = -1e30

BF = jnp.bfloat16
F32 = jnp.float32


def dot_rows(left, right):
    return lax.dot_general(left, right, (((0,), (0,)), ((), ())), preferred_element_type=F32)


def dot_cols(left, right):
    return lax.dot_general(left, right, (((1,), (1,)), ((), ())), preferred_element_type=F32)


def dot(left, right):
    return jnp.dot(left, right, preferred_element_type=F32)


def normalize(values):
    center = jnp.mean(values, axis=-1, keepdims=True)
    deviate = values - center
    spread = jnp.mean(deviate * deviate, axis=-1, keepdims=True)
    inverse = lax.rsqrt(spread + norm_epsilon)
    return deviate * inverse, inverse


def norm_back(hat, inverse, gain, grad):
    scaled = grad * gain
    mean_one = jnp.mean(scaled, axis=-1, keepdims=True)
    mean_two = jnp.mean(scaled * hat, axis=-1, keepdims=True)
    return inverse * (scaled - mean_one - hat * mean_two)


def head_lanes(index, shape):
    lane = lax.broadcasted_iota(jnp.int32, shape, 1)
    return (lane >= index * HEAD_DIM) & (lane < (index + 1) * HEAD_DIM)


def unit_rows(rows, columns):
    row = lax.broadcasted_iota(jnp.int32, (rows, columns), 0)
    column = lax.broadcasted_iota(jnp.int32, (rows, columns), 1)
    return jnp.where(row == column, 1.0, 0.0).astype(BF)


def smem():
    return pl.BlockSpec(memory_space=pltpu.SMEM)


def vmem():
    return pl.BlockSpec(memory_space=pltpu.VMEM)


def whole(*shape):
    return pl.BlockSpec(shape, lambda *index: (0,) * len(shape))


def shaped(shape, kind):
    return jax.ShapeDtypeStruct(shape, kind)


def params(mebibytes):
    return pltpu.CompilerParams(vmem_limit_bytes=mebibytes * 2**20)


COST_SCALE = 1.0


def cost(microseconds):
    return pl.CostEstimate(
        flops=0, transcendentals=0, bytes_accessed=int(microseconds * COST_SCALE * 3.6e6)
    )


def pin(array):
    return pltpu.with_memory_space_constraint(array, pltpu.HBM)


def far_space():
    return pl.BlockSpec(memory_space=pltpu.HBM)


def run(
    kernel,
    name,
    outputs,
    inputs,
    microseconds,
    scratch=(),
    mebibytes=16,
    lazy=(),
    save=(),
    far=(),
    scalars=1,
):
    single = not isinstance(outputs, tuple)
    outputs = [outputs] if single else list(outputs)
    lazy, save, far = list(lazy), list(save), list(far)
    count, produced, own = len(inputs), len(outputs), len(scratch)
    buffers = [pltpu.VMEM(inputs[i].shape, inputs[i].dtype) for i in lazy]
    buffers += [pltpu.VMEM(outputs[i].shape, outputs[i].dtype) for i in far]
    moves = len(lazy) + len(save) + len(far)
    if moves:
        buffers.append(pltpu.SemaphoreType.DMA((moves,)))

    def body(*refs):
        items = list(refs[: count + produced])
        saved = refs[count + produced : count + produced + len(save)]
        rest = refs[count + produced + len(save) :]
        inner, extra = rest[:own], rest[own:]
        copies, number = [], 0
        for j, i in enumerate(lazy):
            copies.append(pltpu.make_async_copy(refs[i], extra[j], extra[-1].at[number]))
            items[i] = extra[j]
            number += 1
        stores = []
        for j, i in enumerate(save):
            stores.append(pltpu.make_async_copy(refs[i], saved[j], extra[-1].at[number]))
            number += 1
        last = []
        for j, i in enumerate(far):
            buffer = extra[len(lazy) + j]
            last.append(pltpu.make_async_copy(buffer, refs[count + i], extra[-1].at[number]))
            items[count + i] = buffer
            number += 1
        for copy in copies + stores:
            copy.start()
        for copy in copies:
            copy.wait()
        kernel(*items, *inner)
        for copy in last:
            copy.start()
        for copy in stores + last:
            copy.wait()

    shapes = [pltpu.HBM(item.shape, item.dtype) if i in far else item for i, item in enumerate(outputs)]
    results = pl.pallas_call(
        body,
        out_shape=shapes + [pltpu.HBM(inputs[i].shape, inputs[i].dtype) for i in save],
        in_specs=[smem()] * scalars
        + [far_space() if i in lazy else vmem() for i in range(scalars, count)],
        out_specs=[far_space() if i in far else vmem() for i in range(produced)]
        + [far_space()] * len(save),
        scratch_shapes=list(scratch) + buffers,
        compiler_params=params(mebibytes),
        cost_estimate=cost(microseconds),
        name=name,
    )(*[pin(item) if i in lazy else item for i, item in enumerate(inputs)])
    return results[0] if single and not save else tuple(results)


GROUPS = 4


def pack_kernel(cols, scal, *refs):
    vector_ref, out_ref = refs[4:6]
    for side in range(2):

        @pl.when(scal[0] % 2 == side)
        def _():
            for i in range(4):
                out_ref[:, i * cols : (i + 1) * cols] = refs[i][
                    :, side * cols : (side + 1) * cols
                ].astype(BF)

    vector = vector_ref[...].astype(BF)
    out_ref[:, 4 * cols :] = dot_rows(vector, unit_rows(vector.shape[0], 128)).astype(BF)


def pack_attention(scal, attention, vector, cols):
    rows = attention.shape[0]

    def pair(i):
        return pl.BlockSpec((rows, 2 * cols), lambda step, scal: (0, 2 * i + scal[0] // 2))

    return pl.pallas_call(
        functools.partial(pack_kernel, cols),
        out_shape=shaped((rows, 4 * cols + 128), BF),
        grid_spec=pltpu.PrefetchScalarGridSpec(
            num_scalar_prefetch=1,
            grid=(1,),
            in_specs=[pair(i) for i in range(4)] + [whole(*vector.shape)],
            out_specs=whole(rows, 4 * cols + 128),
        ),
        compiler_params=params(8),
        cost_estimate=cost(1.5),
        name="pack_attention",
    )(scal, *[attention] * 4, vector)


def cast_kernel(scal, in_ref, out_ref):
    out_ref[...] = in_ref[...].astype(BF)


def pack_forward(scal, forward, part):
    rows = forward.shape[0]
    return pl.pallas_call(
        cast_kernel,
        out_shape=shaped((rows, 2 * part), BF),
        grid_spec=pltpu.PrefetchScalarGridSpec(
            num_scalar_prefetch=1,
            grid=(2,),
            in_specs=[pl.BlockSpec((rows, part), lambda i, scal: (0, GROUPS * i + scal[0]))],
            out_specs=pl.BlockSpec((rows, part), lambda i, scal: (0, i)),
        ),
        compiler_params=params(8),
        cost_estimate=cost(1.5),
        name="pack_forward",
    )(scal, forward)


def place_rows(scal, pieces, target):
    rows = pieces[0].shape[0]
    if len(pieces) == 1:
        target[...] = pieces[0][...]
        return
    for i, piece in enumerate(pieces):
        start = pl.multiple_of(scal[1 + i] * rows, rows)
        target[pl.ds(start, rows), :] = piece[...]


def place_members(scal, pieces, target):
    rows = pieces[0].shape[0]
    for i, piece in enumerate(pieces):
        start = pl.multiple_of((scal[0] ^ i) * rows, rows)
        target[pl.ds(start, rows), :] = piece[...]


def place_kernel(scal, *refs):
    place_members(scal, refs[0:4], refs[8])
    place_members(scal, refs[4:8], refs[9])


def place_blocks(scal, tokens, grads):
    rows, width = tokens[0].shape
    wide = shaped((GROUPS * rows, width), BF)
    return run(place_kernel, "place_blocks", (wide, wide), (scal, *tokens, *grads), 1.0, mebibytes=2)


def fold(value):
    rows, columns = value.shape
    count = 128 // (columns - 128)
    share = rows // count
    rest = [value[i * share : (i + 1) * share, 128:] for i in range(count)]
    return value[:, :128], jnp.concatenate(rest, axis=1)


def folded_rows(rows, columns):
    return rows + rows * (columns - 128) // 128


def project_kernel(count, cols, scal, seg_ref, x_ref, *refs):
    pieces = refs[:count]
    q_ref, k_ref, v_ref, wq_ref, wk_ref, wv_ref, wo_ref, vec_ref, col_ref = refs[count : 9 + count]
    weights = refs[9 + count]
    place_rows(scal, pieces, weights)
    for i, ref in enumerate((wq_ref, wk_ref, wv_ref)):
        ref[...] = weights[:, i * cols : (i + 1) * cols]
    top, rest = fold(weights[:, 3 * cols : 4 * cols])
    wo_ref[: top.shape[0], :] = top
    wo_ref[top.shape[0] :, :] = rest
    unit = unit_rows(16, 128)
    vec_ref[...] = dot_cols(unit, weights[:, 4 * cols :])
    start = pl.multiple_of(scal[0] * cols, cols)
    own = dot_cols(unit, weights[pl.ds(start, cols), 4 * cols :])
    query_bias, value_bias = own[2:3, :], own[3:4, :]
    gain, shift = vec_ref[0:1, :], vec_ref[1:2, :]
    numbers = jnp.broadcast_to(seg_ref[...].astype(F32), (8, seg_ref.shape[1])).astype(BF)
    col_ref[...] = dot_rows(numbers, unit_rows(8, 128))[:, 0:1].astype(jnp.int32)
    block = 256

    def step(i, carry):
        rows = pl.ds(pl.multiple_of(i * block, block), block)
        hat, _ = normalize(x_ref[rows, :].astype(F32))
        normed = (hat * gain + shift).astype(BF)
        q_ref[rows, :] = (dot(normed, wq_ref[...]) + query_bias).astype(BF)
        k_ref[rows, :] = dot(normed, wk_ref[...]).astype(BF)
        v_ref[rows, :] = (dot(normed, wv_ref[...]) + value_bias).astype(BF)
        return carry

    lax.fori_loop(0, x_ref.shape[0] // block, step, 0)


def project(scal, segments, x_all, pieces, cols):
    length, width = x_all.shape
    outputs = (
        (shaped((length, cols), BF),) * 3
        + (shaped((width, cols), BF),) * 3
        + (shaped((folded_rows(width, cols), 128), BF),)
        + (shaped((16, width), F32), shaped((length, 1), jnp.int32))
    )
    return run(
        functools.partial(project_kernel, len(pieces), cols),
        "project",
        outputs,
        (scal, segments, x_all, *pieces),
        4.5,
        [pltpu.VMEM((width, 4 * cols + 128), BF)],
    )


CHUNK = 128
WINDOWS = (4, 6, 8)


def key_window(seg, start, size, length):
    def image(place):
        number = seg[0, place]
        return jnp.where(number < 0, length, number)

    first, last = image(start), image(start + size - 1)
    low, high = jnp.int32(0), jnp.int32(0)
    for chunk in range(length // CHUNK):
        low += (image(chunk * CHUNK + CHUNK - 1) < first).astype(jnp.int32)
        high += (image(chunk * CHUNK) <= last).astype(jnp.int32)
    return low, high - low


def each_window(low, count, length, body):
    chunks = length // CHUNK
    sizes = [size for size in WINDOWS if size < chunks] + [chunks]
    below = 0
    for size in sizes:

        @pl.when((count > below) & (count <= size))
        def _():
            start = jnp.minimum(low, chunks - size) * CHUNK
            body(pl.multiple_of(start, CHUNK), size * CHUNK)

        below = size


def attend_kernel(per, first, scal, seg, q_ref, k_ref, v_ref, seg_row_ref, seg_col_ref, *refs):
    out_ref, held = refs[-2:]
    block = 256
    length = k_ref.shape[0]

    def step(i, carry):
        start = pl.multiple_of(first + i * block, block)
        near = pl.ds(pl.multiple_of(i * block, block), block)
        low, count = key_window(seg, start, block, length)

        def body(key_start, size):
            window = pl.ds(key_start, size)
            keys, values = k_ref[window, :], v_ref[window, :]
            same = seg_col_ref[pl.ds(start, block), :] == seg_row_ref[:, window]
            queries = q_ref[pl.ds(start, block), :] * jnp.asarray(HEAD_DIM**-0.5, BF)
            result = jnp.zeros(queries.shape, F32)
            for head in range(per):
                lanes = head_lanes(head, queries.shape)
                score = dot_cols(jnp.where(lanes, queries, jnp.zeros_like(queries)), keys)
                score = jnp.where(same, score, masked_score)
                largest = jnp.max(score, axis=1, keepdims=True)
                power = jnp.exp(score - largest)
                total = jnp.sum(power, axis=1, keepdims=True)
                chance = (power * (1.0 / total)).astype(BF)
                result = jnp.where(lanes, dot(chance, values), result)
            held[near, :] = result.astype(BF)

        each_window(low, count, length, body)
        return carry

    lax.fori_loop(0, held.shape[0] // block, step, 0)
    top, rest = fold(held[...])
    out_ref[: top.shape[0], :] = top
    out_ref[top.shape[0] :, :] = rest


def attend(scal, queries, keys, values, seg_row, seg_col, per, first, count, kept=()):
    inputs = (scal, seg_row, queries, keys, values, seg_row, seg_col, *kept)
    return run(
        functools.partial(attend_kernel, per, first),
        "attend",
        shaped((folded_rows(count, queries.shape[1]), 128), BF),
        inputs,
        7.0 * count / queries.shape[0],
        [pltpu.VMEM((count, queries.shape[1]), BF)],
        save=(2, 3, 4, 6, *range(7, len(inputs))) if kept else (),
        scalars=2,
    )


def forward_kernel(count, cols, parts, scal, x_ref, dy_ref, *refs):
    mixed, w_out = [refs[k * parts : (k + 1) * parts] for k in range(4)], refs[4 * parts :][:4]
    refs = refs[4 * parts + 4 :]
    pieces = refs[:count]
    vec_ref = refs[count]
    c_ref, u_ref, df_ref, keep_ref, send_ref, h_ref, w_ref, rows_ref, sums_ref, o_ref = refs[
        1 + count : 11 + count
    ]
    out_weight = refs[11 + count]
    member = scal[0]
    length, width = x_ref.shape
    part = w_ref.shape[1] // 2
    block = length // GROUPS
    narrow = cols - 128
    place_rows(scal, pieces, w_ref)

    def unfold(target, first, column, item):
        rows = item.shape[0] * 128 // cols
        share = rows * narrow // 128
        target[first : first + rows, column : column + 128] = item[:rows, :]
        for i in range(rows // share):
            start = first + i * share
            target[start : start + share, column + 128 : column + cols] = item[
                rows:, i * narrow : (i + 1) * narrow
            ]

    for index in range(GROUPS):

        @pl.when(member == index)
        def _():
            for k in range(GROUPS):
                column = (index ^ k) * cols
                unfold(out_weight, 0, column, w_out[k])
                for half in range(parts):
                    unfold(o_ref, half * (length // parts), column, mixed[k][half])

    rows_ref[...] = out_weight[pl.ds(pl.multiple_of(member * cols, cols), cols), :]
    zero = jnp.zeros((1, width), F32)
    up_bias = vec_ref[pl.ds(8 + member, 1), :]

    def run_block(step, carry):
        rows = pl.ds(pl.multiple_of(step * block, block), block)
        resid = x_ref[rows, :].astype(F32) + vec_ref[4:5, :] + dot(o_ref[rows, :], out_weight[...])

        @pl.when(step == member)
        def _():
            h_ref[...] = resid

        hat, _ = normalize(resid)
        normed = (hat * vec_ref[5:6, :] + vec_ref[6:7, :]).astype(BF)
        c_ref[rows, :] = normed
        pre = dot(normed, w_ref[:, :part]) + up_bias
        phi = 0.5 * (1.0 + lax.erf(pre * 0.7071067811865476))
        u_ref[rows, :] = (pre * phi).astype(BF)
        slope = phi + pre * (jnp.exp(-0.5 * pre * pre) * 0.3989422804014327)
        grad_pre = (dot(dy_ref[rows, :], w_ref[:, part:]) * slope).astype(BF)
        df_ref[rows, :] = grad_pre
        grad_normed = dot_cols(grad_pre, w_ref[:, :part])
        split_store(member, step, grad_normed, keep_ref, send_ref)
        return (
            carry[0] + jnp.sum(grad_normed * hat, axis=0, keepdims=True),
            carry[1] + jnp.sum(grad_normed, axis=0, keepdims=True),
            carry[2] + jnp.sum(grad_pre.astype(F32), axis=0, keepdims=True),
        )

    carry = lax.fori_loop(0, GROUPS, run_block, (zero, zero, zero))
    sums_ref[...] = jnp.zeros_like(sums_ref)
    for i in range(3):
        sums_ref[i : i + 1, :] = carry[i]


def split_store(member, index, value, keep_ref, send_ref):
    mine = (index % 2) == (member % 2)

    @pl.when(mine)
    def _():
        keep_ref[index // 2] = value

    @pl.when(jnp.logical_not(mine))
    def _():
        send_ref[index // 2] = value.astype(BF)


def forward_back(scal, x_all, dy_all, mixed, w_out, pieces, vec, cols):
    length, width = x_all.shape
    part = pieces[0].shape[1] // 2
    rows = length // GROUPS
    outputs = (
        shaped((length, width), BF),
        shaped((length, part), BF),
        shaped((length, part), BF),
        shaped((2, rows, width), F32),
        shaped((2, rows, width), BF),
        shaped((rows, width), F32),
        shaped((width, 2 * part), BF),
        shaped((cols, width), BF),
        shaped((8, width), F32),
        shaped((length, width), BF),
    )
    flat = [item for items in mixed for item in items]
    return run(
        functools.partial(forward_kernel, len(pieces), cols, len(mixed[0])),
        "forward_back",
        outputs,
        (scal, x_all, dy_all, *flat, *w_out, *pieces, vec),
        13.0,
        [pltpu.VMEM((width, width), BF)],
    )


def forward_grads_kernel(scal, c_ref, u_ref, df_ref, dy_ref, *refs):
    own_ref, g_ref = refs[-2:]
    part = u_ref.shape[1]
    block = u_ref.shape[0] // GROUPS
    third = c_ref.shape[1] // 3
    own_ref[...] = dy_ref[pl.ds(pl.multiple_of(scal[0] * block, block), block), :]

    def weight(i, carry):
        lanes = pl.ds(pl.multiple_of(i * third, third), third)
        g_ref[lanes, :part] = dot_rows(c_ref[:, lanes], df_ref[...]).astype(BF)
        g_ref[lanes, part:] = dot_rows(dy_ref[:, lanes], u_ref[...]).astype(BF)
        return carry

    lax.fori_loop(0, 3, weight, 0)


def forward_grads(scal, normed, active, grad_pre, dy_all, kept):
    length, width = normed.shape
    part = active.shape[1]
    outputs = (shaped((length // GROUPS, width), BF), shaped((width, 2 * part), BF))
    inputs = (scal, normed, active, grad_pre, dy_all, *kept)
    return run(
        forward_grads_kernel,
        "forward_grads",
        outputs,
        inputs,
        4.0,
        save=(2, *range(5, len(inputs))),
    )


def branch_kernel(scal, u_ref, w_ref, keep_ref, send_ref):
    part = u_ref.shape[1]
    block = u_ref.shape[0] // GROUPS

    def branch(i, carry):
        rows = pl.ds(pl.multiple_of(i * block, block), block)
        split_store(scal[0], i, dot_cols(u_ref[rows, :], w_ref[:, part:]), keep_ref, send_ref)
        return carry

    lax.fori_loop(0, GROUPS, branch, 0)


def branch_part(scal, active, weights):
    rows = active.shape[0] // GROUPS
    width = weights.shape[0]
    return run(
        branch_kernel,
        "branch_part",
        (shaped((2, rows, width), F32), shaped((2, rows, width), BF)),
        (scal, active, weights),
        3.0,
        lazy=(1, 2),
        far=(0,),
    )


def merge_kernel(scal, keep_ref, got_ref, mine_ref, send_ref):
    row = scal[0] // 2
    mine_ref[...] = keep_ref[row] + got_ref[row].astype(F32)
    send_ref[...] = (keep_ref[1 - row] + got_ref[1 - row].astype(F32)).astype(BF)


def merge(scal, keep, got, lazy=()):
    _, rows, width = keep.shape
    outputs = (shaped((rows, width), F32), shaped((rows, width), BF))
    return run(merge_kernel, "merge", outputs, (scal, keep, got), 0.7, mebibytes=8, lazy=lazy)


def resid_kernel(scal, mine_ref, got_ref, h_ref, dy_ref, vec_ref, dh_ref, dp_ref, sums_ref):
    grad = mine_ref[...] + got_ref[...].astype(F32)
    hat, inverse = normalize(h_ref[...])
    dy = dy_ref[...].astype(F32)
    grad_resid = dy + norm_back(hat, inverse, vec_ref[5:6, :], grad)
    dh_ref[...] = grad_resid
    low = grad_resid.astype(BF)
    dp_ref[...] = low
    sums_ref[...] = jnp.zeros_like(sums_ref)
    sums_ref[0:1, :] = jnp.sum(low.astype(F32), axis=0, keepdims=True)
    sums_ref[1:2, :] = jnp.sum(dy, axis=0, keepdims=True)


def resid_back(scal, mine, got, resid, cotangent, vec):
    rows, width = mine.shape
    outputs = (shaped((rows, width), F32), shaped((rows, width), BF), shaped((8, width), F32))
    return run(resid_kernel, "resid_back", outputs, (scal, mine, got, resid, cotangent, vec), 0.8)


def mixed_kernel(cols, scal, *refs):
    grads, (o_ref, rows_ref, do_ref, g_ref, all_ref, own_ref) = refs[0:4], refs[4:10]
    place_members(scal, grads, all_ref)
    do_ref[...] = dot_cols(all_ref[...], rows_ref[...]).astype(BF)
    for index in range(GROUPS):

        @pl.when(scal[0] == index)
        def _():
            own_ref[...] = all_ref[:, index * cols : (index + 1) * cols]

    g_ref[...] = dot_rows(o_ref[...], own_ref[...]).astype(BF)


def mixed_back(scal, grads, mixed, w_rows):
    cols, width = w_rows.shape
    length = mixed.shape[0]
    return run(
        functools.partial(mixed_kernel, cols),
        "mixed_back",
        (shaped((length, cols), BF), shaped((width, cols), BF)),
        (scal, *grads, mixed, w_rows),
        2.5,
        [pltpu.VMEM((length, width), BF), pltpu.VMEM((length, cols), BF)],
        lazy=(5, 6),
    )


def attend_back_kernel(
    per, scal, seg, q_ref, k_ref, v_ref, do_ref, seg_row_ref, seg_col_ref, *refs
):
    dq_ref, dk_ref, dv_ref, k_acc, v_acc = refs[-5:]
    block = 256
    length = k_ref.shape[0]
    k_acc[...] = jnp.zeros_like(k_acc)
    v_acc[...] = jnp.zeros_like(v_acc)

    def step(i, carry):
        start = pl.multiple_of(i * block, block)
        rows = pl.ds(start, block)
        low, count = key_window(seg, start, block, length)

        def body(key_start, size):
            window = pl.ds(key_start, size)
            keys, values = k_ref[window, :], v_ref[window, :]
            same = seg_col_ref[window, :] == seg_row_ref[:, rows]
            queries = q_ref[rows, :] * jnp.asarray(HEAD_DIM**-0.5, BF)
            grads = do_ref[rows, :]
            grad_query = jnp.zeros(queries.shape, F32)
            grad_key = jnp.zeros(keys.shape, F32)
            grad_value = jnp.zeros(keys.shape, F32)
            for head in range(per):
                lanes = head_lanes(head, queries.shape)
                query = jnp.where(lanes, queries, jnp.zeros_like(queries))
                grad = jnp.where(lanes, grads, jnp.zeros_like(grads))
                score = jnp.where(same, dot_cols(keys, query), masked_score)
                largest = jnp.max(score, axis=0, keepdims=True)
                power = jnp.exp(score - largest)
                total = jnp.sum(power, axis=0, keepdims=True)
                chance = power * (1.0 / total)
                grad_chance = dot_cols(values, grad)
                inner = jnp.sum(chance * grad_chance, axis=0, keepdims=True)
                grad_score = (chance * (grad_chance - inner)).astype(BF)
                grad_key += dot(grad_score, query)
                grad_value += dot(chance.astype(BF), grad)
                grad_query = jnp.where(lanes, dot_rows(grad_score, keys), grad_query)
            k_acc[window, :] += grad_key
            v_acc[window, :] += grad_value
            dq_ref[rows, :] = (grad_query * HEAD_DIM**-0.5).astype(BF)

        each_window(low, count, length, body)
        return carry

    lax.fori_loop(0, q_ref.shape[0] // block, step, 0)
    dk_ref[...] = k_acc[...].astype(BF)
    dv_ref[...] = v_acc[...].astype(BF)


def attend_back(scal, queries, keys, values, grad_out, seg_row, seg_col, per, kept):
    shape = shaped(queries.shape, BF)
    wide = pltpu.VMEM(queries.shape, F32)
    inputs = (scal, seg_row, queries, keys, values, grad_out, seg_row, seg_col, *kept)
    return run(
        functools.partial(attend_back_kernel, per),
        "attend_back",
        (shape, shape, shape),
        inputs,
        16.0,
        [wide, wide],
        lazy=(2, 3, 4, 7),
        save=range(8, len(inputs)),
        scalars=2,
    )


def project_back_kernel(cols, scal, *refs):
    x_ref = refs[0]
    grads, weights = refs[1:4], refs[4:7]
    vec_ref, forward_ref, resid_ref, out_ref = refs[7:11]
    g_ref, keep_ref, send_ref, rows_ref, a_ref = refs[11:16]
    member = scal[0]
    block = 256
    width = x_ref.shape[1]
    zero = jnp.zeros((1, width), F32)

    g_ref[:, 3 * cols : 4 * cols] = out_ref[...]

    def step(i, carry):
        rows = pl.ds(pl.multiple_of(i * block, block), block)
        hat, _ = normalize(x_ref[rows, :].astype(F32))
        a_ref[rows, :] = (hat * vec_ref[0:1, :] + vec_ref[1:2, :]).astype(BF)
        grad = dot_cols(grads[0][rows, :], weights[0][...])
        grad += dot_cols(grads[1][rows, :], weights[1][...])
        grad += dot_cols(grads[2][rows, :], weights[2][...])
        split_store(member, i, grad, keep_ref, send_ref)
        return (
            carry[0] + jnp.sum(grad * hat, axis=0, keepdims=True),
            carry[1] + jnp.sum(grad, axis=0, keepdims=True),
        )

    gain, shift = lax.fori_loop(0, GROUPS, step, (zero, zero))
    for i in range(3):
        g_ref[:, i * cols : (i + 1) * cols] = dot_rows(a_ref[...], grads[i][...]).astype(BF)
    rows_ref[...] = jnp.zeros_like(rows_ref)
    listed = (gain, shift, None, None, resid_ref[0:1, :], forward_ref[0:1, :], forward_ref[1:2, :])
    listed += (resid_ref[1:2, :],)
    for i, row in enumerate(listed):
        if row is not None:
            rows_ref[i : i + 1, :] = row
    rows_ref[pl.ds(8 + member, 1), :] = forward_ref[2:3, :]
    rows = rows_ref[...]
    high = rows.astype(BF)
    low = (rows - high.astype(F32)).astype(BF)
    unit = unit_rows(16, 128)
    shifted = jnp.where(
        lax.broadcasted_iota(jnp.int32, (16, 128), 1)
        == lax.broadcasted_iota(jnp.int32, (16, 128), 0) + 16,
        1.0,
        0.0,
    ).astype(BF)
    table = dot_rows(high, unit) + dot_rows(low, shifted)
    lane = lax.broadcasted_iota(jnp.int32, (cols, 128), 1)
    bias = jnp.zeros((cols, 128), F32)
    ones = jnp.ones((grads[0].shape[0], 8), BF)
    for i, column in ((0, 2), (2, 3)):
        total = dot_rows(grads[i][...], ones)[:, 0:1]
        top = total.astype(BF).astype(F32)
        bias = jnp.where(lane == column, top, bias)
        bias = jnp.where(lane == column + 16, total - top, bias)
    g_ref[:, 4 * cols :] = table.astype(BF)
    own = pl.ds(pl.multiple_of(member * cols, cols), cols)
    g_ref[own, 4 * cols :] = (g_ref[own, 4 * cols :].astype(F32) + bias).astype(BF)


def project_back(scal, x_all, grads, weights, vec, sums_forward, sums_resid, grad_out):
    length, width = x_all.shape
    cols = grads[0].shape[1]
    rows = length // GROUPS
    return run(
        functools.partial(project_back_kernel, cols),
        "project_back",
        (
            shaped((width, 4 * cols + 128), BF),
            shaped((2, rows, width), F32),
            shaped((2, rows, width), BF),
        ),
        (scal, x_all, *grads, *weights, vec, sums_forward, sums_resid, grad_out),
        5.0,
        [pltpu.VMEM((16, width), F32), pltpu.VMEM((length, width), BF)],
        lazy=(1, *range(5, 12)),
    )


def input_kernel(scal, mine_ref, got_ref, x_ref, dh_ref, vec_ref, out_ref):
    grad = mine_ref[...] + got_ref[...].astype(F32)
    hat, inverse = normalize(x_ref[...].astype(F32))
    out_ref[...] = dh_ref[...] + norm_back(hat, inverse, vec_ref[0:1, :], grad)


def input_back(scal, mine, got, tokens, grad_resid, vec):
    inputs = (scal, mine, got, tokens, grad_resid, vec)
    return run(input_kernel, "input_back", shaped(mine.shape, F32), inputs, 1.0, lazy=(3, 4, 5))


def output_kernel(scal, mine_ref, got_ref, h_ref, vec_ref, out_ref):
    branch = mine_ref[...] + got_ref[...].astype(F32) + vec_ref[7:8, :]
    out_ref[...] = (h_ref[...] + branch).astype(BF)


def output_sum(scal, mine, got, resid, vec):
    inputs = (scal, mine, got, resid, vec)
    return run(output_kernel, "output_sum", shaped(mine.shape, BF), inputs, 0.8, lazy=(3, 4))


def owned_kernel(scal, in_ref, low_ref):
    total = in_ref[0].astype(F32)
    for i in range(1, in_ref.shape[0]):
        total += in_ref[i].astype(F32)
    low_ref[...] = total.astype(BF)


def owned_sum(scal, pieces):
    outputs = shaped(pieces.shape[1:], BF)
    return run(owned_kernel, "owned_sum", outputs, (scal, pieces), 1.5, lazy=(1,))


def squares_kernel(scal, *refs):
    sums = []
    for piece in refs[:4]:
        wide = piece[...].astype(F32)
        sums.append(jnp.sum(wide * wide))
    total = (sums[0] + sums[1]) + (sums[2] + sums[3])
    refs[4][...] = jnp.full(refs[4].shape, total, F32)


def squares_of(scal, pieces):
    return run(squares_kernel, "squares_of", shaped((8, 128), F32), (scal, *pieces), 1.0)


def owned_vector_kernel(cols, scal, in_ref, low_ref):
    total = in_ref[0].astype(F32)
    for i in range(1, in_ref.shape[0]):
        total += in_ref[i].astype(F32)
    low_ref[:, : 4 * cols] = total[:, : 4 * cols].astype(BF)
    vector = total[:, 4 * cols :]
    low_ref[:, 4 * cols : 4 * cols + 128] = vector.astype(BF)
    low_ref[:, 4 * cols + 128 :] = (vector - vector.astype(BF).astype(F32)).astype(BF)


def owned_vector(scal, pieces, cols):
    _, rows, width = pieces.shape
    return run(
        functools.partial(owned_vector_kernel, cols),
        "owned_vector",
        shaped((rows, width + 128), BF),
        (scal, pieces),
        1.5,
    )


def join_kernel(cols, count, scal, *refs):
    pieces, forward_ref = refs[0:4], refs[4]
    gradient_ref, vector_ref, squares_ref = refs[5:8]
    width = gradient_ref.shape[1] // 4
    for member in range(GROUPS):

        @pl.when(scal[0] == member)
        def _():
            for i in range(4):
                for k in range(GROUPS):
                    start = i * width + (member ^ k) * cols
                    gradient_ref[:, start : start + cols] = pieces[k][
                        :, i * cols : (i + 1) * cols
                    ].astype(F32)

    def vector_of(piece):
        high = piece[:, 4 * cols : 4 * cols + 128].astype(F32)
        return high + piece[:, 4 * cols + 128 :].astype(F32)

    halves = [vector_of(piece) for piece in pieces]
    table = (halves[0] + halves[1]) + (halves[2] + halves[3])
    rows = lax.broadcasted_iota(jnp.int32, (16, 128), 0)
    lanes = lax.broadcasted_iota(jnp.int32, (16, 128), 1)
    unit = jnp.where((lanes == rows) | (lanes == rows + 16), 1.0, 0.0)
    vector = lax.dot_general(
        unit,
        table,
        (((1,), (1,)), ((), ())),
        preferred_element_type=F32,
        precision=lax.Precision.HIGHEST,
    )[:count]
    vector_ref[...] = vector
    gradient = gradient_ref[...]
    total = jnp.sum(gradient * gradient) + jnp.sum(vector * vector)
    squares_ref[...] = forward_ref[...] + total


def join(scal, pieces, squares, width, count, cols):
    rows = pieces[0].shape[0]
    return run(
        functools.partial(join_kernel, cols, count),
        "join",
        (shaped((rows, 4 * width), F32), shaped((count, rows), F32), shaped((8, 128), F32)),
        (scal, *pieces, squares),
        1.5,
    )


def clip_factor(total_ref):
    total = total_ref[0]
    for i in range(1, total_ref.shape[0]):
        total += total_ref[i]
    norm = jnp.sqrt(total[0:1, 0:1])
    return jnp.minimum(1.0, clip_limit / (norm + 1e-06))


def adam_kernel(counts, scal, total_ref, attention_ref, vector_ref, *refs):
    grads = refs[0:4]
    sources, targets = refs[4:16], refs[16:31]
    held, copies = refs[31:43], refs[43:46]
    loads, stores = refs[46:49], refs[49:52]
    factor = clip_factor(total_ref)
    decays = (weight_decay, weight_decay, 0.0)

    def chunk(kind, i):
        if counts[kind] == 1:
            return (slice(None), slice(None))
        size = held[4 * kind].shape[1] // counts[kind]
        return (slice(None), pl.ds(pl.multiple_of(i * size, size), size))

    def load(kind, i, state):
        place = chunk(kind, i)
        number = 4 * kind + state
        return pltpu.make_async_copy(
            sources[number].at[place], held[number].at[place], loads[kind].at[i, state]
        )

    def store(kind, i, state):
        place = chunk(kind, i)
        source = held[4 * kind + state] if state < 4 else copies[kind]
        return pltpu.make_async_copy(
            source.at[place], targets[3 * state + kind].at[place], stores[kind].at[i, state]
        )

    def every(kind, action):
        def step(i, carry):
            action(kind, i)
            return carry

        lax.fori_loop(0, counts[kind], step, 0)

    def start(kind, i):
        for state in range(4):
            load(kind, i, state).start()

    def work(kind, i):
        for state in range(4):
            load(kind, i, state).wait()
        place = chunk(kind, i)
        if kind == 0:
            gradient = attention_ref[place]
        elif kind == 2:
            gradient = vector_ref[...]
        else:
            size = held[4].shape[1] // counts[1]
            half = pl.ds(pl.multiple_of((i // GROUPS) * size, size), size)
            source = scal[0] ^ (i % GROUPS)
            gradient = grads[0][:, half]
            for k in range(1, GROUPS):
                gradient = jnp.where(source == k, grads[k][:, half], gradient)
            gradient = gradient.astype(F32)
        results = adam_update(
            *[held[4 * kind + state][place] for state in range(4)], gradient, factor, decays[kind]
        )
        for state, value in zip((0, 1, 2, 3), results):
            held[4 * kind + state][place] = value
        copies[kind][place] = results[0].astype(BF)
        for state in range(5):
            store(kind, i, state).start()

    def finish(kind, i):
        for state in range(5):
            store(kind, i, state).wait()

    for kind in (1, 0, 2):
        every(kind, start)
    for kind in (1, 0, 2):
        every(kind, work)
    for kind in (1, 0, 2):
        every(kind, finish)


def adam(scal, totals, attention_grad, vector_grad, forward_grads_by_member, states):
    counts = (4, 2 * GROUPS, 1)
    kinds = [states[4 * kind].shape for kind in range(3)]
    out_shape = [pltpu.HBM(shape, F32) for _ in range(4) for shape in kinds]
    out_shape += [pltpu.HBM(shape, BF) for shape in kinds]
    return pl.pallas_call(
        functools.partial(adam_kernel, counts),
        out_shape=out_shape,
        in_specs=[smem()] + [vmem()] * 7 + [far_space()] * 12,
        out_specs=[far_space()] * 15,
        scratch_shapes=[pltpu.VMEM(kinds[kind], F32) for kind in range(3) for _ in range(4)]
        + [pltpu.VMEM(shape, BF) for shape in kinds]
        + [pltpu.SemaphoreType.DMA((count, 4)) for count in counts]
        + [pltpu.SemaphoreType.DMA((count, 5)) for count in counts],
        compiler_params=params(32),
        cost_estimate=cost(9.0),
        name="adam",
    )(scal, totals, attention_grad, vector_grad, *forward_grads_by_member, *map(pin, states))


def adam_update(master, moment, second, teacher, gradient, factor, decay_rate):
    clipped = gradient * factor
    moment_new = beta_one * moment + (1.0 - beta_one) * clipped
    second_new = beta_two * second + (1.0 - beta_two) * clipped * clipped
    scale_one = 1.0 - beta_one**ADAM_STEP
    scale_two = 1.0 - beta_two**ADAM_STEP
    update = (moment_new * (1.0 / scale_one)) / (
        jnp.sqrt(second_new * (1.0 / scale_two)) + adam_epsilon
    )
    master_new = master * (1.0 - learn_rate * decay_rate) - learn_rate * update
    teacher_new = teacher_keep * teacher + (1.0 - teacher_keep) * master_new
    return (master_new, moment_new, second_new, teacher_new)


def swap(part, bit):
    return lax.ppermute(part, "head", [(i, i ^ bit) for i in range(4)])


def spread(part, *others):
    across = swap(part, 2)
    if others:
        return [
            part,
            swap(after(part, *others), 1),
            across,
            swap(after(across, *others), 1),
        ]
    return [part, swap(part, 1), across, swap(across, 1)]


RING = (0, 2, 4, 6, 7, 5, 3, 1)


def ring_owners(count):
    if count != len(RING):
        return np.zeros((count, 1), np.int32)
    table = []
    for device in range(count):
        place = RING.index(device)
        owners = [device]
        for hop in range(1, count // 2 + 1):
            owners.append(RING[(place - hop) % count])
            if hop < count // 2:
                owners.append(RING[(place + hop) % count])
        table.append(owners)
    return np.asarray(table, np.int32)


def after(value, *others):
    return lax.optimization_barrier((value, *others))[0]


class Ring:
    def __init__(self, block, count):
        self.count = count
        self.hops = count // 2 if count == len(RING) else 1
        self.front = self.rear = block
        self.pieces = [block]
        self.done = 0

    def hop(self, *others):
        self.done += 1
        if self.count != len(RING):
            self.pieces = [lax.all_gather(after(self.front, *others), "dp", axis=0, tiled=True)]
            return self
        ahead = [(RING[i], RING[(i + 1) % self.count]) for i in range(self.count)]
        back = [(target, source) for source, target in ahead]
        last = self.done == self.hops
        if self.done > 1 or others:
            self.front, self.rear = lax.optimization_barrier((self.front, self.rear, *others))[:2]
        self.front = lax.ppermute(self.front, "dp", ahead)
        self.pieces.append(self.front)
        if not last:
            self.rear = lax.ppermute(self.rear, "dp", back)
            self.pieces.append(self.rear)
        return self

    def rest(self):
        while self.done < self.hops:
            self.hop()
        return self.pieces


def exchange_owned(grads, count):
    blocks = grads.reshape(count, -1, grads.shape[1])
    return lax.all_to_all(blocks, "dp", split_axis=0, concat_axis=0)


def local(
    tokens,
    cotangent,
    segments,
    attention_master,
    feedforward_master,
    vector_master,
    attention_moment,
    feedforward_moment,
    vector_moment,
    attention_second,
    feedforward_second,
    vector_second,
    attention_teacher,
    feedforward_teacher,
    vector_teacher,
):
    width = tokens.shape[1]
    owners = lax.axis_size("dp")
    groups = lax.axis_size("head")
    hidden = feedforward_master.shape[1] // 2
    per = HEADS // groups
    cols = per * HEAD_DIM
    part = hidden // groups

    owner_table = ring_owners(owners)
    table = np.concatenate(
        [
            np.tile(np.arange(groups, dtype=np.int32), owners)[:, None],
            np.repeat(owner_table, groups, axis=0),
        ],
        axis=1,
    )
    place = lax.axis_index("dp") * groups + lax.axis_index("head")
    scal = lax.dynamic_index_in_dim(jnp.asarray(table), place, 0, keepdims=False)
    first = Ring(pack_attention(scal, attention_master, vector_master, cols), owners)
    first.rest()
    ringed = owners == len(RING)
    early = first.pieces[-3:-1] if ringed else first.pieces
    token_across, grad_across = swap(tokens, 2), swap(cotangent, 2)
    token, token_across, grad, grad_across = lax.optimization_barrier(
        (tokens, token_across, cotangent, grad_across, *early)
    )[:4]
    x_all, dy_all = place_blocks(
        scal,
        [token, swap(token, 1), token_across, swap(token_across, 1)],
        [grad, swap(grad, 1), grad_across, swap(grad_across, 1)],
    )
    second = Ring(pack_forward(scal, feedforward_master, part), owners)
    second.hop(first.pieces[-1])

    queries, keys, values, w_q, w_k, w_v, w_o, vec, seg_col = project(
        scal, segments, x_all, first.pieces, cols
    )
    half = x_all.shape[0] // 2
    w_across = swap(w_o, 2)
    mixed_low, *kept = attend(
        scal,
        queries,
        keys,
        values,
        segments,
        seg_col,
        per,
        0,
        half,
        (x_all, w_q, w_k, w_v, vec),
    )
    far_q, far_k, far_v, far_col, far_x, far_wq, far_wk, far_wv, far_vec = kept
    low_across = swap(mixed_low, 2)
    w_across = after(w_across, mixed_low)
    if ringed:
        second.hop(mixed_low)
    mixed_high = attend(
        scal, after(queries, w_across), keys, values, segments, seg_col, per, half, half
    )
    high_across = swap(after(mixed_high, low_across), 2)
    if ringed:
        second.hop(mixed_high)
    w_across, low_across, w_o, mixed_low = lax.optimization_barrier(
        (w_across, low_across, w_o, mixed_low, high_across)
    )[:4]
    w_out = [w_o, swap(w_o, 1), w_across, swap(w_across, 1)]
    mixed = [
        (mixed_low, mixed_high),
        (swap(mixed_low, 1), swap(mixed_high, 1)),
        (low_across, high_across),
        (swap(low_across, 1), swap(high_across, 1)),
    ]
    (
        normed_two,
        active,
        grad_pre,
        keep,
        send,
        resid,
        w_ff,
        w_rows,
        sums_forward,
        mixed_all,
    ) = forward_back(scal, x_all, dy_all, mixed, w_out, second.rest(), vec, cols)
    cot_own, grad_ff, far_active, *kept = forward_grads(
        scal,
        normed_two,
        active,
        grad_pre,
        dy_all,
        (resid, sums_forward, w_rows, w_ff, mixed_all),
    )
    far_resid, far_sums, far_rows, far_ff, far_mixed = kept
    owned_ff = exchange_owned(grad_ff, owners)
    mine, send = merge(scal, after(keep, grad_ff), swap(send, 1))
    keep_branch, send_branch = branch_part(scal, far_active, after(far_ff, send))
    got = swap(send, 2)
    grad_resid, grad_low, sums_resid = resid_back(
        scal, after(mine, send_branch), got, resid, cot_own, vec
    )
    low_blocks = spread(grad_low)
    grad_mixed, grad_out = mixed_back(scal, low_blocks, far_mixed, far_rows)
    mine, send = merge(
        scal, keep_branch, swap(after(send_branch, grad_mixed), 1), lazy=(1,)
    )
    *grad_qkv, far_dh, far_sums_resid, far_grad_out = attend_back(
        scal,
        far_q,
        far_k,
        far_v,
        grad_mixed,
        segments,
        far_col,
        per,
        (grad_resid, sums_resid, grad_out),
    )
    block_output = output_sum(scal, mine, swap(send, 2), far_resid, far_vec)
    pack, keep, send = project_back(
        scal,
        after(far_x, block_output),
        grad_qkv,
        (far_wq, far_wk, far_wv),
        far_vec,
        far_sums,
        far_sums_resid,
        far_grad_out,
    )
    owned_pack = exchange_owned(pack, owners)
    mine, send = merge(scal, keep, swap(send, 1))
    input_gradient = input_back(scal, mine, swap(send, 2), tokens, far_dh, far_vec)
    forward_parts = spread(owned_sum(scal, after(owned_ff, pack)))
    forward_squares = squares_of(scal, forward_parts)
    owned_pack = after(owned_pack, input_gradient, forward_squares)
    attention_parts = spread(owned_vector(scal, owned_pack, cols))
    attention_grad, vector_grad, squares = join(
        scal, attention_parts, forward_squares, width, vector_master.shape[0], cols
    )
    totals = lax.all_to_all(
        jnp.broadcast_to(squares, (owners, 8, 128)), "dp", split_axis=0, concat_axis=0
    )
    gradient_norm = jnp.sqrt(jnp.sum(totals[:, 0, 0]))
    results = adam(
        scal,
        totals,
        attention_grad,
        vector_grad,
        forward_parts,
        (
            attention_master,
            attention_moment,
            attention_second,
            attention_teacher,
            feedforward_master,
            feedforward_moment,
            feedforward_second,
            feedforward_teacher,
            vector_master,
            vector_moment,
            vector_second,
            vector_teacher,
        ),
    )
    return (block_output, input_gradient, gradient_norm, *results)


def solution(mesh):
    rows = P(("dp", "head"), None)
    shard = P("dp", None)
    vector = P(None, "dp")
    return jax.shard_map(
        local,
        mesh=mesh,
        in_specs=(rows, rows, shard) + (shard, shard, vector) * 4,
        out_specs=(rows, rows, P()) + (shard, shard, vector) * 5,
        check_vma=False,
    )
```

```python
import functools

import jax
import jax.numpy as jnp
import numpy as np
from jax import lax
from jax.experimental import pallas as pl
from jax.experimental.pallas import tpu as pltpu
from jax.sharding import PartitionSpec as P

HEADS = 12
HEAD_DIM = 64
ADAM_STEP = 3

norm_epsilon = 1e-06
beta_one = 0.5
beta_two = 0.5
adam_epsilon = 1e-08
learn_rate = 0.05
weight_decay = 0.05
teacher_keep = 0.8
clip_limit = 1.0
masked_score = -1e30

BF = jnp.bfloat16
F32 = jnp.float32


def dot_rows(left, right):
    return lax.dot_general(left, right, (((0,), (0,)), ((), ())), preferred_element_type=F32)


def dot_cols(left, right):
    return lax.dot_general(left, right, (((1,), (1,)), ((), ())), preferred_element_type=F32)


def dot(left, right):
    return jnp.dot(left, right, preferred_element_type=F32)


def normalize(values):
    center = jnp.mean(values, axis=-1, keepdims=True)
    deviate = values - center
    spread = jnp.mean(deviate * deviate, axis=-1, keepdims=True)
    inverse = lax.rsqrt(spread + norm_epsilon)
    return deviate * inverse, inverse


def norm_back(hat, inverse, gain, grad):
    scaled = grad * gain
    mean_one = jnp.mean(scaled, axis=-1, keepdims=True)
    mean_two = jnp.mean(scaled * hat, axis=-1, keepdims=True)
    return inverse * (scaled - mean_one - hat * mean_two)


def head_lanes(index, shape):
    lane = lax.broadcasted_iota(jnp.int32, shape, 1)
    return (lane >= index * HEAD_DIM) & (lane < (index + 1) * HEAD_DIM)


def unit_rows(rows, columns):
    row = lax.broadcasted_iota(jnp.int32, (rows, columns), 0)
    column = lax.broadcasted_iota(jnp.int32, (rows, columns), 1)
    return jnp.where(row == column, 1.0, 0.0).astype(BF)


def smem():
    return pl.BlockSpec(memory_space=pltpu.SMEM)


def vmem():
    return pl.BlockSpec(memory_space=pltpu.VMEM)


def whole(*shape):
    return pl.BlockSpec(shape, lambda *index: (0,) * len(shape))


def shaped(shape, kind):
    return jax.ShapeDtypeStruct(shape, kind)


def params(mebibytes):
    return pltpu.CompilerParams(vmem_limit_bytes=mebibytes * 2**20)


COST_SCALE = 1.0


def cost(microseconds):
    return pl.CostEstimate(
        flops=0, transcendentals=0, bytes_accessed=int(microseconds * COST_SCALE * 3.6e6)
    )


def pin(array):
    return pltpu.with_memory_space_constraint(array, pltpu.HBM)


def far_space():
    return pl.BlockSpec(memory_space=pltpu.HBM)


def run(
    kernel,
    name,
    outputs,
    inputs,
    microseconds,
    scratch=(),
    mebibytes=16,
    lazy=(),
    save=(),
    far=(),
    scalars=1,
):
    single = not isinstance(outputs, tuple)
    outputs = [outputs] if single else list(outputs)
    lazy, save, far = list(lazy), list(save), list(far)
    count, produced, own = len(inputs), len(outputs), len(scratch)
    buffers = [pltpu.VMEM(inputs[i].shape, inputs[i].dtype) for i in lazy]
    buffers += [pltpu.VMEM(outputs[i].shape, outputs[i].dtype) for i in far]
    moves = len(lazy) + len(save) + len(far)
    if moves:
        buffers.append(pltpu.SemaphoreType.DMA((moves,)))

    def body(*refs):
        items = list(refs[: count + produced])
        saved = refs[count + produced : count + produced + len(save)]
        rest = refs[count + produced + len(save) :]
        inner, extra = rest[:own], rest[own:]
        copies, number = [], 0
        for j, i in enumerate(lazy):
            copies.append(pltpu.make_async_copy(refs[i], extra[j], extra[-1].at[number]))
            items[i] = extra[j]
            number += 1
        stores = []
        for j, i in enumerate(save):
            stores.append(pltpu.make_async_copy(refs[i], saved[j], extra[-1].at[number]))
            number += 1
        last = []
        for j, i in enumerate(far):
            buffer = extra[len(lazy) + j]
            last.append(pltpu.make_async_copy(buffer, refs[count + i], extra[-1].at[number]))
            items[count + i] = buffer
            number += 1
        for copy in copies + stores:
            copy.start()
        for copy in copies:
            copy.wait()
        kernel(*items, *inner)
        for copy in last:
            copy.start()
        for copy in stores + last:
            copy.wait()

    shapes = [pltpu.HBM(item.shape, item.dtype) if i in far else item for i, item in enumerate(outputs)]
    results = pl.pallas_call(
        body,
        out_shape=shapes + [pltpu.HBM(inputs[i].shape, inputs[i].dtype) for i in save],
        in_specs=[smem()] * scalars
        + [far_space() if i in lazy else vmem() for i in range(scalars, count)],
        out_specs=[far_space() if i in far else vmem() for i in range(produced)]
        + [far_space()] * len(save),
        scratch_shapes=list(scratch) + buffers,
        compiler_params=params(mebibytes),
        cost_estimate=cost(microseconds),
        name=name,
    )(*[pin(item) if i in lazy else item for i, item in enumerate(inputs)])
    return results[0] if single and not save else tuple(results)


GROUPS = 4


def pack_kernel(cols, scal, *refs):
    vector_ref, out_ref = refs[4:6]
    for side in range(2):

        @pl.when(scal[0] % 2 == side)
        def _():
            for i in range(4):
                out_ref[:, i * cols : (i + 1) * cols] = refs[i][
                    :, side * cols : (side + 1) * cols
                ].astype(BF)

    vector = vector_ref[...].astype(BF)
    out_ref[:, 4 * cols :] = dot_rows(vector, unit_rows(vector.shape[0], 128)).astype(BF)


def pack_attention(scal, attention, vector, cols):
    rows = attention.shape[0]

    def pair(i):
        return pl.BlockSpec((rows, 2 * cols), lambda step, scal: (0, 2 * i + scal[0] // 2))

    return pl.pallas_call(
        functools.partial(pack_kernel, cols),
        out_shape=shaped((rows, 4 * cols + 128), BF),
        grid_spec=pltpu.PrefetchScalarGridSpec(
            num_scalar_prefetch=1,
            grid=(1,),
            in_specs=[pair(i) for i in range(4)] + [whole(*vector.shape)],
            out_specs=whole(rows, 4 * cols + 128),
        ),
        compiler_params=params(8),
        cost_estimate=cost(1.5),
        name="pack_attention",
    )(scal, *[attention] * 4, vector)


def cast_kernel(scal, in_ref, out_ref):
    out_ref[...] = in_ref[...].astype(BF)


def pack_forward(scal, forward, part):
    rows = forward.shape[0]
    return pl.pallas_call(
        cast_kernel,
        out_shape=shaped((rows, 2 * part), BF),
        grid_spec=pltpu.PrefetchScalarGridSpec(
            num_scalar_prefetch=1,
            grid=(2,),
            in_specs=[pl.BlockSpec((rows, part), lambda i, scal: (0, GROUPS * i + scal[0]))],
            out_specs=pl.BlockSpec((rows, part), lambda i, scal: (0, i)),
        ),
        compiler_params=params(8),
        cost_estimate=cost(1.5),
        name="pack_forward",
    )(scal, forward)


def place_rows(scal, pieces, target):
    rows = pieces[0].shape[0]
    if len(pieces) == 1:
        target[...] = pieces[0][...]
        return
    for i, piece in enumerate(pieces):
        start = pl.multiple_of(scal[1 + i] * rows, rows)
        target[pl.ds(start, rows), :] = piece[...]


def place_members(scal, pieces, target):
    rows = pieces[0].shape[0]
    for i, piece in enumerate(pieces):
        start = pl.multiple_of((scal[0] ^ i) * rows, rows)
        target[pl.ds(start, rows), :] = piece[...]


def place_kernel(scal, *refs):
    place_members(scal, refs[0:4], refs[4])


def place_blocks(scal, blocks):
    rows, width = blocks[0].shape
    wide = shaped((GROUPS * rows, width), BF)
    return run(place_kernel, "place_blocks", wide, (scal, *blocks), 0.5, mebibytes=2)


def fold(value):
    rows, columns = value.shape
    count = 128 // (columns - 128)
    share = rows // count
    rest = [value[i * share : (i + 1) * share, 128:] for i in range(count)]
    return value[:, :128], jnp.concatenate(rest, axis=1)


def folded_rows(rows, columns):
    return rows + rows * (columns - 128) // 128


def project_kernel(count, cols, scal, seg_ref, x_ref, *refs):
    pieces = refs[:count]
    q_ref, k_ref, v_ref, w_ref, wo_ref, vec_ref, col_ref, a_ref, hat_ref = refs[count : 9 + count]
    weights, wq_ref, wk_ref, wv_ref = refs[9 + count : 13 + count]
    place_rows(scal, pieces, weights)
    for i, ref in enumerate((wq_ref, wk_ref, wv_ref)):
        ref[...] = weights[:, i * cols : (i + 1) * cols]
    w_ref[...] = weights[:, : 3 * cols]
    top, rest = fold(weights[:, 3 * cols : 4 * cols])
    wo_ref[: top.shape[0], :] = top
    wo_ref[top.shape[0] :, :] = rest
    unit = unit_rows(16, 128)
    vec_ref[...] = dot_cols(unit, weights[:, 4 * cols :])
    start = pl.multiple_of(scal[0] * cols, cols)
    own = dot_cols(unit, weights[pl.ds(start, cols), 4 * cols :])
    query_bias, value_bias = own[2:3, :], own[3:4, :]
    gain, shift = vec_ref[0:1, :], vec_ref[1:2, :]
    numbers = jnp.broadcast_to(seg_ref[...].astype(F32), (8, seg_ref.shape[1])).astype(BF)
    col_ref[...] = dot_rows(numbers, unit_rows(8, 128))[:, 0:1].astype(jnp.int32)
    block = 256

    def step(i, carry):
        rows = pl.ds(pl.multiple_of(i * block, block), block)
        hat, _ = normalize(x_ref[rows, :].astype(F32))
        normed = (hat * gain + shift).astype(BF)
        a_ref[rows, :] = normed
        hat_ref[rows, :] = hat.astype(BF)
        q_ref[rows, :] = (dot(normed, wq_ref[...]) + query_bias).astype(BF)
        k_ref[rows, :] = dot(normed, wk_ref[...]).astype(BF)
        v_ref[rows, :] = (dot(normed, wv_ref[...]) + value_bias).astype(BF)
        return carry

    lax.fori_loop(0, x_ref.shape[0] // block, step, 0)


def project(scal, segments, x_all, pieces, cols):
    length, width = x_all.shape
    outputs = (
        (shaped((length, cols), BF),) * 3
        + (shaped((width, 3 * cols), BF),)
        + (shaped((folded_rows(width, cols), 128), BF),)
        + (shaped((16, width), F32), shaped((length, 1), jnp.int32))
        + (shaped((length, width), BF),) * 2
    )
    return run(
        functools.partial(project_kernel, len(pieces), cols),
        "project",
        outputs,
        (scal, segments, x_all, *pieces),
        4.5,
        [pltpu.VMEM((width, 4 * cols + 128), BF)] + [pltpu.VMEM((width, cols), BF)] * 3,
    )


CHUNK = 128
WINDOWS = (4, 5, 8)


def key_window(seg, start, size, length):
    def image(place):
        number = seg[0, place]
        return jnp.where(number < 0, length, number)

    first, last = image(start), image(start + size - 1)
    low, high = jnp.int32(0), jnp.int32(0)
    for chunk in range(length // CHUNK):
        low += (image(chunk * CHUNK + CHUNK - 1) < first).astype(jnp.int32)
        high += (image(chunk * CHUNK) <= last).astype(jnp.int32)
    return low, high - low


def each_window(low, count, length, body):
    chunks = length // CHUNK
    sizes = [size for size in WINDOWS if size < chunks] + [chunks]
    below = 0
    for size in sizes:

        @pl.when((count > below) & (count <= size))
        def _():
            start = jnp.minimum(low, chunks - size) * CHUNK
            body(pl.multiple_of(start, CHUNK), size * CHUNK)

        below = size


def each_head(per, size, body, carry):
    if size > WINDOWS[0] * CHUNK:
        return lax.fori_loop(0, per, body, carry)
    for head in range(per):
        carry = body(head, carry)
    return carry


def attend_kernel(per, first, scal, seg, q_ref, k_ref, v_ref, seg_row_ref, seg_col_ref, *refs):
    out_ref, held = refs[-2:]
    block = 256
    length = k_ref.shape[0]

    def step(i, carry):
        start = pl.multiple_of(first + i * block, block)
        near = pl.ds(pl.multiple_of(i * block, block), block)
        low, count = key_window(seg, start, block, length)

        def body(key_start, size):
            window = pl.ds(key_start, size)
            keys, values = k_ref[window, :], v_ref[window, :]
            same = seg_col_ref[pl.ds(start, block), :] == seg_row_ref[:, window]
            queries = q_ref[pl.ds(start, block), :] * jnp.asarray(HEAD_DIM**-0.5, BF)

            def one(head, result):
                lanes = head_lanes(head, queries.shape)
                score = dot_cols(jnp.where(lanes, queries, jnp.zeros_like(queries)), keys)
                score = jnp.where(same, score, masked_score)
                largest = jnp.max(score, axis=1, keepdims=True)
                power = jnp.exp(score - largest)
                total = jnp.sum(power, axis=1, keepdims=True)
                chance = (power * (1.0 / total)).astype(BF)
                return jnp.where(lanes, dot(chance, values), result)

            result = each_head(per, size, one, jnp.zeros(queries.shape, F32))
            held[near, :] = result.astype(BF)

        each_window(low, count, length, body)
        return carry

    lax.fori_loop(0, held.shape[0] // block, step, 0)
    top, rest = fold(held[...])
    out_ref[: top.shape[0], :] = top
    out_ref[top.shape[0] :, :] = rest


def attend(scal, queries, keys, values, seg_row, seg_col, per, first, count, kept=()):
    inputs = (scal, seg_row, queries, keys, values, seg_row, seg_col, *kept)
    return run(
        functools.partial(attend_kernel, per, first),
        "attend",
        shaped((folded_rows(count, queries.shape[1]), 128), BF),
        inputs,
        7.0 * count / queries.shape[0],
        [pltpu.VMEM((count, queries.shape[1]), BF)],
        save=(2, 3, 4, 6, *range(7, len(inputs))) if kept else (),
        scalars=2,
    )


def forward_kernel(count, cols, parts, scal, x_ref, dy_ref, *refs):
    mixed, w_out = [refs[k * parts : (k + 1) * parts] for k in range(4)], refs[4 * parts :][:4]
    refs = refs[4 * parts + 4 :]
    pieces = refs[:count]
    vec_ref = refs[count]
    c_ref, u_ref, df_ref, keep_ref, send_ref, h_ref, w_ref, rows_ref, sums_ref, o_ref = refs[
        1 + count : 11 + count
    ]
    out_weight = refs[11 + count]
    member = scal[0]
    length, width = x_ref.shape
    part = w_ref.shape[1] // 2
    block = length // GROUPS
    narrow = cols - 128
    place_rows(scal, pieces, w_ref)

    def unfold(target, first, column, item):
        rows = item.shape[0] * 128 // cols
        share = rows * narrow // 128
        target[first : first + rows, column : column + 128] = item[:rows, :]
        for i in range(rows // share):
            start = first + i * share
            target[start : start + share, column + 128 : column + cols] = item[
                rows:, i * narrow : (i + 1) * narrow
            ]

    for index in range(GROUPS):

        @pl.when(member == index)
        def _():
            for k in range(GROUPS):
                column = (index ^ k) * cols
                unfold(out_weight, 0, column, w_out[k])
                for half in range(parts):
                    unfold(o_ref, half * (length // parts), column, mixed[k][half])

    rows_ref[...] = out_weight[pl.ds(pl.multiple_of(member * cols, cols), cols), :]
    zero = jnp.zeros((1, width), F32)
    up_bias = vec_ref[pl.ds(8 + member, 1), :]

    def run_block(step, carry):
        rows = pl.ds(pl.multiple_of(step * block, block), block)
        resid = x_ref[rows, :].astype(F32) + vec_ref[4:5, :] + dot(o_ref[rows, :], out_weight[...])

        @pl.when(step == member)
        def _():
            h_ref[...] = resid

        hat, _ = normalize(resid)
        normed = (hat * vec_ref[5:6, :] + vec_ref[6:7, :]).astype(BF)
        c_ref[rows, :] = normed
        pre = dot(normed, w_ref[:, :part]) + up_bias
        phi = 0.5 * (1.0 + lax.erf(pre * 0.7071067811865476))
        u_ref[rows, :] = (pre * phi).astype(BF)
        slope = phi + pre * (jnp.exp(-0.5 * pre * pre) * 0.3989422804014327)
        grad_pre = (dot(dy_ref[rows, :], w_ref[:, part:]) * slope).astype(BF)
        df_ref[rows, :] = grad_pre
        grad_normed = dot_cols(grad_pre, w_ref[:, :part])
        split_store(member, step, grad_normed, keep_ref, send_ref)
        return (
            carry[0] + jnp.sum(grad_normed * hat, axis=0, keepdims=True),
            carry[1] + jnp.sum(grad_normed, axis=0, keepdims=True),
            carry[2] + jnp.sum(grad_pre.astype(F32), axis=0, keepdims=True),
        )

    carry = lax.fori_loop(0, GROUPS, run_block, (zero, zero, zero))
    sums_ref[...] = jnp.zeros_like(sums_ref)
    for i in range(3):
        sums_ref[i : i + 1, :] = carry[i]


def split_store(member, index, value, keep_ref, send_ref):
    mine = (index % 2) == (member % 2)
    rows = value.shape[0]
    place = pl.ds(pl.multiple_of((index // 2) * rows, rows), rows)

    @pl.when(mine)
    def _():
        keep_ref[place, :] = value

    @pl.when(jnp.logical_not(mine))
    def _():
        send_ref[place, :] = value.astype(BF)


def forward_back(scal, x_all, dy_all, mixed, w_out, pieces, vec, cols):
    length, width = x_all.shape
    part = pieces[0].shape[1] // 2
    rows = length // GROUPS
    outputs = (
        shaped((length, width), BF),
        shaped((length, part), BF),
        shaped((length, part), BF),
        shaped((2 * rows, width), F32),
        shaped((2 * rows, width), BF),
        shaped((rows, width), F32),
        shaped((width, 2 * part), BF),
        shaped((cols, width), BF),
        shaped((8, width), F32),
        shaped((length, width), BF),
    )
    flat = [item for items in mixed for item in items]
    return run(
        functools.partial(forward_kernel, len(pieces), cols, len(mixed[0])),
        "forward_back",
        outputs,
        (scal, x_all, dy_all, *flat, *w_out, *pieces, vec),
        13.0,
        [pltpu.VMEM((width, width), BF)],
    )


def forward_grads_kernel(scal, c_ref, u_ref, df_ref, dy_ref, *refs):
    g_ref = refs[-1]
    part = u_ref.shape[1]
    third = c_ref.shape[1] // 3

    def weight(i, carry):
        lanes = pl.ds(pl.multiple_of(i * third, third), third)
        g_ref[lanes, :part] = dot_rows(c_ref[:, lanes], df_ref[...]).astype(BF)
        g_ref[lanes, part:] = dot_rows(dy_ref[:, lanes], u_ref[...]).astype(BF)
        return carry

    lax.fori_loop(0, 3, weight, 0)


def forward_grads(scal, normed, active, grad_pre, dy_all, kept):
    width = normed.shape[1]
    part = active.shape[1]
    outputs = shaped((width, 2 * part), BF)
    inputs = (scal, normed, active, grad_pre, dy_all, *kept)
    return run(
        forward_grads_kernel,
        "forward_grads",
        outputs,
        inputs,
        4.0,
        save=(2, *range(5, len(inputs))),
    )


def branch_kernel(scal, u_ref, w_ref, dy_ref, keep_ref, send_ref, own_ref):
    own_ref[...] = dy_ref[...]
    part = u_ref.shape[1]
    block = u_ref.shape[0] // GROUPS

    def branch(i, carry):
        rows = pl.ds(pl.multiple_of(i * block, block), block)
        split_store(scal[0], i, dot_cols(u_ref[rows, :], w_ref[:, part:]), keep_ref, send_ref)
        return carry

    lax.fori_loop(0, GROUPS, branch, 0)


def branch_part(scal, active, weights, cotangent):
    rows = active.shape[0] // GROUPS
    width = weights.shape[0]
    return run(
        branch_kernel,
        "branch_part",
        (
            shaped((2 * rows, width), F32),
            shaped((2 * rows, width), BF),
            shaped(cotangent.shape, BF),
        ),
        (scal, active, weights, cotangent),
        3.0,
        lazy=(1, 2, 3),
        far=(0,),
    )


def merge_kernel(scal, keep_ref, got_ref, mine_ref, send_ref):
    rows = mine_ref.shape[0]
    mine = pl.ds(pl.multiple_of((scal[0] // 2) * rows, rows), rows)
    other = pl.ds(pl.multiple_of((1 - scal[0] // 2) * rows, rows), rows)
    mine_ref[...] = keep_ref[mine, :] + got_ref[mine, :].astype(F32)
    send_ref[...] = (keep_ref[other, :] + got_ref[other, :].astype(F32)).astype(BF)


def merge(scal, keep, got, lazy=()):
    rows, width = keep.shape
    outputs = (shaped((rows // 2, width), F32), shaped((rows // 2, width), BF))
    return run(merge_kernel, "merge", outputs, (scal, keep, got), 0.7, mebibytes=8, lazy=lazy)


def resid_kernel(scal, mine_ref, got_ref, h_ref, dy_ref, vec_ref, dh_ref, dp_ref, sums_ref):
    grad = mine_ref[...] + got_ref[...].astype(F32)
    hat, inverse = normalize(h_ref[...])
    dy = dy_ref[...].astype(F32)
    grad_resid = dy + norm_back(hat, inverse, vec_ref[5:6, :], grad)
    dh_ref[...] = grad_resid
    low = grad_resid.astype(BF)
    dp_ref[...] = low
    sums_ref[...] = jnp.zeros_like(sums_ref)
    sums_ref[0:1, :] = jnp.sum(low.astype(F32), axis=0, keepdims=True)
    sums_ref[1:2, :] = jnp.sum(dy, axis=0, keepdims=True)


def resid_back(scal, mine, got, resid, cotangent, vec):
    rows, width = mine.shape
    outputs = (shaped((rows, width), F32), shaped((rows, width), BF), shaped((8, width), F32))
    return run(resid_kernel, "resid_back", outputs, (scal, mine, got, resid, cotangent, vec), 0.8)


def mixed_kernel(cols, scal, *refs):
    grads, (o_ref, rows_ref, do_ref, g_ref, all_ref, own_ref) = refs[0:4], refs[4:10]
    place_members(scal, grads, all_ref)
    do_ref[...] = dot_cols(all_ref[...], rows_ref[...]).astype(BF)
    for index in range(GROUPS):

        @pl.when(scal[0] == index)
        def _():
            own_ref[...] = all_ref[:, index * cols : (index + 1) * cols]

    g_ref[...] = dot_rows(o_ref[...], own_ref[...]).astype(BF)


def mixed_back(scal, grads, mixed, w_rows):
    cols, width = w_rows.shape
    length = mixed.shape[0]
    return run(
        functools.partial(mixed_kernel, cols),
        "mixed_back",
        (shaped((length, cols), BF), shaped((width, cols), BF)),
        (scal, *grads, mixed, w_rows),
        2.5,
        [pltpu.VMEM((length, width), BF), pltpu.VMEM((length, cols), BF)],
        lazy=(5, 6),
    )


def attend_back_kernel(
    per, scal, seg, q_ref, k_ref, v_ref, do_ref, seg_row_ref, seg_col_ref, *refs
):
    out_ref, k_acc, v_acc = refs[-3:]
    cols = q_ref.shape[1]
    block = 256
    length = k_ref.shape[0]
    k_acc[...] = jnp.zeros_like(k_acc)
    v_acc[...] = jnp.zeros_like(v_acc)

    def step(i, carry):
        start = pl.multiple_of(i * block, block)
        rows = pl.ds(start, block)
        low, count = key_window(seg, start, block, length)

        def body(key_start, size):
            window = pl.ds(key_start, size)
            keys, values = k_ref[window, :], v_ref[window, :]
            same = seg_col_ref[window, :] == seg_row_ref[:, rows]
            queries = q_ref[rows, :] * jnp.asarray(HEAD_DIM**-0.5, BF)
            grads = do_ref[rows, :]

            def one(head, carry):
                grad_query, grad_key, grad_value = carry
                lanes = head_lanes(head, queries.shape)
                query = jnp.where(lanes, queries, jnp.zeros_like(queries))
                grad = jnp.where(lanes, grads, jnp.zeros_like(grads))
                score = jnp.where(same, dot_cols(keys, query), masked_score)
                largest = jnp.max(score, axis=0, keepdims=True)
                power = jnp.exp(score - largest)
                total = jnp.sum(power, axis=0, keepdims=True)
                chance = power * (1.0 / total)
                grad_chance = dot_cols(values, grad)
                inner = jnp.sum(chance * grad_chance, axis=0, keepdims=True)
                grad_score = (chance * (grad_chance - inner)).astype(BF)
                return (
                    jnp.where(lanes, dot_rows(grad_score, keys), grad_query),
                    grad_key + dot(grad_score, query),
                    grad_value + dot(chance.astype(BF), grad),
                )

            zeros = jnp.zeros(keys.shape, F32)
            grad_query, grad_key, grad_value = each_head(
                per, size, one, (jnp.zeros(queries.shape, F32), zeros, zeros)
            )
            k_acc[window, :] += grad_key
            v_acc[window, :] += grad_value
            out_ref[rows, :cols] = (grad_query * HEAD_DIM**-0.5).astype(BF)

        each_window(low, count, length, body)
        return carry

    lax.fori_loop(0, q_ref.shape[0] // block, step, 0)
    out_ref[:, cols : 2 * cols] = k_acc[...].astype(BF)
    out_ref[:, 2 * cols :] = v_acc[...].astype(BF)


def attend_back(scal, queries, keys, values, grad_out, seg_row, seg_col, per, kept):
    length, cols = queries.shape
    wide = pltpu.VMEM(queries.shape, F32)
    inputs = (scal, seg_row, queries, keys, values, grad_out, seg_row, seg_col, *kept)
    return run(
        functools.partial(attend_back_kernel, per),
        "attend_back",
        shaped((length, 3 * cols), BF),
        inputs,
        16.0,
        [wide, wide],
        lazy=(2, 3, 4, 7),
        save=range(8, len(inputs)),
        scalars=2,
    )


def query_grads_kernel(cols, scal, *refs):
    a_ref, hat_ref, out_ref, grad_ref, w_ref, forward_ref, resid_ref = refs[0:7]
    g_ref, rows_ref, table_ref = refs[7:10]
    member = scal[0]
    length, width = a_ref.shape
    ones = jnp.ones((length, 8), BF)
    grad = grad_ref[...]
    row = lax.broadcasted_iota(jnp.int32, (8, 3 * cols), 0)
    rest = dot_rows(ones, grad)
    terms = jnp.zeros((8, 3 * cols), F32)
    for term in range(3):
        high = rest.astype(BF).astype(F32)
        terms = jnp.where(row == term, high, terms)
        rest = rest - high
    terms = terms.astype(BF)

    rows_ref[...] = jnp.zeros_like(rows_ref)
    rows_ref[4:5, :] = resid_ref[0:1, :]
    rows_ref[5:7, :] = forward_ref[0:2, :]
    rows_ref[7:8, :] = resid_ref[1:2, :]
    rows_ref[pl.ds(8 + member, 1), :] = forward_ref[2:3, :]
    rest = rows_ref[...]
    unit = unit_rows(16, 128)
    table = jnp.zeros((width, 128), F32)
    for _ in range(3):
        high = rest.astype(BF)
        rest = rest - high.astype(F32)
        table += dot_rows(high, unit)
    table_ref[...] = table

    block = 256
    lane = lax.broadcasted_iota(jnp.int32, (block, 128), 1)

    def step(i, carry):
        lanes = pl.ds(pl.multiple_of(i * block, block), block)
        weight = w_ref[lanes, :]
        g_ref[lanes, : 3 * cols] = dot_rows(a_ref[:, lanes], grad).astype(BF)
        product = dot_rows(hat_ref[:, lanes], grad) * weight.astype(F32)
        gain = jnp.sum(product, axis=1, keepdims=True)
        shift = jnp.sum(dot_cols(weight, terms), axis=1, keepdims=True)
        table = jnp.where(lane == 0, gain, table_ref[lanes, :])
        table_ref[lanes, :] = jnp.where(lane == 1, shift, table)
        return carry

    lax.fori_loop(0, width // block, step, 0)
    g_ref[:, 3 * cols : 4 * cols] = out_ref[...]
    own = pl.ds(pl.multiple_of(member * cols, cols), cols)
    bias = table_ref[own, :]
    near = lax.broadcasted_iota(jnp.int32, (cols, 128), 1)
    for i, column in ((0, 2), (2, 3)):
        part = grad_ref[:, i * cols : (i + 1) * cols]
        bias = jnp.where(near == column, dot_rows(part, ones)[:, 0:1], bias)
    table_ref[own, :] = bias
    total = table_ref[:, 0:16]
    high = total.astype(BF)
    g_ref[:, 4 * cols : 4 * cols + 16] = high
    g_ref[:, 4 * cols + 16 : 4 * cols + 32] = (total - high.astype(F32)).astype(BF)
    g_ref[:, 4 * cols + 32 :] = jnp.zeros((width, 96), BF)


def query_grads(scal, normed, hat, grad_out, grad, weights, sums_forward, sums_resid):
    width, cols = grad_out.shape
    return run(
        functools.partial(query_grads_kernel, cols),
        "query_grads",
        shaped((width, 4 * cols + 128), BF),
        (scal, normed, hat, grad_out, grad, weights, sums_forward, sums_resid),
        4.0,
        [pltpu.VMEM((16, width), F32), pltpu.VMEM((width, 128), F32)],
        lazy=(1, 2, 3, 5, 6, 7),
        far=(0,),
    )


def project_back_kernel(scal, grad_ref, w_ref, keep_ref, send_ref):
    block = grad_ref.shape[0] // GROUPS

    def step(i, carry):
        rows = pl.ds(pl.multiple_of(i * block, block), block)
        split_store(scal[0], i, dot_cols(grad_ref[rows, :], w_ref[...]), keep_ref, send_ref)
        return carry

    lax.fori_loop(0, GROUPS, step, 0)


def project_back(scal, grad, weights):
    rows, width = grad.shape[0] // 2, weights.shape[0]
    return run(
        project_back_kernel,
        "project_back",
        (shaped((rows, width), F32), shaped((rows, width), BF)),
        (scal, grad, weights),
        3.0,
        lazy=(2,),
    )


def input_kernel(scal, mine_ref, got_ref, x_ref, dh_ref, vec_ref, out_ref):
    grad = mine_ref[...] + got_ref[...].astype(F32)
    hat, inverse = normalize(x_ref[...].astype(F32))
    out_ref[...] = dh_ref[...] + norm_back(hat, inverse, vec_ref[0:1, :], grad)


def input_back(scal, mine, got, tokens, grad_resid, vec):
    inputs = (scal, mine, got, tokens, grad_resid, vec)
    return run(input_kernel, "input_back", shaped(mine.shape, F32), inputs, 1.0, lazy=(2, 3, 4, 5))


def output_kernel(scal, mine_ref, got_ref, h_ref, vec_ref, out_ref):
    branch = mine_ref[...] + got_ref[...].astype(F32) + vec_ref[7:8, :]
    out_ref[...] = (h_ref[...] + branch).astype(BF)


def output_sum(scal, mine, got, resid, vec):
    inputs = (scal, mine, got, resid, vec)
    return run(output_kernel, "output_sum", shaped(mine.shape, BF), inputs, 0.8, lazy=(2, 3, 4))


def owned_kernel(scal, in_ref, low_ref):
    total = in_ref[0].astype(F32)
    for i in range(1, in_ref.shape[0]):
        total += in_ref[i].astype(F32)
    low_ref[...] = total.astype(BF)


def owned_sum(scal, pieces):
    outputs = shaped(pieces.shape[1:], BF)
    return run(owned_kernel, "owned_sum", outputs, (scal, pieces), 1.5, lazy=(1,))


def squares_kernel(scal, *refs):
    sums = []
    for piece in refs[:4]:
        wide = piece[...].astype(F32)
        sums.append(jnp.sum(wide * wide))
    total = (sums[0] + sums[1]) + (sums[2] + sums[3])
    refs[4][...] = jnp.full(refs[4].shape, total, F32)


def squares_of(scal, pieces):
    outputs = shaped((8, 128), F32)
    return run(squares_kernel, "squares_of", outputs, (scal, *pieces), 1.0, save=range(1, 5))


def owned_vector_kernel(cols, scal, in_ref, low_ref):
    total = in_ref[0].astype(F32)
    for i in range(1, in_ref.shape[0]):
        total += in_ref[i].astype(F32)
    low_ref[:, : 4 * cols] = total[:, : 4 * cols].astype(BF)
    vector = total[:, 4 * cols :]
    low_ref[:, 4 * cols : 4 * cols + 128] = vector.astype(BF)
    low_ref[:, 4 * cols + 128 :] = (vector - vector.astype(BF).astype(F32)).astype(BF)


def owned_vector(scal, pieces, cols):
    _, rows, width = pieces.shape
    return run(
        functools.partial(owned_vector_kernel, cols),
        "owned_vector",
        shaped((rows, width + 128), BF),
        (scal, pieces),
        1.5,
    )


def join_kernel(cols, count, scal, *refs):
    pieces, forward_ref = refs[0:4], refs[4]
    gradient_ref, vector_ref, squares_ref = refs[5:8]
    width = gradient_ref.shape[1] // 4
    for member in range(GROUPS):

        @pl.when(scal[0] == member)
        def _():
            for i in range(4):
                for k in range(GROUPS):
                    start = i * width + (member ^ k) * cols
                    gradient_ref[:, start : start + cols] = pieces[k][
                        :, i * cols : (i + 1) * cols
                    ].astype(F32)

    def vector_of(piece):
        high = piece[:, 4 * cols : 4 * cols + 128].astype(F32)
        return high + piece[:, 4 * cols + 128 :].astype(F32)

    halves = [vector_of(piece) for piece in pieces]
    table = (halves[0] + halves[1]) + (halves[2] + halves[3])
    rows = lax.broadcasted_iota(jnp.int32, (16, 128), 0)
    lanes = lax.broadcasted_iota(jnp.int32, (16, 128), 1)
    unit = jnp.where((lanes == rows) | (lanes == rows + 16), 1.0, 0.0)
    vector = lax.dot_general(
        unit,
        table,
        (((1,), (1,)), ((), ())),
        preferred_element_type=F32,
        precision=lax.Precision.HIGHEST,
    )[:count]
    vector_ref[...] = vector
    gradient = gradient_ref[...]
    total = jnp.sum(gradient * gradient) + jnp.sum(vector * vector)
    total = forward_ref[...] + total
    for i in range(squares_ref.shape[0] // 8):
        squares_ref[8 * i : 8 * i + 8, :] = total


def join(scal, pieces, squares, width, count, cols, owners):
    rows = pieces[0].shape[0]
    return run(
        functools.partial(join_kernel, cols, count),
        "join",
        (
            shaped((rows, 4 * width), F32),
            shaped((count, rows), F32),
            shaped((8 * owners, 128), F32),
        ),
        (scal, *pieces, squares),
        1.5,
    )


def clip_factor(total_ref):
    total = total_ref[0]
    for i in range(1, total_ref.shape[0]):
        total += total_ref[i]
    norm = jnp.sqrt(total[0:1, 0:1])
    return norm, jnp.minimum(1.0, clip_limit / (norm + 1e-06))


def adam_kernel(counts, scal, total_ref, attention_ref, vector_ref, *refs):
    pieces, sources, targets, norm_ref = refs[0:4], refs[4:16], refs[16:31], refs[31]
    held, copies = refs[32:44], refs[44:47]
    loads, stores = refs[47:50], refs[50:53]
    grads, grad_loads = refs[53:57], refs[57]
    norm, factor = clip_factor(total_ref)
    norm_ref[...] = jnp.broadcast_to(norm, norm_ref.shape)
    decays = (weight_decay, weight_decay, 0.0)

    def chunk(kind, i):
        if counts[kind] == 1:
            return (slice(None), slice(None))
        size = held[4 * kind].shape[1] // counts[kind]
        return (slice(None), pl.ds(pl.multiple_of(i * size, size), size))

    def load(kind, i, state):
        place = chunk(kind, i)
        number = 4 * kind + state
        return pltpu.make_async_copy(
            sources[number].at[place], held[number].at[place], loads[kind].at[i, state]
        )

    def store(kind, i, state):
        place = chunk(kind, i)
        source = held[4 * kind + state] if state < 4 else copies[kind]
        return pltpu.make_async_copy(
            source.at[place], targets[3 * state + kind].at[place], stores[kind].at[i, state]
        )

    def every(kind, action):
        def step(i, carry):
            action(kind, i)
            return carry

        lax.fori_loop(0, counts[kind], step, 0)

    def start(kind, i):
        for state in range(4):
            load(kind, i, state).start()

    def work(kind, i):
        for state in range(4):
            load(kind, i, state).wait()
        place = chunk(kind, i)
        if kind == 0:
            gradient = attention_ref[place]
        elif kind == 2:
            gradient = vector_ref[...]
        else:
            size = held[4].shape[1] // counts[1]
            half = pl.ds(pl.multiple_of((i // GROUPS) * size, size), size)
            source = scal[0] ^ (i % GROUPS)
            gradient = grads[0][:, half]
            for k in range(1, GROUPS):
                gradient = jnp.where(source == k, grads[k][:, half], gradient)
            gradient = gradient.astype(F32)
        results = adam_update(
            *[held[4 * kind + state][place] for state in range(4)], gradient, factor, decays[kind]
        )
        for state, value in zip((0, 1, 2, 3), results):
            held[4 * kind + state][place] = value
        copies[kind][place] = results[0].astype(BF)
        for state in range(5):
            store(kind, i, state).start()

    def finish(kind, i):
        for state in range(5):
            store(kind, i, state).wait()

    moves = [
        pltpu.make_async_copy(piece, grad, grad_loads.at[i])
        for i, (piece, grad) in enumerate(zip(pieces, grads))
    ]
    for move in moves:
        move.start()
    for kind in (1, 0, 2):
        every(kind, start)
    for move in moves:
        move.wait()
    for kind in (1, 0, 2):
        every(kind, work)
    for kind in (1, 0, 2):
        every(kind, finish)


def adam(scal, totals, attention_grad, vector_grad, forward_grads_by_member, states):
    counts = (4, 2 * GROUPS, 1)
    kinds = [states[4 * kind].shape for kind in range(3)]
    out_shape = [pltpu.HBM(shape, F32) for _ in range(4) for shape in kinds]
    out_shape += [pltpu.HBM(shape, BF) for shape in kinds]
    out_shape += [shaped((8, 128), F32)]
    return pl.pallas_call(
        functools.partial(adam_kernel, counts),
        out_shape=out_shape,
        in_specs=[smem()] + [vmem()] * 3 + [far_space()] * 16,
        out_specs=[far_space()] * 15 + [vmem()],
        scratch_shapes=[pltpu.VMEM(kinds[kind], F32) for kind in range(3) for _ in range(4)]
        + [pltpu.VMEM(shape, BF) for shape in kinds]
        + [pltpu.SemaphoreType.DMA((count, 4)) for count in counts]
        + [pltpu.SemaphoreType.DMA((count, 5)) for count in counts]
        + [pltpu.VMEM(item.shape, item.dtype) for item in forward_grads_by_member]
        + [pltpu.SemaphoreType.DMA((GROUPS,))],
        compiler_params=params(32),
        cost_estimate=cost(9.0),
        name="adam",
    )(scal, totals, attention_grad, vector_grad, *map(pin, forward_grads_by_member), *map(pin, states))


def adam_update(master, moment, second, teacher, gradient, factor, decay_rate):
    clipped = gradient * factor
    moment_new = beta_one * moment + (1.0 - beta_one) * clipped
    second_new = beta_two * second + (1.0 - beta_two) * clipped * clipped
    scale_one = 1.0 - beta_one**ADAM_STEP
    scale_two = 1.0 - beta_two**ADAM_STEP
    update = (moment_new * (1.0 / scale_one)) / (
        jnp.sqrt(second_new * (1.0 / scale_two)) + adam_epsilon
    )
    master_new = master * (1.0 - learn_rate * decay_rate) - learn_rate * update
    teacher_new = teacher_keep * teacher + (1.0 - teacher_keep) * master_new
    return (master_new, moment_new, second_new, teacher_new)


def swap(part, bit):
    return lax.ppermute(part, "head", [(i, i ^ bit) for i in range(4)])


def spread(part, *others):
    across = swap(part, 2)
    if others:
        return [
            part,
            swap(after(part, *others), 1),
            across,
            swap(after(across, *others), 1),
        ]
    return [part, swap(part, 1), across, swap(across, 1)]


RING = (0, 2, 4, 6, 7, 5, 3, 1)


def ring_owners(count):
    if count != len(RING):
        return np.zeros((count, 1), np.int32)
    table = []
    for device in range(count):
        place = RING.index(device)
        owners = [device]
        for hop in range(1, count // 2 + 1):
            owners.append(RING[(place - hop) % count])
            if hop < count // 2:
                owners.append(RING[(place + hop) % count])
        table.append(owners)
    return np.asarray(table, np.int32)


def after(value, *others):
    return lax.optimization_barrier((value, *others))[0]


class Ring:
    def __init__(self, block, count):
        self.count = count
        self.hops = count // 2 if count == len(RING) else 1
        self.front = self.rear = block
        self.pieces = [block]
        self.done = 0

    def hop(self, *others):
        self.done += 1
        if self.count != len(RING):
            self.pieces = [lax.all_gather(after(self.front, *others), "dp", axis=0, tiled=True)]
            return self
        ahead = [(RING[i], RING[(i + 1) % self.count]) for i in range(self.count)]
        back = [(target, source) for source, target in ahead]
        last = self.done == self.hops
        if self.done > 1 or others:
            self.front, self.rear = lax.optimization_barrier((self.front, self.rear, *others))[:2]
        self.front = lax.ppermute(self.front, "dp", ahead)
        self.pieces.append(self.front)
        if not last:
            self.rear = lax.ppermute(self.rear, "dp", back)
            self.pieces.append(self.rear)
        return self

    def rest(self):
        while self.done < self.hops:
            self.hop()
        return self.pieces


def exchange_owned(grads, count):
    blocks = grads.reshape(count, -1, grads.shape[1])
    return lax.all_to_all(blocks, "dp", split_axis=0, concat_axis=0)


def local(
    tokens,
    cotangent,
    segments,
    attention_master,
    feedforward_master,
    vector_master,
    attention_moment,
    feedforward_moment,
    vector_moment,
    attention_second,
    feedforward_second,
    vector_second,
    attention_teacher,
    feedforward_teacher,
    vector_teacher,
):
    width = tokens.shape[1]
    owners = lax.axis_size("dp")
    groups = lax.axis_size("head")
    hidden = feedforward_master.shape[1] // 2
    per = HEADS // groups
    cols = per * HEAD_DIM
    part = hidden // groups

    owner_table = ring_owners(owners)
    table = np.concatenate(
        [
            np.tile(np.arange(groups, dtype=np.int32), owners)[:, None],
            np.repeat(owner_table, groups, axis=0),
        ],
        axis=1,
    )
    place = lax.axis_index("dp") * groups + lax.axis_index("head")
    scal = lax.dynamic_index_in_dim(jnp.asarray(table), place, 0, keepdims=False)
    first = Ring(pack_attention(scal, attention_master, vector_master, cols), owners)
    first.rest()
    ringed = owners == len(RING)
    early = first.pieces[-3:-1] if ringed else first.pieces
    token_across, grad_across = swap(tokens, 2), swap(cotangent, 2)
    token, token_across = lax.optimization_barrier((tokens, token_across, *early))[:2]
    x_all = place_blocks(scal, [token, swap(token, 1), token_across, swap(token_across, 1)])
    second = Ring(pack_forward(scal, feedforward_master, part), owners)
    second.hop(first.pieces[-1])

    queries, keys, values, w_qkv, w_o, vec, seg_col, normed, hat = project(
        scal, segments, x_all, first.pieces, cols
    )
    half = x_all.shape[0] // 2
    w_across = swap(w_o, 2)
    mixed_low, *kept = attend(
        scal,
        after(queries, grad_across),
        keys,
        values,
        segments,
        seg_col,
        per,
        0,
        half,
        (w_qkv, vec, normed, hat),
    )
    far_q, far_k, far_v, far_col, far_weights, far_vec, *far_normed = kept
    low_across = swap(mixed_low, 2)
    w_across = after(w_across, mixed_low)
    if ringed:
        second.hop(mixed_low)
    mixed_high = attend(
        scal, after(queries, w_across), keys, values, segments, seg_col, per, half, half
    )
    high_across = swap(after(mixed_high, low_across), 2)
    if ringed:
        second.hop(mixed_high)
    w_across, low_across, w_o, mixed_low, grad, grad_across = lax.optimization_barrier(
        (w_across, low_across, w_o, mixed_low, cotangent, grad_across, high_across)
    )[:6]
    dy_all = place_blocks(scal, [grad, swap(grad, 1), grad_across, swap(grad_across, 1)])
    w_out = [w_o, swap(w_o, 1), w_across, swap(w_across, 1)]
    mixed = [
        (mixed_low, mixed_high),
        (swap(mixed_low, 1), swap(mixed_high, 1)),
        (low_across, high_across),
        (swap(low_across, 1), swap(high_across, 1)),
    ]
    (
        normed_two,
        active,
        grad_pre,
        keep,
        send,
        resid,
        w_ff,
        w_rows,
        sums_forward,
        mixed_all,
    ) = forward_back(scal, x_all, dy_all, mixed, w_out, second.rest(), vec, cols)
    grad_ff, far_active, *kept = forward_grads(
        scal,
        normed_two,
        active,
        grad_pre,
        dy_all,
        (resid, sums_forward, w_rows, w_ff, mixed_all),
    )
    far_resid, far_sums, far_rows, far_ff, far_mixed = kept
    got = swap(send, 1)
    grad_ff, got = lax.optimization_barrier((grad_ff, got))
    owned_ff = exchange_owned(grad_ff, owners)
    mine, send = merge(scal, keep, got)
    keep_branch, send_branch, cot_own = branch_part(
        scal, far_active, after(far_ff, send), cotangent
    )
    got = swap(send, 2)
    grad_resid, grad_low, sums_resid = resid_back(
        scal, after(mine, send_branch), got, resid, cot_own, vec
    )
    low_blocks = spread(grad_low)
    mine, send = merge(
        scal, keep_branch, swap(after(send_branch, grad_low), 1), lazy=(1,)
    )
    low_blocks[0] = after(low_blocks[0], send)
    grad_mixed, grad_out = mixed_back(scal, low_blocks, far_mixed, far_rows)
    grad_qkv, far_dh, far_sums_resid, far_grad_out = attend_back(
        scal,
        far_q,
        far_k,
        far_v,
        grad_mixed,
        segments,
        far_col,
        per,
        (grad_resid, sums_resid, grad_out),
    )
    got_branch = swap(send, 2)
    pack = query_grads(
        scal,
        after(far_normed[0], got_branch),
        far_normed[1],
        far_grad_out,
        grad_qkv,
        far_weights,
        far_sums,
        far_sums_resid,
    )
    owned_pack = exchange_owned(pack, owners)
    forward_parts = spread(owned_sum(scal, after(owned_ff, pack)))
    forward_squares, *forward_parts = squares_of(scal, forward_parts)
    keep, send = project_back(scal, grad_qkv, after(far_weights, pack))
    mine_input, send = merge(scal, keep, swap(send, 1))
    block_output = output_sum(scal, after(mine, pack), got_branch, far_resid, far_vec)
    got_input = swap(send, 2)
    owned_pack = after(owned_pack, block_output, forward_squares, got_input)
    input_gradient = input_back(scal, mine_input, got_input, tokens, far_dh, far_vec)
    attention_parts = spread(owned_vector(scal, owned_pack, cols))
    attention_grad, vector_grad, squares = join(
        scal, attention_parts, forward_squares, width, vector_master.shape[0], cols, owners
    )
    totals = lax.all_to_all(
        squares.reshape(owners, 8, 128), "dp", split_axis=0, concat_axis=0
    )
    *results, norm = adam(
        scal,
        totals,
        attention_grad,
        vector_grad,
        forward_parts,
        (
            attention_master,
            attention_moment,
            attention_second,
            attention_teacher,
            feedforward_master,
            feedforward_moment,
            feedforward_second,
            feedforward_teacher,
            vector_master,
            vector_moment,
            vector_second,
            vector_teacher,
        ),
    )
    return (block_output, input_gradient, norm[0, 0], *results)


def solution(mesh):
    rows = P(("dp", "head"), None)
    shard = P("dp", None)
    vector = P(None, "dp")
    return jax.shard_map(
        local,
        mesh=mesh,
        in_specs=(rows, rows, shard) + (shard, shard, vector) * 4,
        out_specs=(rows, rows, P()) + (shard, shard, vector) * 5,
        check_vma=False,
    )
```

```python
import functools

import jax
import jax.numpy as jnp
import numpy as np
from jax import lax
from jax.experimental import pallas as pl
from jax.experimental.pallas import tpu as pltpu
from jax.sharding import PartitionSpec as P

HEADS = 12
HEAD_DIM = 64
ADAM_STEP = 3

norm_epsilon = 1e-06
beta_one = 0.5
beta_two = 0.5
adam_epsilon = 1e-08
learn_rate = 0.05
weight_decay = 0.05
teacher_keep = 0.8
clip_limit = 1.0
masked_score = -1e30

BF = jnp.bfloat16
F32 = jnp.float32


def dot_rows(left, right):
    return lax.dot_general(left, right, (((0,), (0,)), ((), ())), preferred_element_type=F32)


def dot_cols(left, right):
    return lax.dot_general(left, right, (((1,), (1,)), ((), ())), preferred_element_type=F32)


def dot(left, right):
    return jnp.dot(left, right, preferred_element_type=F32)


def normalize(values):
    center = jnp.mean(values, axis=-1, keepdims=True)
    deviate = values - center
    spread = jnp.mean(deviate * deviate, axis=-1, keepdims=True)
    inverse = lax.rsqrt(spread + norm_epsilon)
    return deviate * inverse, inverse


def norm_back(hat, inverse, gain, grad):
    scaled = grad * gain
    mean_one = jnp.mean(scaled, axis=-1, keepdims=True)
    mean_two = jnp.mean(scaled * hat, axis=-1, keepdims=True)
    return inverse * (scaled - mean_one - hat * mean_two)


def head_lanes(index, shape):
    lane = lax.broadcasted_iota(jnp.int32, shape, 1)
    return (lane >= index * HEAD_DIM) & (lane < (index + 1) * HEAD_DIM)


def unit_rows(rows, columns):
    row = lax.broadcasted_iota(jnp.int32, (rows, columns), 0)
    column = lax.broadcasted_iota(jnp.int32, (rows, columns), 1)
    return jnp.where(row == column, 1.0, 0.0).astype(BF)


def smem():
    return pl.BlockSpec(memory_space=pltpu.SMEM)


def vmem():
    return pl.BlockSpec(memory_space=pltpu.VMEM)


def whole(*shape):
    return pl.BlockSpec(shape, lambda *index: (0,) * len(shape))


def shaped(shape, kind):
    return jax.ShapeDtypeStruct(shape, kind)


def params(mebibytes):
    return pltpu.CompilerParams(vmem_limit_bytes=mebibytes * 2**20)


COST_SCALE = 1.0


def cost(microseconds):
    return pl.CostEstimate(
        flops=0, transcendentals=0, bytes_accessed=int(microseconds * COST_SCALE * 3.6e6)
    )


def pin(array):
    return pltpu.with_memory_space_constraint(array, pltpu.HBM)


def far_space():
    return pl.BlockSpec(memory_space=pltpu.HBM)


def run(
    kernel,
    name,
    outputs,
    inputs,
    microseconds,
    scratch=(),
    mebibytes=16,
    lazy=(),
    save=(),
    far=(),
    late=(),
    scalars=1,
    scalar_outputs=(),
):
    single = not isinstance(outputs, tuple)
    outputs = [outputs] if single else list(outputs)
    lazy, save, far = list(lazy), list(save), list(far)
    count, produced, own = len(inputs), len(outputs), len(scratch)
    buffers = [pltpu.VMEM(inputs[i].shape, inputs[i].dtype) for i in lazy]
    buffers += [pltpu.VMEM(outputs[i].shape, outputs[i].dtype) for i in far]
    moves = len(lazy) + len(save) + len(far)
    if moves:
        buffers.append(pltpu.SemaphoreType.DMA((moves,)))

    def body(*refs):
        items = list(refs[: count + produced])
        saved = refs[count + produced : count + produced + len(save)]
        rest = refs[count + produced + len(save) :]
        inner, extra = rest[:own], rest[own:]
        copies, number = [], 0
        for j, i in enumerate(lazy):
            copies.append(pltpu.make_async_copy(refs[i], extra[j], extra[-1].at[number]))
            items[i] = extra[j]
            number += 1
        stores = []
        for j, i in enumerate(save):
            stores.append(pltpu.make_async_copy(refs[i], saved[j], extra[-1].at[number]))
            number += 1
        last = []
        for j, i in enumerate(far):
            buffer = extra[len(lazy) + j]
            last.append(pltpu.make_async_copy(buffer, refs[count + i], extra[-1].at[number]))
            items[count + i] = buffer
            number += 1
        for copy in copies + stores:
            copy.start()
        for i, copy in zip(lazy, copies):
            if i not in late:
                copy.wait()
        if late:
            kernel(*items, *inner, ready=lambda i: copies[lazy.index(i)].wait())
        else:
            kernel(*items, *inner)
        for copy in last:
            copy.start()
        for copy in stores + last:
            copy.wait()

    shapes = [pltpu.HBM(item.shape, item.dtype) if i in far else item for i, item in enumerate(outputs)]
    results = pl.pallas_call(
        body,
        out_shape=shapes + [pltpu.HBM(inputs[i].shape, inputs[i].dtype) for i in save],
        in_specs=[smem()] * scalars
        + [far_space() if i in lazy else vmem() for i in range(scalars, count)],
        out_specs=[
            far_space() if i in far else smem() if i in scalar_outputs else vmem()
            for i in range(produced)
        ]
        + [far_space()] * len(save),
        scratch_shapes=list(scratch) + buffers,
        compiler_params=params(mebibytes),
        cost_estimate=cost(microseconds),
        name=name,
    )(*[pin(item) if i in lazy else item for i, item in enumerate(inputs)])
    return results[0] if single and not save else tuple(results)


GROUPS = 4


def pack_kernel(cols, scal, *refs):
    vector_ref, out_ref = refs[4:6]
    for side in range(2):

        @pl.when(scal[0] % 2 == side)
        def _():
            for i in range(4):
                out_ref[:, i * cols : (i + 1) * cols] = refs[i][
                    :, side * cols : (side + 1) * cols
                ].astype(BF)

    vector = vector_ref[...].astype(BF)
    out_ref[:, 4 * cols :] = dot_rows(vector, unit_rows(vector.shape[0], 128)).astype(BF)


def pack_attention(scal, attention, vector, cols):
    rows = attention.shape[0]

    def pair(i):
        return pl.BlockSpec((rows, 2 * cols), lambda step, scal: (0, 2 * i + scal[0] // 2))

    return pl.pallas_call(
        functools.partial(pack_kernel, cols),
        out_shape=shaped((rows, 4 * cols + 128), BF),
        grid_spec=pltpu.PrefetchScalarGridSpec(
            num_scalar_prefetch=1,
            grid=(1,),
            in_specs=[pair(i) for i in range(4)] + [whole(*vector.shape)],
            out_specs=whole(rows, 4 * cols + 128),
        ),
        compiler_params=params(8),
        cost_estimate=cost(1.5),
        name="pack_attention",
    )(scal, *[attention] * 4, vector)


def cast_kernel(scal, in_ref, out_ref):
    out_ref[...] = in_ref[...].astype(BF)


def pack_forward(scal, forward, part):
    rows = forward.shape[0]
    return pl.pallas_call(
        cast_kernel,
        out_shape=shaped((rows, 2 * part), BF),
        grid_spec=pltpu.PrefetchScalarGridSpec(
            num_scalar_prefetch=1,
            grid=(2,),
            in_specs=[pl.BlockSpec((rows, part), lambda i, scal: (0, GROUPS * i + scal[0]))],
            out_specs=pl.BlockSpec((rows, part), lambda i, scal: (0, i)),
        ),
        compiler_params=params(8),
        cost_estimate=cost(1.5),
        name="pack_forward",
    )(scal, forward)


def place_rows(scal, pieces, target):
    rows = pieces[0].shape[0]
    if len(pieces) == 1:
        target[...] = pieces[0][...]
        return
    for i, piece in enumerate(pieces):
        size = piece.shape[0]
        first = rows - size if i == len(RING) else 0
        start = pl.multiple_of(scal[1 + i] * rows + first, size)
        target[pl.ds(start, size), :] = piece[...]


def place_members(scal, pieces, target):
    rows = pieces[0].shape[0]
    for i, piece in enumerate(pieces):
        start = pl.multiple_of((scal[0] ^ i) * rows, rows)
        target[pl.ds(start, rows), :] = piece[...]


def place_kernel(scal, *refs):
    place_members(scal, refs[0:4], refs[4])


def place_blocks(scal, blocks):
    rows, width = blocks[0].shape
    wide = shaped((GROUPS * rows, width), BF)
    return run(place_kernel, "place_blocks", wide, (scal, *blocks), 0.5, mebibytes=2)


def fold(value):
    rows, columns = value.shape
    count = 128 // (columns - 128)
    share = rows // count
    rest = [value[i * share : (i + 1) * share, 128:] for i in range(count)]
    return value[:, :128], jnp.concatenate(rest, axis=1)


def folded_rows(rows, columns):
    return rows + rows * (columns - 128) // 128


def project_kernel(count, cols, scal, seg_ref, x_ref, *refs):
    pieces = refs[:count]
    q_ref, k_ref, v_ref, w_ref, wo_ref, vec_ref, col_ref, a_ref, hat_ref, ranges_ref = refs[
        count : 10 + count
    ]
    weights, wq_ref, wk_ref, wv_ref = refs[10 + count : 14 + count]
    key_ranges(seg_ref[...], ranges_ref)
    place_rows(scal, pieces, weights)
    for i, ref in enumerate((wq_ref, wk_ref, wv_ref)):
        ref[...] = weights[:, i * cols : (i + 1) * cols]
    w_ref[...] = weights[:, : 3 * cols]
    top, rest = fold(weights[:, 3 * cols : 4 * cols])
    wo_ref[: top.shape[0], :] = top
    wo_ref[top.shape[0] :, :] = rest
    unit = unit_rows(16, 128)
    vec_ref[...] = dot_cols(unit, weights[:, 4 * cols :])
    start = pl.multiple_of(scal[0] * cols, cols)
    own = dot_cols(unit, weights[pl.ds(start, cols), 4 * cols :])
    query_bias, value_bias = own[2:3, :], own[3:4, :]
    gain, shift = vec_ref[0:1, :], vec_ref[1:2, :]
    numbers = jnp.broadcast_to(seg_ref[...].astype(F32), (8, seg_ref.shape[1])).astype(BF)
    col_ref[...] = dot_rows(numbers, unit_rows(8, 128))[:, 0:1].astype(jnp.int32)
    block = 256

    def step(i, carry):
        rows = pl.ds(pl.multiple_of(i * block, block), block)
        hat, _ = normalize(x_ref[rows, :].astype(F32))
        normed = (hat * gain + shift).astype(BF)
        a_ref[rows, :] = normed
        hat_ref[rows, :] = hat.astype(BF)
        q_ref[rows, :] = (dot(normed, wq_ref[...]) + query_bias).astype(BF)
        k_ref[rows, :] = dot(normed, wk_ref[...]).astype(BF)
        v_ref[rows, :] = (dot(normed, wv_ref[...]) + value_bias).astype(BF)
        return carry

    lax.fori_loop(0, x_ref.shape[0] // block, step, 0)


def project(scal, segments, x_all, pieces, cols):
    length, width = x_all.shape
    outputs = (
        (shaped((length, cols), BF),) * 3
        + (shaped((width, 3 * cols), BF),)
        + (shaped((folded_rows(width, cols), 128), BF),)
        + (shaped((16, width), F32), shaped((length, 1), jnp.int32))
        + (shaped((length, width), BF),) * 2
        + (shaped((16,), jnp.int32),)
    )
    return run(
        functools.partial(project_kernel, len(pieces), cols),
        "project",
        outputs,
        (scal, segments, x_all, *pieces),
        4.5,
        scalar_outputs=(9,),
        scratch=[pltpu.VMEM((width, 4 * cols + 128), BF)] + [pltpu.VMEM((width, cols), BF)] * 3,
    )


QUERIES = 256
WINDOWS = (512, 576)


def key_ranges(numbers, ranges_ref):
    length = numbers.shape[1]
    images = jnp.where(numbers < 0, length, numbers)
    place = lax.broadcasted_iota(jnp.int32, numbers.shape, 1)
    for block in range(length // QUERIES):
        first = jnp.max(jnp.where(place == block * QUERIES, images, 0))
        last = jnp.max(jnp.where(place == (block + 1) * QUERIES - 1, images, 0))
        ranges_ref[2 * block] = jnp.sum((images < first).astype(jnp.int32))
        ranges_ref[2 * block + 1] = jnp.sum((images <= last).astype(jnp.int32))


def each_window(ranges, block, length, body):
    low, high = ranges[2 * block], ranges[2 * block + 1]
    taken = jnp.bool_(False)
    for size in [size for size in WINDOWS if size < length] + [length]:
        start = (jnp.minimum(low, length - size) // 16) * 16
        fits = high - start <= size

        @pl.when(fits & jnp.logical_not(taken))
        def _():
            body(pl.multiple_of(start, 16), size)

        taken = taken | fits


def each_head(per, size, body, carry):
    if size > WINDOWS[0]:
        return lax.fori_loop(0, per, body, carry)
    for head in range(per):
        carry = body(head, carry)
    return carry


def attend_kernel(per, first, scal, ranges, q_ref, k_ref, v_ref, seg_row_ref, seg_col_ref, *refs):
    out_ref, held = refs[-2:]
    block = QUERIES
    length = k_ref.shape[0]

    def step(i, carry):
        start = pl.multiple_of(first + i * block, block)
        near = pl.ds(pl.multiple_of(i * block, block), block)

        def body(key_start, size):
            window = pl.ds(key_start, size)
            keys, values = k_ref[window, :], v_ref[window, :]
            numbers = seg_row_ref[...]
            if size < length:
                span = size - size % 128 + 256
                base = jnp.minimum(key_start // 128, (length - span) // 128) * 128
                numbers = seg_row_ref[:, pl.ds(pl.multiple_of(base, 128), span)]
                numbers = jnp.broadcast_to(numbers, (8, span))
                numbers = pltpu.roll(numbers, span - (key_start - base), 1)[0:1, :size]
            same = seg_col_ref[pl.ds(start, block), :] == numbers
            queries = q_ref[pl.ds(start, block), :] * jnp.asarray(HEAD_DIM**-0.5, BF)

            def one(head, result):
                lanes = head_lanes(head, queries.shape)
                score = dot_cols(jnp.where(lanes, queries, jnp.zeros_like(queries)), keys)
                score = jnp.where(same, score, masked_score)
                largest = jnp.max(score, axis=1, keepdims=True)
                power = jnp.exp(score - largest)
                total = jnp.sum(power, axis=1, keepdims=True)
                chance = (power * (1.0 / total)).astype(BF)
                return jnp.where(lanes, dot(chance, values), result)

            result = each_head(per, size, one, jnp.zeros(queries.shape, F32))
            held[near, :] = result.astype(BF)

        each_window(ranges, first // block + i, length, body)
        return carry

    lax.fori_loop(0, held.shape[0] // block, step, 0)
    top, rest = fold(held[...])
    out_ref[: top.shape[0], :] = top
    out_ref[top.shape[0] :, :] = rest


def attend(scal, ranges, queries, keys, values, seg_row, seg_col, per, first, count, kept=()):
    inputs = (scal, ranges, queries, keys, values, seg_row, seg_col, *kept)
    return run(
        functools.partial(attend_kernel, per, first),
        "attend",
        shaped((folded_rows(count, queries.shape[1]), 128), BF),
        inputs,
        7.0 * count / queries.shape[0],
        [pltpu.VMEM((count, queries.shape[1]), BF)],
        save=(2, 3, 4, 6, *range(7, len(inputs))) if kept else (),
        scalars=2,
    )


def forward_kernel(count, cols, parts, scal, x_ref, dy_ref, *refs):
    mixed, w_out = [refs[k * parts : (k + 1) * parts] for k in range(4)], refs[4 * parts :][:4]
    refs = refs[4 * parts + 4 :]
    pieces = refs[:count]
    vec_ref = refs[count]
    c_ref, u_ref, df_ref, keep_ref, send_ref, h_ref, w_ref, rows_ref, sums_ref, o_ref = refs[
        1 + count : 11 + count
    ]
    out_weight = refs[11 + count]
    member = scal[0]
    length, width = x_ref.shape
    part = w_ref.shape[1] // 2
    block = length // GROUPS
    narrow = cols - 128
    place_rows(scal, pieces, w_ref)

    def unfold(target, first, column, item):
        rows = item.shape[0] * 128 // cols
        share = rows * narrow // 128
        target[first : first + rows, column : column + 128] = item[:rows, :]
        for i in range(rows // share):
            start = first + i * share
            target[start : start + share, column + 128 : column + cols] = item[
                rows:, i * narrow : (i + 1) * narrow
            ]

    for index in range(GROUPS):

        @pl.when(member == index)
        def _():
            for k in range(GROUPS):
                column = (index ^ k) * cols
                unfold(out_weight, 0, column, w_out[k])
                for half in range(parts):
                    unfold(o_ref, half * (length // parts), column, mixed[k][half])

    rows_ref[...] = out_weight[pl.ds(pl.multiple_of(member * cols, cols), cols), :]
    zero = jnp.zeros((1, width), F32)
    up_bias = vec_ref[pl.ds(8 + member, 1), :]

    def run_block(step, carry):
        rows = pl.ds(pl.multiple_of(step * block, block), block)
        resid = x_ref[rows, :].astype(F32) + vec_ref[4:5, :] + dot(o_ref[rows, :], out_weight[...])

        @pl.when(step == member)
        def _():
            h_ref[...] = resid

        hat, _ = normalize(resid)
        normed = (hat * vec_ref[5:6, :] + vec_ref[6:7, :]).astype(BF)
        c_ref[rows, :] = normed
        pre = dot(normed, w_ref[:, :part]) + up_bias
        phi = 0.5 * (1.0 + lax.erf(pre * 0.7071067811865476))
        u_ref[rows, :] = (pre * phi).astype(BF)
        slope = phi + pre * (jnp.exp(-0.5 * pre * pre) * 0.3989422804014327)
        grad_pre = (dot(dy_ref[rows, :], w_ref[:, part:]) * slope).astype(BF)
        df_ref[rows, :] = grad_pre
        grad_normed = dot_cols(grad_pre, w_ref[:, :part])
        split_store(member, step, grad_normed, keep_ref, send_ref)
        return (
            carry[0] + jnp.sum(grad_normed * hat, axis=0, keepdims=True),
            carry[1] + jnp.sum(grad_normed, axis=0, keepdims=True),
            carry[2] + jnp.sum(grad_pre.astype(F32), axis=0, keepdims=True),
        )

    carry = lax.fori_loop(0, GROUPS, run_block, (zero, zero, zero))
    sums_ref[...] = jnp.zeros_like(sums_ref)
    for i in range(3):
        sums_ref[i : i + 1, :] = carry[i]


def split_store(member, index, value, keep_ref, send_ref):
    mine = (index % 2) == (member % 2)
    rows = value.shape[0]
    place = pl.ds(pl.multiple_of((index // 2) * rows, rows), rows)

    @pl.when(mine)
    def _():
        keep_ref[place, :] = value

    @pl.when(jnp.logical_not(mine))
    def _():
        send_ref[place, :] = value.astype(BF)


def forward_back(scal, x_all, dy_all, mixed, w_out, pieces, vec, cols):
    length, width = x_all.shape
    part = pieces[0].shape[1] // 2
    rows = length // GROUPS
    outputs = (
        shaped((length, width), BF),
        shaped((length, part), BF),
        shaped((length, part), BF),
        shaped((2 * rows, width), F32),
        shaped((2 * rows, width), BF),
        shaped((rows, width), F32),
        shaped((width, 2 * part), BF),
        shaped((cols, width), BF),
        shaped((8, width), F32),
        shaped((length, width), BF),
    )
    flat = [item for items in mixed for item in items]
    return run(
        functools.partial(forward_kernel, len(pieces), cols, len(mixed[0])),
        "forward_back",
        outputs,
        (scal, x_all, dy_all, *flat, *w_out, *pieces, vec),
        13.0,
        [pltpu.VMEM((width, width), BF)],
    )


def forward_grads_kernel(scal, c_ref, u_ref, df_ref, dy_ref, *refs):
    g_ref = refs[-1]
    part = u_ref.shape[1]
    third = c_ref.shape[1] // 3

    def weight(i, carry):
        lanes = pl.ds(pl.multiple_of(i * third, third), third)
        g_ref[lanes, :part] = dot_rows(c_ref[:, lanes], df_ref[...]).astype(BF)
        g_ref[lanes, part:] = dot_rows(dy_ref[:, lanes], u_ref[...]).astype(BF)
        return carry

    lax.fori_loop(0, 3, weight, 0)


def forward_grads(scal, normed, active, grad_pre, dy_all, kept):
    width = normed.shape[1]
    part = active.shape[1]
    outputs = shaped((width, 2 * part), BF)
    inputs = (scal, normed, active, grad_pre, dy_all, *kept)
    return run(
        forward_grads_kernel,
        "forward_grads",
        outputs,
        inputs,
        4.0,
        save=(2, *range(5, len(inputs))),
    )


def branch_kernel(scal, u_ref, w_ref, dy_ref, keep_ref, send_ref, own_ref):
    own_ref[...] = dy_ref[...]
    part = u_ref.shape[1]
    block = u_ref.shape[0] // GROUPS

    def branch(i, carry):
        rows = pl.ds(pl.multiple_of(i * block, block), block)
        split_store(scal[0], i, dot_cols(u_ref[rows, :], w_ref[:, part:]), keep_ref, send_ref)
        return carry

    lax.fori_loop(0, GROUPS, branch, 0)


def branch_part(scal, active, weights, cotangent):
    rows = active.shape[0] // GROUPS
    width = weights.shape[0]
    return run(
        branch_kernel,
        "branch_part",
        (
            shaped((2 * rows, width), F32),
            shaped((2 * rows, width), BF),
            shaped(cotangent.shape, BF),
        ),
        (scal, active, weights, cotangent),
        3.0,
        lazy=(1, 2, 3),
        far=(0,),
    )


def merge_kernel(scal, keep_ref, got_ref, mine_ref, send_ref):
    rows = mine_ref.shape[0]
    mine = pl.ds(pl.multiple_of((scal[0] // 2) * rows, rows), rows)
    other = pl.ds(pl.multiple_of((1 - scal[0] // 2) * rows, rows), rows)
    mine_ref[...] = keep_ref[mine, :] + got_ref[mine, :].astype(F32)
    send_ref[...] = (keep_ref[other, :] + got_ref[other, :].astype(F32)).astype(BF)


def merge(scal, keep, got, lazy=()):
    rows, width = keep.shape
    outputs = (shaped((rows // 2, width), F32), shaped((rows // 2, width), BF))
    return run(merge_kernel, "merge", outputs, (scal, keep, got), 0.7, mebibytes=8, lazy=lazy)


def resid_kernel(scal, mine_ref, got_ref, h_ref, dy_ref, vec_ref, dh_ref, dp_ref, sums_ref):
    grad = mine_ref[...] + got_ref[...].astype(F32)
    hat, inverse = normalize(h_ref[...])
    dy = dy_ref[...].astype(F32)
    grad_resid = dy + norm_back(hat, inverse, vec_ref[5:6, :], grad)
    dh_ref[...] = grad_resid
    low = grad_resid.astype(BF)
    dp_ref[...] = low
    sums_ref[...] = jnp.zeros_like(sums_ref)
    sums_ref[0:1, :] = jnp.sum(low.astype(F32), axis=0, keepdims=True)
    sums_ref[1:2, :] = jnp.sum(dy, axis=0, keepdims=True)


def resid_back(scal, mine, got, resid, cotangent, vec):
    rows, width = mine.shape
    outputs = (shaped((rows, width), F32), shaped((rows, width), BF), shaped((8, width), F32))
    return run(resid_kernel, "resid_back", outputs, (scal, mine, got, resid, cotangent, vec), 0.8)


def mixed_kernel(cols, scal, *refs, ready):
    grads, (o_ref, rows_ref, do_ref, g_ref, all_ref, own_ref) = refs[0:4], refs[4:10]
    place_members(scal, grads, all_ref)
    do_ref[...] = dot_cols(all_ref[...], rows_ref[...]).astype(BF)
    for index in range(GROUPS):

        @pl.when(scal[0] == index)
        def _():
            own_ref[...] = all_ref[:, index * cols : (index + 1) * cols]

    ready(5)
    g_ref[...] = dot_rows(o_ref[...], own_ref[...]).astype(BF)


def mixed_back(scal, grads, mixed, w_rows):
    cols, width = w_rows.shape
    length = mixed.shape[0]
    return run(
        functools.partial(mixed_kernel, cols),
        "mixed_back",
        (shaped((length, cols), BF), shaped((width, cols), BF)),
        (scal, *grads, mixed, w_rows),
        2.5,
        [pltpu.VMEM((length, width), BF), pltpu.VMEM((length, cols), BF)],
        lazy=(5, 6),
        late=(5,),
    )


def attend_back_kernel(
    per, scal, ranges, q_ref, k_ref, v_ref, do_ref, seg_row_ref, seg_col_ref, *refs, ready
):
    out_ref, k_acc, v_acc = refs[-3:]
    cols = q_ref.shape[1]
    block = 256
    length = k_ref.shape[0]
    k_acc[...] = jnp.zeros_like(k_acc)
    v_acc[...] = jnp.zeros_like(v_acc)
    for position in (2, 3, 4, 7):
        ready(position)

    def step(i, carry):
        start = pl.multiple_of(i * block, block)
        rows = pl.ds(start, block)

        def body(key_start, size):
            window = pl.ds(key_start, size)
            keys, values = k_ref[window, :], v_ref[window, :]
            same = seg_col_ref[window, :] == seg_row_ref[:, rows]
            queries = q_ref[rows, :] * jnp.asarray(HEAD_DIM**-0.5, BF)
            grads = do_ref[rows, :]

            def one(head, carry):
                grad_query, grad_key, grad_value = carry
                lanes = head_lanes(head, queries.shape)
                query = jnp.where(lanes, queries, jnp.zeros_like(queries))
                grad = jnp.where(lanes, grads, jnp.zeros_like(grads))
                score = jnp.where(same, dot_cols(keys, query), masked_score)
                largest = jnp.max(score, axis=0, keepdims=True)
                power = jnp.exp(score - largest)
                total = jnp.sum(power, axis=0, keepdims=True)
                chance = power * (1.0 / total)
                grad_chance = dot_cols(values, grad)
                inner = jnp.sum(chance * grad_chance, axis=0, keepdims=True)
                grad_score = (chance * (grad_chance - inner)).astype(BF)
                return (
                    jnp.where(lanes, dot_rows(grad_score, keys), grad_query),
                    grad_key + dot(grad_score, query),
                    grad_value + dot(chance.astype(BF), grad),
                )

            zeros = jnp.zeros(keys.shape, F32)
            grad_query, grad_key, grad_value = each_head(
                per, size, one, (jnp.zeros(queries.shape, F32), zeros, zeros)
            )
            k_acc[window, :] += grad_key
            v_acc[window, :] += grad_value
            out_ref[rows, :cols] = (grad_query * HEAD_DIM**-0.5).astype(BF)

        each_window(ranges, i, length, body)
        return carry

    lax.fori_loop(0, q_ref.shape[0] // block, step, 0)
    out_ref[:, cols : 2 * cols] = k_acc[...].astype(BF)
    out_ref[:, 2 * cols :] = v_acc[...].astype(BF)


def attend_back(scal, ranges, queries, keys, values, grad_out, seg_row, seg_col, per, kept):
    length, cols = queries.shape
    wide = pltpu.VMEM(queries.shape, F32)
    inputs = (scal, ranges, queries, keys, values, grad_out, seg_row, seg_col, *kept)
    return run(
        functools.partial(attend_back_kernel, per),
        "attend_back",
        shaped((length, 3 * cols), BF),
        inputs,
        16.0,
        [wide, wide],
        lazy=(2, 3, 4, 7),
        late=(2, 3, 4, 7),
        save=range(8, len(inputs)),
        scalars=2,
    )


def table_kernel(scal, forward_ref, resid_ref, table_ref, rows_ref):
    rows_ref[...] = jnp.zeros_like(rows_ref)
    rows_ref[4:5, :] = resid_ref[0:1, :]
    rows_ref[5:7, :] = forward_ref[0:2, :]
    rows_ref[7:8, :] = resid_ref[1:2, :]
    rows_ref[pl.ds(8 + scal[0], 1), :] = forward_ref[2:3, :]
    rest = rows_ref[...]
    unit = unit_rows(16, 128)
    table = jnp.zeros(table_ref.shape, F32)
    for _ in range(3):
        high = rest.astype(BF)
        rest = rest - high.astype(F32)
        table += dot_rows(high, unit)
    table_ref[...] = table


def vector_table(scal, sums_forward, sums_resid):
    width = sums_resid.shape[1]
    return run(
        table_kernel,
        "vector_table",
        shaped((width, 128), F32),
        (scal, sums_forward, sums_resid),
        1.0,
        [pltpu.VMEM((16, width), F32)],
        mebibytes=8,
        lazy=(1,),
    )


def query_grads_kernel(cols, scal, *refs, ready):
    a_ref, hat_ref, out_ref, grad_ref, w_ref, table_ref, g_ref = refs
    width = a_ref.shape[1]
    block = 256
    ready(1)

    def weights(i, carry):
        lanes = pl.ds(pl.multiple_of(i * block, block), block)
        g_ref[lanes, : 3 * cols] = dot_rows(a_ref[:, lanes], grad_ref[...]).astype(BF)
        return carry

    lax.fori_loop(0, width // block, weights, 0)
    row = lax.broadcasted_iota(jnp.int32, (8, 3 * cols), 0)
    rest = dot_rows(jnp.ones((a_ref.shape[0], 8), BF), grad_ref[...])
    terms = jnp.zeros((8, 3 * cols), F32)
    for term in range(3):
        high = rest.astype(BF).astype(F32)
        terms = jnp.where(row == term, high, terms)
        rest = rest - high
    terms = terms.astype(BF)
    for position in (2, 3, 5, 6):
        ready(position)
    lane = lax.broadcasted_iota(jnp.int32, (block, 128), 1)

    def vectors(i, carry):
        lanes = pl.ds(pl.multiple_of(i * block, block), block)
        weight = w_ref[lanes, :]
        product = dot_rows(hat_ref[:, lanes], grad_ref[...]) * weight.astype(F32)
        gain = jnp.sum(product, axis=1, keepdims=True)
        shift = jnp.sum(dot_cols(weight, terms), axis=1, keepdims=True)
        table = jnp.where(lane == 0, gain, table_ref[lanes, :])
        table_ref[lanes, :] = jnp.where(lane == 1, shift, table)
        return carry

    lax.fori_loop(0, width // block, vectors, 0)
    g_ref[:, 3 * cols : 4 * cols] = out_ref[...]
    own = pl.ds(pl.multiple_of(scal[0] * cols, cols), cols)
    bias = table_ref[own, :]
    near = lax.broadcasted_iota(jnp.int32, (cols, 128), 1)
    ones = jnp.ones((8, 8), BF)
    for i, column in ((0, 2), (2, 3)):
        part = dot_rows(terms[:, i * cols : (i + 1) * cols], ones)
        bias = jnp.where(near == column, part[:, 0:1], bias)
    table_ref[own, :] = bias
    total = table_ref[...]
    high = total.astype(BF)
    low = (total - high.astype(F32)).astype(BF)
    g_ref[:, 4 * cols : 4 * cols + 16] = high[:, 0:16]
    g_ref[:, 4 * cols + 16 : 4 * cols + 32] = low[:, 0:16]
    g_ref[:, 4 * cols + 32 :] = jnp.zeros((width, 96), BF)


def query_grads(scal, normed, hat, grad_out, grad, weights, table):
    width, cols = grad_out.shape
    return run(
        functools.partial(query_grads_kernel, cols),
        "query_grads",
        shaped((width, 4 * cols + 128), BF),
        (scal, normed, hat, grad_out, grad, weights, table),
        4.0,
        lazy=(1, 2, 3, 5, 6),
        late=(1, 2, 3, 5, 6),
        far=(0,),
    )


def project_back_kernel(scal, grad_ref, w_ref, keep_ref, send_ref):
    block = grad_ref.shape[0] // GROUPS

    def step(i, carry):
        rows = pl.ds(pl.multiple_of(i * block, block), block)
        split_store(scal[0], i, dot_cols(grad_ref[rows, :], w_ref[...]), keep_ref, send_ref)
        return carry

    lax.fori_loop(0, GROUPS, step, 0)


def project_back(scal, grad, weights):
    rows, width = grad.shape[0] // 2, weights.shape[0]
    return run(
        project_back_kernel,
        "project_back",
        (shaped((rows, width), F32), shaped((rows, width), BF)),
        (scal, grad, weights),
        3.0,
        lazy=(2,),
    )


def input_kernel(scal, mine_ref, got_ref, x_ref, dh_ref, vec_ref, out_ref):
    grad = mine_ref[...] + got_ref[...].astype(F32)
    hat, inverse = normalize(x_ref[...].astype(F32))
    out_ref[...] = dh_ref[...] + norm_back(hat, inverse, vec_ref[0:1, :], grad)


def input_back(scal, mine, got, tokens, grad_resid, vec):
    inputs = (scal, mine, got, tokens, grad_resid, vec)
    return run(input_kernel, "input_back", shaped(mine.shape, F32), inputs, 1.0, lazy=(2, 3, 4, 5))


def output_kernel(scal, mine_ref, got_ref, h_ref, vec_ref, out_ref):
    branch = mine_ref[...] + got_ref[...].astype(F32) + vec_ref[7:8, :]
    out_ref[...] = (h_ref[...] + branch).astype(BF)


def output_sum(scal, mine, got, resid, vec):
    inputs = (scal, mine, got, resid, vec)
    return run(output_kernel, "output_sum", shaped(mine.shape, BF), inputs, 0.8, lazy=(2, 3, 4))


def owned_kernel(scal, in_ref, low_ref):
    total = in_ref[0].astype(F32)
    for i in range(1, in_ref.shape[0]):
        total += in_ref[i].astype(F32)
    low_ref[...] = total.astype(BF)


def owned_sum(scal, pieces):
    outputs = shaped(pieces.shape[1:], BF)
    return run(owned_kernel, "owned_sum", outputs, (scal, pieces), 1.5, lazy=(1,))


def squares_kernel(scal, *refs):
    sums = []
    for piece in refs[:4]:
        wide = piece[...].astype(F32)
        sums.append(jnp.sum(wide * wide))
    total = (sums[0] + sums[1]) + (sums[2] + sums[3])
    refs[4][...] = jnp.full(refs[4].shape, total, F32)


def squares_of(scal, pieces):
    outputs = shaped((8, 128), F32)
    return run(squares_kernel, "squares_of", outputs, (scal, *pieces), 1.0, save=range(1, 5))


def owned_vector_kernel(cols, scal, in_ref, low_ref):
    total = in_ref[0].astype(F32)
    for i in range(1, in_ref.shape[0]):
        total += in_ref[i].astype(F32)
    low_ref[:, : 4 * cols] = total[:, : 4 * cols].astype(BF)
    vector = total[:, 4 * cols :]
    high = vector.astype(BF).astype(F32)
    lane = lax.broadcasted_iota(jnp.int32, vector.shape, 1)
    rest = pltpu.roll(vector - high, 32, 1)
    low_ref[:, 4 * cols :] = jnp.where(lane < 32, high, rest).astype(BF)


def owned_vector(scal, pieces, cols):
    _, rows, width = pieces.shape
    return run(
        functools.partial(owned_vector_kernel, cols),
        "owned_vector",
        shaped((rows, width), BF),
        (scal, pieces),
        1.5,
    )


def join_kernel(cols, count, scal, *refs):
    pieces, forward_ref = refs[0:4], refs[4]
    gradient_ref, vector_ref, squares_ref = refs[5:8]
    width = gradient_ref.shape[1] // 4
    for member in range(GROUPS):

        @pl.when(scal[0] == member)
        def _():
            for i in range(4):
                for k in range(GROUPS):
                    start = i * width + (member ^ k) * cols
                    gradient_ref[:, start : start + cols] = pieces[k][
                        :, i * cols : (i + 1) * cols
                    ].astype(F32)

    def vector_of(piece):
        return piece[:, 4 * cols :].astype(F32)

    halves = [vector_of(piece) for piece in pieces]
    table = (halves[0] + halves[1]) + (halves[2] + halves[3])
    rows = lax.broadcasted_iota(jnp.int32, (16, 128), 0)
    lanes = lax.broadcasted_iota(jnp.int32, (16, 128), 1)
    unit = jnp.where((lanes % 16 == rows) & (lanes < 64), 1.0, 0.0)
    vector = lax.dot_general(
        unit,
        table,
        (((1,), (1,)), ((), ())),
        preferred_element_type=F32,
        precision=lax.Precision.HIGHEST,
    )[:count]
    vector_ref[...] = vector
    gradient = gradient_ref[...]
    total = jnp.sum(gradient * gradient) + jnp.sum(vector * vector)
    total = forward_ref[...] + total
    for i in range(squares_ref.shape[0] // 8):
        squares_ref[8 * i : 8 * i + 8, :] = total


def join(scal, pieces, squares, width, count, cols, owners):
    rows = pieces[0].shape[0]
    return run(
        functools.partial(join_kernel, cols, count),
        "join",
        (
            shaped((rows, 4 * width), F32),
            shaped((count, rows), F32),
            shaped((8 * owners, 128), F32),
        ),
        (scal, *pieces, squares),
        1.5,
    )


def clip_factor(total_ref):
    total = total_ref[0]
    for i in range(1, total_ref.shape[0]):
        total += total_ref[i]
    norm = jnp.sqrt(total[0:1, 0:1])
    return norm, jnp.minimum(1.0, clip_limit / (norm + 1e-06))


def adam_kernel(counts, scal, total_ref, attention_ref, vector_ref, *refs):
    pieces, sources, targets, norm_ref = refs[0:4], refs[4:16], refs[16:31], refs[31]
    held, copies = refs[32:44], refs[44:47]
    loads, stores = refs[47:50], refs[50:53]
    grads, grad_loads = refs[53:57], refs[57]
    norm, factor = clip_factor(total_ref)
    norm_ref[...] = jnp.broadcast_to(norm, norm_ref.shape)
    decays = (weight_decay, weight_decay, 0.0)

    def chunk(kind, i):
        if counts[kind] == 1:
            return (slice(None), slice(None))
        size = held[4 * kind].shape[1] // counts[kind]
        return (slice(None), pl.ds(pl.multiple_of(i * size, size), size))

    def load(kind, i, state):
        place = chunk(kind, i)
        number = 4 * kind + state
        return pltpu.make_async_copy(
            sources[number].at[place], held[number].at[place], loads[kind].at[i, state]
        )

    def store(kind, i, state):
        place = chunk(kind, i)
        source = held[4 * kind + state] if state < 4 else copies[kind]
        return pltpu.make_async_copy(
            source.at[place], targets[3 * state + kind].at[place], stores[kind].at[i, state]
        )

    def every(kind, action):
        def step(i, carry):
            action(kind, i)
            return carry

        lax.fori_loop(0, counts[kind], step, 0)

    def start(kind, i):
        for state in range(4):
            load(kind, i, state).start()

    def work(kind, i):
        for state in range(4):
            load(kind, i, state).wait()
        place = chunk(kind, i)
        if kind == 0:
            gradient = attention_ref[place]
        elif kind == 2:
            gradient = vector_ref[...]
        else:
            size = held[4].shape[1] // counts[1]
            half = pl.ds(pl.multiple_of((i // GROUPS) * size, size), size)
            source = scal[0] ^ (i % GROUPS)
            gradient = grads[0][:, half]
            for k in range(1, GROUPS):
                gradient = jnp.where(source == k, grads[k][:, half], gradient)
            gradient = gradient.astype(F32)
        results = adam_update(
            *[held[4 * kind + state][place] for state in range(4)], gradient, factor, decays[kind]
        )
        for state, value in zip((0, 1, 2, 3), results):
            held[4 * kind + state][place] = value
        copies[kind][place] = results[0].astype(BF)
        for state in range(5):
            store(kind, i, state).start()

    def finish(kind, i):
        for state in range(5):
            store(kind, i, state).wait()

    moves = [
        pltpu.make_async_copy(piece, grad, grad_loads.at[i])
        for i, (piece, grad) in enumerate(zip(pieces, grads))
    ]
    for move in moves:
        move.start()
    for kind in (1, 0, 2):
        every(kind, start)
    for move in moves:
        move.wait()
    for kind in (1, 0, 2):
        every(kind, work)
    for kind in (1, 0, 2):
        every(kind, finish)


def adam(scal, totals, attention_grad, vector_grad, forward_grads_by_member, states):
    counts = (4, 2 * GROUPS, 1)
    kinds = [states[4 * kind].shape for kind in range(3)]
    out_shape = [pltpu.HBM(shape, F32) for _ in range(4) for shape in kinds]
    out_shape += [pltpu.HBM(shape, BF) for shape in kinds]
    out_shape += [shaped((8, 128), F32)]
    return pl.pallas_call(
        functools.partial(adam_kernel, counts),
        out_shape=out_shape,
        in_specs=[smem()] + [vmem()] * 3 + [far_space()] * 16,
        out_specs=[far_space()] * 15 + [vmem()],
        scratch_shapes=[pltpu.VMEM(kinds[kind], F32) for kind in range(3) for _ in range(4)]
        + [pltpu.VMEM(shape, BF) for shape in kinds]
        + [pltpu.SemaphoreType.DMA((count, 4)) for count in counts]
        + [pltpu.SemaphoreType.DMA((count, 5)) for count in counts]
        + [pltpu.VMEM(item.shape, item.dtype) for item in forward_grads_by_member]
        + [pltpu.SemaphoreType.DMA((GROUPS,))],
        compiler_params=params(32),
        cost_estimate=cost(9.0),
        name="adam",
    )(scal, totals, attention_grad, vector_grad, *map(pin, forward_grads_by_member), *map(pin, states))


def adam_update(master, moment, second, teacher, gradient, factor, decay_rate):
    clipped = gradient * factor
    moment_new = beta_one * moment + (1.0 - beta_one) * clipped
    second_new = beta_two * second + (1.0 - beta_two) * clipped * clipped
    scale_one = 1.0 - beta_one**ADAM_STEP
    scale_two = 1.0 - beta_two**ADAM_STEP
    update = (moment_new * (1.0 / scale_one)) / (
        jnp.sqrt(second_new * (1.0 / scale_two)) + adam_epsilon
    )
    master_new = master * (1.0 - learn_rate * decay_rate) - learn_rate * update
    teacher_new = teacher_keep * teacher + (1.0 - teacher_keep) * master_new
    return (master_new, moment_new, second_new, teacher_new)


def swap(part, bit):
    return lax.ppermute(part, "head", [(i, i ^ bit) for i in range(4)])


def spread(part, *others):
    across = swap(part, 2)
    if others:
        return [
            part,
            swap(after(part, *others), 1),
            across,
            swap(after(across, *others), 1),
        ]
    return [part, swap(part, 1), across, swap(across, 1)]


RING = (0, 2, 4, 6, 7, 5, 3, 1)


def ring_owners(count):
    if count != len(RING):
        return np.zeros((count, 1), np.int32)
    table = []
    for device in range(count):
        place = RING.index(device)
        owners = [device]
        for hop in range(1, count // 2 + 1):
            owners.append(RING[(place - hop) % count])
            owners.append(RING[(place + hop) % count])
        table.append(owners)
    return np.asarray(table, np.int32)


def after(value, *others):
    return lax.optimization_barrier((value, *others))[0]


class Ring:
    def __init__(self, block, count, halved=False):
        self.count = count
        self.halved = halved
        self.ringed = count == len(RING)
        self.hops = count // 2 if self.ringed else 1
        self.front = self.rear = block
        self.pieces = [block]
        self.done = 0

    def send(self, array, distance):
        count = self.count
        pairs = [(RING[i], RING[(i + distance) % count]) for i in range(count)]
        return lax.ppermute(array, "dp", pairs)

    def hop(self, *others):
        self.done += 1
        if not self.ringed:
            self.pieces = [lax.all_gather(after(self.front, *others), "dp", axis=0, tiled=True)]
            return self
        if self.done > 1 or others:
            self.front, self.rear = lax.optimization_barrier((self.front, self.rear, *others))[:2]
        if self.done == self.hops and self.halved:
            half = self.front.shape[0] // 2
            self.front, self.rear = self.front[:half], self.rear[half:]
        self.front = self.send(self.front, 1)
        self.pieces.append(self.front)
        if self.done < self.hops or self.halved:
            self.rear = self.send(self.rear, -1)
            self.pieces.append(self.rear)
        return self

    def rest(self):
        while self.done < self.hops:
            self.hop()
        return self.pieces


def exchange_owned(grads, count):
    blocks = grads.reshape(count, -1, grads.shape[1])
    return lax.all_to_all(blocks, "dp", split_axis=0, concat_axis=0)


def local(
    tokens,
    cotangent,
    segments,
    attention_master,
    feedforward_master,
    vector_master,
    attention_moment,
    feedforward_moment,
    vector_moment,
    attention_second,
    feedforward_second,
    vector_second,
    attention_teacher,
    feedforward_teacher,
    vector_teacher,
):
    width = tokens.shape[1]
    owners = lax.axis_size("dp")
    groups = lax.axis_size("head")
    hidden = feedforward_master.shape[1] // 2
    per = HEADS // groups
    cols = per * HEAD_DIM
    part = hidden // groups

    owner_table = ring_owners(owners)
    table = np.concatenate(
        [
            np.tile(np.arange(groups, dtype=np.int32), owners)[:, None],
            np.repeat(owner_table, groups, axis=0),
        ],
        axis=1,
    )
    place = lax.axis_index("dp") * groups + lax.axis_index("head")
    scal = lax.dynamic_index_in_dim(jnp.asarray(table), place, 0, keepdims=False)
    first = Ring(pack_attention(scal, attention_master, vector_master, cols), owners)
    first.rest()
    ringed = owners == len(RING)
    early = first.pieces[-3:-1] if ringed else first.pieces
    token_across, grad_across = swap(tokens, 2), swap(cotangent, 2)
    token, token_across = lax.optimization_barrier((tokens, token_across, *early))[:2]
    x_all = place_blocks(scal, [token, swap(token, 1), token_across, swap(token_across, 1)])
    second = Ring(pack_forward(scal, feedforward_master, part), owners)
    second.hop(first.pieces[-1])

    queries, keys, values, w_qkv, w_o, vec, seg_col, normed, hat, ranges = project(
        scal, segments, x_all, first.pieces, cols
    )
    half = x_all.shape[0] // 2
    w_across = swap(w_o, 2)
    mixed_low, *kept = attend(
        scal,
        ranges,
        after(queries, grad_across),
        keys,
        values,
        segments,
        seg_col,
        per,
        0,
        half,
        (w_qkv, vec, normed, hat),
    )
    far_q, far_k, far_v, far_col, far_weights, far_vec, *far_normed = kept
    low_across = swap(mixed_low, 2)
    w_across = after(w_across, mixed_low)
    if ringed:
        second.hop(mixed_low)
    mixed_high = attend(
        scal, ranges, after(queries, w_across), keys, values, segments, seg_col, per, half, half
    )
    high_across = swap(after(mixed_high, low_across), 2)
    if ringed:
        second.hop(mixed_high)
    w_across, low_across, w_o, mixed_low, grad, grad_across = lax.optimization_barrier(
        (w_across, low_across, w_o, mixed_low, cotangent, grad_across, high_across)
    )[:6]
    dy_all = place_blocks(scal, [grad, swap(grad, 1), grad_across, swap(grad_across, 1)])
    w_out = [w_o, swap(w_o, 1), w_across, swap(w_across, 1)]
    mixed = [
        (mixed_low, mixed_high),
        (swap(mixed_low, 1), swap(mixed_high, 1)),
        (low_across, high_across),
        (swap(low_across, 1), swap(high_across, 1)),
    ]
    (
        normed_two,
        active,
        grad_pre,
        keep,
        send,
        resid,
        w_ff,
        w_rows,
        sums_forward,
        mixed_all,
    ) = forward_back(scal, x_all, dy_all, mixed, w_out, second.rest(), vec, cols)
    grad_ff, far_active, *kept = forward_grads(
        scal,
        normed_two,
        active,
        grad_pre,
        dy_all,
        (resid, sums_forward, w_rows, w_ff, mixed_all),
    )
    far_resid, far_sums, far_rows, far_ff, far_mixed = kept
    got = swap(send, 1)
    grad_ff, got = lax.optimization_barrier((grad_ff, got))
    owned_ff = exchange_owned(grad_ff, owners)
    mine, send = merge(scal, keep, got)
    keep_branch, send_branch, cot_own = branch_part(
        scal, far_active, after(far_ff, send), cotangent
    )
    got = swap(send, 2)
    grad_resid, grad_low, sums_resid = resid_back(
        scal, after(mine, send_branch), got, resid, cot_own, vec
    )
    low_across = swap(grad_low, 2)
    mine, send = merge(
        scal, keep_branch, swap(after(send_branch, grad_low), 1), lazy=(1,)
    )
    table = vector_table(scal, far_sums, sums_resid)
    low_across = after(low_across, send, table)
    low_blocks = [grad_low, swap(grad_low, 1), low_across, swap(low_across, 1)]
    grad_mixed, grad_out = mixed_back(scal, low_blocks, far_mixed, far_rows)
    grad_qkv, far_dh, far_table, far_grad_out = attend_back(
        scal,
        ranges,
        far_q,
        far_k,
        far_v,
        grad_mixed,
        segments,
        far_col,
        per,
        (grad_resid, table, grad_out),
    )
    got_branch = swap(after(send, grad_mixed), 2)
    pack = query_grads(
        scal,
        after(far_normed[0], got_branch),
        far_normed[1],
        far_grad_out,
        grad_qkv,
        far_weights,
        far_table,
    )
    owned_pack = exchange_owned(pack, owners)
    forward_parts = spread(owned_sum(scal, after(owned_ff, pack)))
    forward_squares, *forward_parts = squares_of(scal, forward_parts)
    keep, send = project_back(scal, grad_qkv, after(far_weights, pack))
    mine_input, send = merge(scal, keep, swap(send, 1))
    block_output = output_sum(scal, after(mine, pack), got_branch, far_resid, far_vec)
    got_input = swap(send, 2)
    owned_pack = after(owned_pack, block_output, forward_squares, got_input)
    input_gradient = input_back(scal, mine_input, got_input, tokens, far_dh, far_vec)
    attention_parts = spread(owned_vector(scal, owned_pack, cols))
    attention_grad, vector_grad, squares = join(
        scal, attention_parts, forward_squares, width, vector_master.shape[0], cols, owners
    )
    totals = lax.all_to_all(
        squares.reshape(owners, 8, 128), "dp", split_axis=0, concat_axis=0
    )
    *results, norm = adam(
        scal,
        totals,
        attention_grad,
        vector_grad,
        forward_parts,
        (
            attention_master,
            attention_moment,
            attention_second,
            attention_teacher,
            feedforward_master,
            feedforward_moment,
            feedforward_second,
            feedforward_teacher,
            vector_master,
            vector_moment,
            vector_second,
            vector_teacher,
        ),
    )
    return (block_output, input_gradient, norm[0, 0], *results)


def solution(mesh):
    rows = P(("dp", "head"), None)
    shard = P("dp", None)
    vector = P(None, "dp")
    return jax.shard_map(
        local,
        mesh=mesh,
        in_specs=(rows, rows, shard) + (shard, shard, vector) * 4,
        out_specs=(rows, rows, P()) + (shard, shard, vector) * 5,
        check_vma=False,
    )
```

```python
import functools

import jax
import jax.numpy as jnp
import numpy as np
from jax import lax
from jax.experimental import pallas as pl
from jax.experimental.pallas import tpu as pltpu
from jax.sharding import PartitionSpec as P

HEADS = 12
HEAD_DIM = 64
ADAM_STEP = 3

norm_epsilon = 1e-06
beta_one = 0.5
beta_two = 0.5
adam_epsilon = 1e-08
learn_rate = 0.05
weight_decay = 0.05
teacher_keep = 0.8
clip_limit = 1.0
masked_score = -1e30

BF = jnp.bfloat16
F32 = jnp.float32


def dot_rows(left, right):
    return lax.dot_general(left, right, (((0,), (0,)), ((), ())), preferred_element_type=F32)


def dot_cols(left, right):
    return lax.dot_general(left, right, (((1,), (1,)), ((), ())), preferred_element_type=F32)


def dot(left, right):
    return jnp.dot(left, right, preferred_element_type=F32)


def normalize(values):
    center = jnp.mean(values, axis=-1, keepdims=True)
    deviate = values - center
    spread = jnp.mean(deviate * deviate, axis=-1, keepdims=True)
    inverse = lax.rsqrt(spread + norm_epsilon)
    return deviate * inverse, inverse


def norm_back(hat, inverse, gain, grad):
    scaled = grad * gain
    mean_one = jnp.mean(scaled, axis=-1, keepdims=True)
    mean_two = jnp.mean(scaled * hat, axis=-1, keepdims=True)
    return inverse * (scaled - mean_one - hat * mean_two)


def head_lanes(index, shape):
    lane = lax.broadcasted_iota(jnp.int32, shape, 1)
    return (lane >= index * HEAD_DIM) & (lane < (index + 1) * HEAD_DIM)


def unit_rows(rows, columns):
    row = lax.broadcasted_iota(jnp.int32, (rows, columns), 0)
    column = lax.broadcasted_iota(jnp.int32, (rows, columns), 1)
    return jnp.where(row == column, 1.0, 0.0).astype(BF)


def smem():
    return pl.BlockSpec(memory_space=pltpu.SMEM)


def vmem():
    return pl.BlockSpec(memory_space=pltpu.VMEM)


def whole(*shape):
    return pl.BlockSpec(shape, lambda *index: (0,) * len(shape))


def shaped(shape, kind):
    return jax.ShapeDtypeStruct(shape, kind)


def params(mebibytes):
    return pltpu.CompilerParams(vmem_limit_bytes=mebibytes * 2**20)


COST_SCALE = 1.0


def cost(microseconds):
    return pl.CostEstimate(
        flops=0, transcendentals=0, bytes_accessed=int(microseconds * COST_SCALE * 3.6e6)
    )


def pin(array):
    return pltpu.with_memory_space_constraint(array, pltpu.HBM)


def far_space():
    return pl.BlockSpec(memory_space=pltpu.HBM)


def run(
    kernel,
    name,
    outputs,
    inputs,
    microseconds,
    scratch=(),
    mebibytes=16,
    lazy=(),
    save=(),
    far=(),
    late=(),
    scalars=1,
    scalar_outputs=(),
):
    single = not isinstance(outputs, tuple)
    outputs = [outputs] if single else list(outputs)
    lazy, save, far = list(lazy), list(save), list(far)
    count, produced, own = len(inputs), len(outputs), len(scratch)
    buffers = [pltpu.VMEM(inputs[i].shape, inputs[i].dtype) for i in lazy]
    buffers += [pltpu.VMEM(outputs[i].shape, outputs[i].dtype) for i in far]
    moves = len(lazy) + len(save) + len(far)
    if moves:
        buffers.append(pltpu.SemaphoreType.DMA((moves,)))

    def body(*refs):
        items = list(refs[: count + produced])
        saved = refs[count + produced : count + produced + len(save)]
        rest = refs[count + produced + len(save) :]
        inner, extra = rest[:own], rest[own:]
        copies, number = [], 0
        for j, i in enumerate(lazy):
            copies.append(pltpu.make_async_copy(refs[i], extra[j], extra[-1].at[number]))
            items[i] = extra[j]
            number += 1
        stores = []
        for j, i in enumerate(save):
            stores.append(pltpu.make_async_copy(refs[i], saved[j], extra[-1].at[number]))
            number += 1
        last = []
        for j, i in enumerate(far):
            buffer = extra[len(lazy) + j]
            last.append(pltpu.make_async_copy(buffer, refs[count + i], extra[-1].at[number]))
            items[count + i] = buffer
            number += 1
        for copy in copies + stores:
            copy.start()
        for i, copy in zip(lazy, copies):
            if i not in late:
                copy.wait()
        if late:
            kernel(*items, *inner, ready=lambda i: copies[lazy.index(i)].wait())
        else:
            kernel(*items, *inner)
        for copy in last:
            copy.start()
        for copy in stores + last:
            copy.wait()

    shapes = [pltpu.HBM(item.shape, item.dtype) if i in far else item for i, item in enumerate(outputs)]
    results = pl.pallas_call(
        body,
        out_shape=shapes + [pltpu.HBM(inputs[i].shape, inputs[i].dtype) for i in save],
        in_specs=[smem()] * scalars
        + [far_space() if i in lazy else vmem() for i in range(scalars, count)],
        out_specs=[
            far_space() if i in far else smem() if i in scalar_outputs else vmem()
            for i in range(produced)
        ]
        + [far_space()] * len(save),
        scratch_shapes=list(scratch) + buffers,
        compiler_params=params(mebibytes),
        cost_estimate=cost(microseconds),
        name=name,
    )(*[pin(item) if i in lazy else item for i, item in enumerate(inputs)])
    return results[0] if single and not save else tuple(results)


GROUPS = 4


def pack_kernel(cols, scal, *refs):
    vector_ref, out_ref = refs[4:6]
    for side in range(2):

        @pl.when(scal[0] % 2 == side)
        def _():
            for i in range(4):
                out_ref[:, i * cols : (i + 1) * cols] = refs[i][
                    :, side * cols : (side + 1) * cols
                ].astype(BF)

    vector = vector_ref[...].astype(BF)
    out_ref[:, 4 * cols :] = dot_rows(vector, unit_rows(vector.shape[0], 128)).astype(BF)


def pack_attention(scal, attention, vector, cols):
    rows = attention.shape[0]

    def pair(i):
        return pl.BlockSpec((rows, 2 * cols), lambda step, scal: (0, 2 * i + scal[0] // 2))

    return pl.pallas_call(
        functools.partial(pack_kernel, cols),
        out_shape=shaped((rows, 4 * cols + 128), BF),
        grid_spec=pltpu.PrefetchScalarGridSpec(
            num_scalar_prefetch=1,
            grid=(1,),
            in_specs=[pair(i) for i in range(4)] + [whole(*vector.shape)],
            out_specs=whole(rows, 4 * cols + 128),
        ),
        compiler_params=params(8),
        cost_estimate=cost(1.5),
        name="pack_attention",
    )(scal, *[pin(attention)] * 4, pin(vector))


def cast_kernel(scal, in_ref, out_ref):
    out_ref[...] = in_ref[...].astype(BF)


def pack_forward(scal, forward, part):
    rows = forward.shape[0]
    return pl.pallas_call(
        cast_kernel,
        out_shape=shaped((rows, 2 * part), BF),
        grid_spec=pltpu.PrefetchScalarGridSpec(
            num_scalar_prefetch=1,
            grid=(2,),
            in_specs=[pl.BlockSpec((rows, part), lambda i, scal: (0, GROUPS * i + scal[0]))],
            out_specs=pl.BlockSpec((rows, part), lambda i, scal: (0, i)),
        ),
        compiler_params=params(8),
        cost_estimate=cost(1.5),
        name="pack_forward",
    )(scal, forward)


def place_rows(scal, pieces, target):
    rows = pieces[0].shape[0]
    if len(pieces) == 1:
        target[...] = pieces[0][...]
        return
    for i, piece in enumerate(pieces):
        size = piece.shape[0]
        first = rows - size if i == len(RING) else 0
        start = pl.multiple_of(scal[1 + i] * rows + first, size)
        target[pl.ds(start, size), :] = piece[...]


def place_members(scal, pieces, target):
    rows = pieces[0].shape[0]
    for i, piece in enumerate(pieces):
        start = pl.multiple_of((scal[0] ^ i) * rows, rows)
        target[pl.ds(start, rows), :] = piece[...]


def place_kernel(scal, *refs):
    place_members(scal, refs[0:4], refs[4])


def place_blocks(scal, blocks):
    rows, width = blocks[0].shape
    wide = shaped((GROUPS * rows, width), BF)
    return run(place_kernel, "place_blocks", wide, (scal, *blocks), 0.5, mebibytes=2)


def fold(value):
    rows, columns = value.shape
    count = 128 // (columns - 128)
    share = rows // count
    rest = [value[i * share : (i + 1) * share, 128:] for i in range(count)]
    return value[:, :128], jnp.concatenate(rest, axis=1)


def folded_rows(rows, columns):
    return rows + rows * (columns - 128) // 128


def project_kernel(count, cols, scal, seg_ref, x_ref, *refs):
    pieces = refs[:count]
    q_ref, k_ref, v_ref, w_ref, wo_ref, vec_ref, col_ref, a_ref, hat_ref, ranges_ref = refs[
        count : 10 + count
    ]
    weights, wq_ref, wk_ref, wv_ref = refs[10 + count : 14 + count]
    key_ranges(seg_ref[...], ranges_ref)
    place_rows(scal, pieces, weights)
    for i, ref in enumerate((wq_ref, wk_ref, wv_ref)):
        ref[...] = weights[:, i * cols : (i + 1) * cols]
    w_ref[...] = weights[:, : 3 * cols]
    top, rest = fold(weights[:, 3 * cols : 4 * cols])
    wo_ref[: top.shape[0], :] = top
    wo_ref[top.shape[0] :, :] = rest
    unit = unit_rows(16, 128)
    vec_ref[...] = dot_cols(unit, weights[:, 4 * cols :])
    start = pl.multiple_of(scal[0] * cols, cols)
    own = dot_cols(unit, weights[pl.ds(start, cols), 4 * cols :])
    query_bias, value_bias = own[2:3, :], own[3:4, :]
    gain, shift = vec_ref[0:1, :], vec_ref[1:2, :]
    numbers = jnp.broadcast_to(seg_ref[...].astype(F32), (8, seg_ref.shape[1])).astype(BF)
    col_ref[...] = dot_rows(numbers, unit_rows(8, 128))[:, 0:1].astype(jnp.int32)
    block = 256

    def step(i, carry):
        rows = pl.ds(pl.multiple_of(i * block, block), block)
        hat, _ = normalize(x_ref[rows, :].astype(F32))
        normed = (hat * gain + shift).astype(BF)
        a_ref[rows, :] = normed
        hat_ref[rows, :] = hat.astype(BF)
        q_ref[rows, :] = (dot(normed, wq_ref[...]) + query_bias).astype(BF)
        k_ref[rows, :] = dot(normed, wk_ref[...]).astype(BF)
        v_ref[rows, :] = (dot(normed, wv_ref[...]) + value_bias).astype(BF)
        return carry

    lax.fori_loop(0, x_ref.shape[0] // block, step, 0)


def project(scal, segments, x_all, pieces, cols):
    length, width = x_all.shape
    outputs = (
        (shaped((length, cols), BF),) * 3
        + (shaped((width, 3 * cols), BF),)
        + (shaped((folded_rows(width, cols), 128), BF),)
        + (shaped((16, width), F32), shaped((length, 1), jnp.int32))
        + (shaped((length, width), BF),) * 2
        + (shaped((16,), jnp.int32),)
    )
    return run(
        functools.partial(project_kernel, len(pieces), cols),
        "project",
        outputs,
        (scal, segments, x_all, *pieces),
        4.5,
        scalar_outputs=(9,),
        scratch=[pltpu.VMEM((width, 4 * cols + 128), BF)] + [pltpu.VMEM((width, cols), BF)] * 3,
    )


QUERIES = 256
WINDOWS = (512, 576)


def key_ranges(numbers, ranges_ref):
    length = numbers.shape[1]
    images = jnp.where(numbers < 0, length, numbers)
    place = lax.broadcasted_iota(jnp.int32, numbers.shape, 1)
    for block in range(length // QUERIES):
        first = jnp.max(jnp.where(place == block * QUERIES, images, 0))
        last = jnp.max(jnp.where(place == (block + 1) * QUERIES - 1, images, 0))
        ranges_ref[2 * block] = jnp.sum((images < first).astype(jnp.int32))
        ranges_ref[2 * block + 1] = jnp.sum((images <= last).astype(jnp.int32))


def each_window(ranges, block, length, body):
    low, high = ranges[2 * block], ranges[2 * block + 1]
    taken = jnp.bool_(False)
    for size in [size for size in WINDOWS if size < length] + [length]:
        start = (jnp.minimum(low, length - size) // 16) * 16
        fits = high - start <= size

        @pl.when(fits & jnp.logical_not(taken))
        def _():
            body(pl.multiple_of(start, 16), size)

        taken = taken | fits


def each_head(per, size, body, carry):
    if size > WINDOWS[0]:
        return lax.fori_loop(0, per, body, carry)
    for head in range(per):
        carry = body(head, carry)
    return carry


def attend_kernel(per, first, scal, ranges, q_ref, k_ref, v_ref, seg_row_ref, seg_col_ref, *refs):
    out_ref, held = refs[-2:]
    block = QUERIES
    length = k_ref.shape[0]

    def step(i, carry):
        start = pl.multiple_of(first + i * block, block)
        near = pl.ds(pl.multiple_of(i * block, block), block)

        def body(key_start, size):
            window = pl.ds(key_start, size)
            keys, values = k_ref[window, :], v_ref[window, :]
            numbers = seg_row_ref[...]
            if size < length:
                span = size - size % 128 + 256
                base = jnp.minimum(key_start // 128, (length - span) // 128) * 128
                numbers = seg_row_ref[:, pl.ds(pl.multiple_of(base, 128), span)]
                numbers = jnp.broadcast_to(numbers, (8, span))
                numbers = pltpu.roll(numbers, span - (key_start - base), 1)[0:1, :size]
            same = seg_col_ref[pl.ds(start, block), :] == numbers
            queries = q_ref[pl.ds(start, block), :] * jnp.asarray(HEAD_DIM**-0.5, BF)

            def one(head, result):
                lanes = head_lanes(head, queries.shape)
                score = dot_cols(jnp.where(lanes, queries, jnp.zeros_like(queries)), keys)
                score = jnp.where(same, score, masked_score)
                largest = jnp.max(score, axis=1, keepdims=True)
                power = jnp.exp(score - largest)
                total = jnp.sum(power, axis=1, keepdims=True)
                chance = (power * (1.0 / total)).astype(BF)
                return jnp.where(lanes, dot(chance, values), result)

            result = each_head(per, size, one, jnp.zeros(queries.shape, F32))
            held[near, :] = result.astype(BF)

        each_window(ranges, first // block + i, length, body)
        return carry

    lax.fori_loop(0, held.shape[0] // block, step, 0)
    top, rest = fold(held[...])
    out_ref[: top.shape[0], :] = top
    out_ref[top.shape[0] :, :] = rest


def attend(scal, ranges, queries, keys, values, seg_row, seg_col, per, first, count, kept=()):
    inputs = (scal, ranges, queries, keys, values, seg_row, seg_col, *kept)
    return run(
        functools.partial(attend_kernel, per, first),
        "attend",
        shaped((folded_rows(count, queries.shape[1]), 128), BF),
        inputs,
        7.0 * count / queries.shape[0],
        [pltpu.VMEM((count, queries.shape[1]), BF)],
        save=(2, 3, 4, 6, *range(7, len(inputs))) if kept else (),
        scalars=2,
    )


def forward_kernel(count, cols, parts, scal, x_ref, dy_ref, *refs):
    mixed, w_out = [refs[k * parts : (k + 1) * parts] for k in range(4)], refs[4 * parts :][:4]
    refs = refs[4 * parts + 4 :]
    pieces = refs[:count]
    vec_ref = refs[count]
    c_ref, u_ref, df_ref, keep_ref, send_ref, h_ref, w_ref, rows_ref, sums_ref, o_ref = refs[
        1 + count : 11 + count
    ]
    out_weight = refs[11 + count]
    member = scal[0]
    length, width = x_ref.shape
    part = w_ref.shape[1] // 2
    block = length // GROUPS
    narrow = cols - 128
    place_rows(scal, pieces, w_ref)

    def unfold(target, first, column, item):
        rows = item.shape[0] * 128 // cols
        share = rows * narrow // 128
        target[first : first + rows, column : column + 128] = item[:rows, :]
        for i in range(rows // share):
            start = first + i * share
            target[start : start + share, column + 128 : column + cols] = item[
                rows:, i * narrow : (i + 1) * narrow
            ]

    for index in range(GROUPS):

        @pl.when(member == index)
        def _():
            for k in range(GROUPS):
                column = (index ^ k) * cols
                unfold(out_weight, 0, column, w_out[k])
                for half in range(parts):
                    unfold(o_ref, half * (length // parts), column, mixed[k][half])

    rows_ref[...] = out_weight[pl.ds(pl.multiple_of(member * cols, cols), cols), :]
    zero = jnp.zeros((1, width), F32)
    up_bias = vec_ref[pl.ds(8 + member, 1), :]

    def run_block(step, carry):
        rows = pl.ds(pl.multiple_of(step * block, block), block)
        resid = x_ref[rows, :].astype(F32) + vec_ref[4:5, :] + dot(o_ref[rows, :], out_weight[...])

        @pl.when(step == member)
        def _():
            h_ref[...] = resid

        hat, _ = normalize(resid)
        normed = (hat * vec_ref[5:6, :] + vec_ref[6:7, :]).astype(BF)
        c_ref[rows, :] = normed
        pre = dot(normed, w_ref[:, :part]) + up_bias
        phi = 0.5 * (1.0 + lax.erf(pre * 0.7071067811865476))
        u_ref[rows, :] = (pre * phi).astype(BF)
        slope = phi + pre * (jnp.exp(-0.5 * pre * pre) * 0.3989422804014327)
        grad_pre = (dot(dy_ref[rows, :], w_ref[:, part:]) * slope).astype(BF)
        df_ref[rows, :] = grad_pre
        grad_normed = dot_cols(grad_pre, w_ref[:, :part])
        split_store(member, step, grad_normed, keep_ref, send_ref)
        return (
            carry[0] + jnp.sum(grad_normed * hat, axis=0, keepdims=True),
            carry[1] + jnp.sum(grad_normed, axis=0, keepdims=True),
            carry[2] + jnp.sum(grad_pre.astype(F32), axis=0, keepdims=True),
        )

    carry = lax.fori_loop(0, GROUPS, run_block, (zero, zero, zero))
    sums_ref[...] = jnp.zeros_like(sums_ref)
    for i in range(3):
        sums_ref[i : i + 1, :] = carry[i]


def split_store(member, index, value, keep_ref, send_ref):
    mine = (index % 2) == (member % 2)
    rows = value.shape[0]
    place = pl.ds(pl.multiple_of((index // 2) * rows, rows), rows)

    @pl.when(mine)
    def _():
        keep_ref[place, :] = value

    @pl.when(jnp.logical_not(mine))
    def _():
        send_ref[place, :] = value.astype(BF)


def forward_back(scal, x_all, dy_all, mixed, w_out, pieces, vec, cols):
    length, width = x_all.shape
    part = pieces[0].shape[1] // 2
    rows = length // GROUPS
    outputs = (
        shaped((length, width), BF),
        shaped((length, part), BF),
        shaped((length, part), BF),
        shaped((2 * rows, width), F32),
        shaped((2 * rows, width), BF),
        shaped((rows, width), F32),
        shaped((width, 2 * part), BF),
        shaped((cols, width), BF),
        shaped((8, width), F32),
        shaped((length, width), BF),
    )
    flat = [item for items in mixed for item in items]
    return run(
        functools.partial(forward_kernel, len(pieces), cols, len(mixed[0])),
        "forward_back",
        outputs,
        (scal, x_all, dy_all, *flat, *w_out, *pieces, vec),
        13.0,
        [pltpu.VMEM((width, width), BF)],
    )


def forward_grads_kernel(scal, c_ref, u_ref, df_ref, dy_ref, *refs):
    g_ref = refs[-1]
    part = u_ref.shape[1]
    third = c_ref.shape[1] // 3

    def weight(i, carry):
        lanes = pl.ds(pl.multiple_of(i * third, third), third)
        g_ref[lanes, :part] = dot_rows(c_ref[:, lanes], df_ref[...]).astype(BF)
        g_ref[lanes, part:] = dot_rows(dy_ref[:, lanes], u_ref[...]).astype(BF)
        return carry

    lax.fori_loop(0, 3, weight, 0)


def forward_grads(scal, normed, active, grad_pre, dy_all, kept):
    width = normed.shape[1]
    part = active.shape[1]
    outputs = shaped((width, 2 * part), BF)
    inputs = (scal, normed, active, grad_pre, dy_all, *kept)
    return run(
        forward_grads_kernel,
        "forward_grads",
        outputs,
        inputs,
        4.0,
        save=(2, *range(5, len(inputs))),
    )


def branch_kernel(scal, u_ref, w_ref, dy_ref, keep_ref, send_ref, own_ref):
    own_ref[...] = dy_ref[...]
    part = u_ref.shape[1]
    block = u_ref.shape[0] // GROUPS

    def branch(i, carry):
        rows = pl.ds(pl.multiple_of(i * block, block), block)
        split_store(scal[0], i, dot_cols(u_ref[rows, :], w_ref[:, part:]), keep_ref, send_ref)
        return carry

    lax.fori_loop(0, GROUPS, branch, 0)


def branch_part(scal, active, weights, cotangent):
    rows = active.shape[0] // GROUPS
    width = weights.shape[0]
    return run(
        branch_kernel,
        "branch_part",
        (
            shaped((2 * rows, width), F32),
            shaped((2 * rows, width), BF),
            shaped(cotangent.shape, BF),
        ),
        (scal, active, weights, cotangent),
        3.0,
        lazy=(1, 2, 3),
        far=(0,),
    )


def merge_kernel(scal, keep_ref, got_ref, mine_ref, send_ref):
    rows = mine_ref.shape[0]
    mine = pl.ds(pl.multiple_of((scal[0] // 2) * rows, rows), rows)
    other = pl.ds(pl.multiple_of((1 - scal[0] // 2) * rows, rows), rows)
    mine_ref[...] = keep_ref[mine, :] + got_ref[mine, :].astype(F32)
    send_ref[...] = (keep_ref[other, :] + got_ref[other, :].astype(F32)).astype(BF)


def merge(scal, keep, got, lazy=()):
    rows, width = keep.shape
    outputs = (shaped((rows // 2, width), F32), shaped((rows // 2, width), BF))
    return run(merge_kernel, "merge", outputs, (scal, keep, got), 0.7, mebibytes=8, lazy=lazy)


def resid_kernel(scal, mine_ref, got_ref, h_ref, dy_ref, vec_ref, dh_ref, dp_ref, sums_ref):
    grad = mine_ref[...] + got_ref[...].astype(F32)
    hat, inverse = normalize(h_ref[...])
    dy = dy_ref[...].astype(F32)
    grad_resid = dy + norm_back(hat, inverse, vec_ref[5:6, :], grad)
    dh_ref[...] = grad_resid
    low = grad_resid.astype(BF)
    dp_ref[...] = low
    sums_ref[...] = jnp.zeros_like(sums_ref)
    sums_ref[0:1, :] = jnp.sum(low.astype(F32), axis=0, keepdims=True)
    sums_ref[1:2, :] = jnp.sum(dy, axis=0, keepdims=True)


def resid_back(scal, mine, got, resid, cotangent, vec):
    rows, width = mine.shape
    outputs = (shaped((rows, width), F32), shaped((rows, width), BF), shaped((8, width), F32))
    return run(resid_kernel, "resid_back", outputs, (scal, mine, got, resid, cotangent, vec), 0.8)


def mixed_kernel(cols, scal, *refs, ready):
    grads, (o_ref, rows_ref, do_ref, g_ref, all_ref, own_ref) = refs[0:4], refs[4:10]
    place_members(scal, grads, all_ref)
    do_ref[...] = dot_cols(all_ref[...], rows_ref[...]).astype(BF)
    for index in range(GROUPS):

        @pl.when(scal[0] == index)
        def _():
            own_ref[...] = all_ref[:, index * cols : (index + 1) * cols]

    ready(5)
    g_ref[...] = dot_rows(o_ref[...], own_ref[...]).astype(BF)


def mixed_back(scal, grads, mixed, w_rows):
    cols, width = w_rows.shape
    length = mixed.shape[0]
    return run(
        functools.partial(mixed_kernel, cols),
        "mixed_back",
        (shaped((length, cols), BF), shaped((width, cols), BF)),
        (scal, *grads, mixed, w_rows),
        2.5,
        [pltpu.VMEM((length, width), BF), pltpu.VMEM((length, cols), BF)],
        lazy=(5, 6),
        late=(5,),
    )


def attend_back_kernel(
    per, scal, ranges, q_ref, k_ref, v_ref, do_ref, seg_row_ref, seg_col_ref, *refs, ready
):
    out_ref, k_acc, v_acc = refs[-3:]
    cols = q_ref.shape[1]
    block = 256
    length = k_ref.shape[0]
    k_acc[...] = jnp.zeros_like(k_acc)
    v_acc[...] = jnp.zeros_like(v_acc)
    for position in (2, 3, 4, 7):
        ready(position)

    def step(i, carry):
        start = pl.multiple_of(i * block, block)
        rows = pl.ds(start, block)

        def body(key_start, size):
            window = pl.ds(key_start, size)
            keys, values = k_ref[window, :], v_ref[window, :]
            same = seg_col_ref[window, :] == seg_row_ref[:, rows]
            queries = q_ref[rows, :] * jnp.asarray(HEAD_DIM**-0.5, BF)
            grads = do_ref[rows, :]

            def one(head, carry):
                grad_query, grad_key, grad_value = carry
                lanes = head_lanes(head, queries.shape)
                query = jnp.where(lanes, queries, jnp.zeros_like(queries))
                grad = jnp.where(lanes, grads, jnp.zeros_like(grads))
                score = jnp.where(same, dot_cols(keys, query), masked_score)
                largest = jnp.max(score, axis=0, keepdims=True)
                power = jnp.exp(score - largest)
                total = jnp.sum(power, axis=0, keepdims=True)
                chance = power * (1.0 / total)
                grad_chance = dot_cols(values, grad)
                inner = jnp.sum(chance * grad_chance, axis=0, keepdims=True)
                grad_score = (chance * (grad_chance - inner)).astype(BF)
                return (
                    jnp.where(lanes, dot_rows(grad_score, keys), grad_query),
                    grad_key + dot(grad_score, query),
                    grad_value + dot(chance.astype(BF), grad),
                )

            zeros = jnp.zeros(keys.shape, F32)
            grad_query, grad_key, grad_value = each_head(
                per, size, one, (jnp.zeros(queries.shape, F32), zeros, zeros)
            )
            k_acc[window, :] += grad_key
            v_acc[window, :] += grad_value
            out_ref[rows, :cols] = (grad_query * HEAD_DIM**-0.5).astype(BF)

        each_window(ranges, i, length, body)
        return carry

    lax.fori_loop(0, q_ref.shape[0] // block, step, 0)
    out_ref[:, cols : 2 * cols] = k_acc[...].astype(BF)
    out_ref[:, 2 * cols :] = v_acc[...].astype(BF)


def attend_back(scal, ranges, queries, keys, values, grad_out, seg_row, seg_col, per, kept):
    length, cols = queries.shape
    wide = pltpu.VMEM(queries.shape, F32)
    inputs = (scal, ranges, queries, keys, values, grad_out, seg_row, seg_col, *kept)
    return run(
        functools.partial(attend_back_kernel, per),
        "attend_back",
        shaped((length, 3 * cols), BF),
        inputs,
        16.0,
        [wide, wide],
        lazy=(2, 3, 4, 7),
        late=(2, 3, 4, 7),
        save=range(8, len(inputs)),
        scalars=2,
    )


def table_kernel(scal, forward_ref, resid_ref, table_ref, rows_ref):
    rows_ref[...] = jnp.zeros_like(rows_ref)
    rows_ref[4:5, :] = resid_ref[0:1, :]
    rows_ref[5:7, :] = forward_ref[0:2, :]
    rows_ref[7:8, :] = resid_ref[1:2, :]
    rows_ref[pl.ds(8 + scal[0], 1), :] = forward_ref[2:3, :]
    rest = rows_ref[...]
    unit = unit_rows(16, 128)
    table = jnp.zeros(table_ref.shape, F32)
    for _ in range(3):
        high = rest.astype(BF)
        rest = rest - high.astype(F32)
        table += dot_rows(high, unit)
    table_ref[...] = table


def vector_table(scal, sums_forward, sums_resid):
    width = sums_resid.shape[1]
    return run(
        table_kernel,
        "vector_table",
        shaped((width, 128), F32),
        (scal, sums_forward, sums_resid),
        1.0,
        [pltpu.VMEM((16, width), F32)],
        mebibytes=8,
        lazy=(1,),
    )


TERMS = 8


def vector_places(count, rows, width):
    each = width // rows
    return [(i // each, (i % each) * rows) for i in range(2 * count)]


def query_grads_kernel(cols, count, ringed, scal, *refs, ready):
    a_ref, hat_ref, out_ref, grad_ref, w_ref, table_ref, g_ref = refs
    width = a_ref.shape[1]
    owners = len(RING)
    rows = width // owners
    block = 4 * rows if ringed else 256
    ready(1)

    def place(first):
        if not ringed:
            return slice(first, first + block)
        owner = first // rows
        return slice(first + TERMS * owner, first + TERMS * owner + rows)

    for first in range(0, width, block):
        total = dot_rows(a_ref[:, first : first + block], grad_ref[...]).astype(BF)
        if not ringed:
            g_ref[place(first), : 3 * cols] = total
        else:
            for i in range(4):
                g_ref[place(first + i * rows), : 3 * cols] = total[i * rows : (i + 1) * rows, :]
    row = lax.broadcasted_iota(jnp.int32, (8, 3 * cols), 0)
    rest = dot_rows(jnp.ones((a_ref.shape[0], 8), BF), grad_ref[...])
    terms = jnp.zeros((8, 3 * cols), F32)
    for term in range(3):
        high = rest.astype(BF).astype(F32)
        terms = jnp.where(row == term, high, terms)
        rest = rest - high
    terms = terms.astype(BF)
    for position in (2, 3, 5, 6):
        ready(position)
    chunk = 256
    lane = lax.broadcasted_iota(jnp.int32, (chunk, 128), 1)

    def vectors(i, carry):
        lanes = pl.ds(pl.multiple_of(i * chunk, chunk), chunk)
        weight = w_ref[lanes, :]
        product = dot_rows(hat_ref[:, lanes], grad_ref[...]) * weight.astype(F32)
        gain = jnp.sum(product, axis=1, keepdims=True)
        shift = jnp.sum(dot_cols(weight, terms), axis=1, keepdims=True)
        table = jnp.where(lane == 0, gain, table_ref[lanes, :])
        table_ref[lanes, :] = jnp.where(lane == 1, shift, table)
        return carry

    lax.fori_loop(0, width // chunk, vectors, 0)
    own = pl.ds(pl.multiple_of(scal[0] * cols, cols), cols)
    bias = table_ref[own, :]
    near = lax.broadcasted_iota(jnp.int32, (cols, 128), 1)
    ones = jnp.ones((8, 8), BF)
    for i, column in ((0, 2), (2, 3)):
        part = dot_rows(terms[:, i * cols : (i + 1) * cols], ones)
        bias = jnp.where(near == column, part[:, 0:1], bias)
    table_ref[own, :] = bias
    total = table_ref[...]
    high = total.astype(BF)
    low = (total - high.astype(F32)).astype(BF)
    if not ringed:
        g_ref[:, 3 * cols : 4 * cols] = out_ref[...]
        g_ref[:, 4 * cols : 4 * cols + 16] = high[:, 0:16]
        g_ref[:, 4 * cols + 16 : 4 * cols + 32] = low[:, 0:16]
        g_ref[:, 4 * cols + 32 :] = jnp.zeros((width, 96), BF)
        return
    unit = unit_rows(16, 128)
    lines = (dot_cols(unit, high), dot_cols(unit, low))
    places = vector_places(count, rows, width)
    for owner in range(owners):
        first = owner * rows
        g_ref[place(first), 3 * cols :] = out_ref[first : first + rows, :]
        base = first + TERMS * owner + rows
        g_ref[base : base + TERMS, :] = jnp.zeros((TERMS, width), BF)
        for i, (line, start) in enumerate(places):
            piece = lines[i // count][i % count : i % count + 1, first : first + rows]
            g_ref[base + line : base + line + 1, start : start + rows] = piece.astype(BF)


def query_grads(scal, normed, hat, grad_out, grad, weights, table, count, ringed):
    width, cols = grad_out.shape
    shape = (width, 4 * cols + 128)
    if ringed:
        shape = (width + TERMS * len(RING), 4 * cols)
    return run(
        functools.partial(query_grads_kernel, cols, count, ringed),
        "query_grads",
        shaped(shape, BF),
        (scal, normed, hat, grad_out, grad, weights, table),
        4.0,
        lazy=(1, 2, 3, 5, 6),
        late=(1, 2, 3, 5, 6),
        far=(0,),
    )


def project_back_kernel(scal, grad_ref, w_ref, keep_ref, send_ref):
    block = grad_ref.shape[0] // GROUPS

    def step(i, carry):
        rows = pl.ds(pl.multiple_of(i * block, block), block)
        split_store(scal[0], i, dot_cols(grad_ref[rows, :], w_ref[...]), keep_ref, send_ref)
        return carry

    lax.fori_loop(0, GROUPS, step, 0)


def project_back(scal, grad, weights):
    rows, width = grad.shape[0] // 2, weights.shape[0]
    return run(
        project_back_kernel,
        "project_back",
        (shaped((rows, width), F32), shaped((rows, width), BF)),
        (scal, grad, weights),
        3.0,
        lazy=(2,),
    )


def input_kernel(scal, mine_ref, got_ref, x_ref, dh_ref, vec_ref, out_ref):
    grad = mine_ref[...] + got_ref[...].astype(F32)
    hat, inverse = normalize(x_ref[...].astype(F32))
    out_ref[...] = dh_ref[...] + norm_back(hat, inverse, vec_ref[0:1, :], grad)


def input_back(scal, mine, got, tokens, grad_resid, vec):
    inputs = (scal, mine, got, tokens, grad_resid, vec)
    return run(input_kernel, "input_back", shaped(mine.shape, F32), inputs, 1.0, lazy=(2, 3, 4, 5))


def output_kernel(scal, mine_ref, got_ref, h_ref, vec_ref, out_ref):
    branch = mine_ref[...] + got_ref[...].astype(F32) + vec_ref[7:8, :]
    out_ref[...] = (h_ref[...] + branch).astype(BF)


def output_sum(scal, mine, got, resid, vec):
    inputs = (scal, mine, got, resid, vec)
    return run(output_kernel, "output_sum", shaped(mine.shape, BF), inputs, 0.8, lazy=(2, 3, 4))


def owned_kernel(scal, in_ref, low_ref):
    total = in_ref[0].astype(F32)
    for i in range(1, in_ref.shape[0]):
        total += in_ref[i].astype(F32)
    low_ref[...] = total.astype(BF)


def owned_sum(scal, pieces):
    outputs = shaped(pieces.shape[1:], BF)
    return run(owned_kernel, "owned_sum", outputs, (scal, pieces), 1.5, lazy=(1,))


def squares_kernel(scal, *refs):
    sums = []
    for piece in refs[:4]:
        wide = piece[...].astype(F32)
        sums.append(jnp.sum(wide * wide))
    total = (sums[0] + sums[1]) + (sums[2] + sums[3])
    refs[4][...] = jnp.full(refs[4].shape, total, F32)


def squares_of(scal, pieces):
    outputs = shaped((8, 128), F32)
    return run(squares_kernel, "squares_of", outputs, (scal, *pieces), 1.0, save=range(1, 5))


def owned_vector_kernel(cols, ringed, scal, in_ref, low_ref):
    total = in_ref[0].astype(F32)
    for i in range(1, in_ref.shape[0]):
        total += in_ref[i].astype(F32)
    if ringed:
        rows = total.shape[0] - TERMS
        low_ref[:rows, :] = total[:rows, :].astype(BF)
        vector = total[rows:, :]
        high = vector.astype(BF).astype(F32)
        line = lax.broadcasted_iota(jnp.int32, vector.shape, 0)
        rest = pltpu.roll(vector - high, 3, 0)
        low_ref[rows:, :] = jnp.where(line < 3, high, rest).astype(BF)
        return
    low_ref[:, : 4 * cols] = total[:, : 4 * cols].astype(BF)
    vector = total[:, 4 * cols :]
    high = vector.astype(BF).astype(F32)
    lane = lax.broadcasted_iota(jnp.int32, vector.shape, 1)
    rest = pltpu.roll(vector - high, 32, 1)
    low_ref[:, 4 * cols :] = jnp.where(lane < 32, high, rest).astype(BF)


def owned_vector(scal, pieces, cols, ringed):
    return run(
        functools.partial(owned_vector_kernel, cols, ringed),
        "owned_vector",
        shaped(pieces.shape[1:], BF),
        (scal, pieces),
        1.5,
    )


def vector_sum(pieces, cols, count, ringed, held):
    if ringed:
        rows, width = pieces[0].shape
        rows -= TERMS
        parts = [piece[rows:, :].astype(F32) for piece in pieces]
        lines = (parts[0] + parts[1]) + (parts[2] + parts[3])
        lines = lines + pltpu.roll(lines, TERMS - 3, 0)
        places = vector_places(count, rows, width)
        for i in range(count):
            total = jnp.zeros((1, rows), F32)
            for line, start in (places[i], places[i + count]):
                total += lines[line : line + 1, start : start + rows]
            held[i : i + 1, :] = total
        return held[...]
    parts = [piece[:, 4 * cols :].astype(F32) for piece in pieces]
    table = (parts[0] + parts[1]) + (parts[2] + parts[3])
    rows = lax.broadcasted_iota(jnp.int32, (16, 128), 0)
    lanes = lax.broadcasted_iota(jnp.int32, (16, 128), 1)
    unit = jnp.where((lanes % 16 == rows) & (lanes < 64), 1.0, 0.0)
    return lax.dot_general(
        unit,
        table,
        (((1,), (1,)), ((), ())),
        preferred_element_type=F32,
        precision=lax.Precision.HIGHEST,
    )[:count]


def join_kernel(cols, count, ringed, scal, *refs):
    pieces, forward_ref, squares_ref, held = refs[0:4], refs[4], refs[5], refs[6]
    rows = held.shape[1]
    sums = []
    for piece in pieces:
        wide = piece[:rows, : 4 * cols].astype(F32)
        sums.append(wide * wide)
    vector = vector_sum(pieces, cols, count, ringed, held)
    total = jnp.sum((sums[0] + sums[1]) + (sums[2] + sums[3])) + jnp.sum(vector * vector)
    total = forward_ref[...] + total
    for i in range(squares_ref.shape[0] // 8):
        squares_ref[8 * i : 8 * i + 8, :] = total


def join(scal, pieces, squares, shape, cols, owners, ringed):
    return run(
        functools.partial(join_kernel, cols, shape[0], ringed),
        "join",
        shaped((8 * owners, 128), F32),
        (scal, *pieces, squares),
        1.5,
        [pltpu.VMEM(shape, F32)],
    )


def clip_factor(total_ref):
    total = total_ref[0]
    for i in range(1, total_ref.shape[0]):
        total += total_ref[i]
    norm = jnp.sqrt(total[0:1, 0:1])
    return norm, jnp.minimum(1.0, clip_limit / (norm + 1e-06))


def adam_kernel(counts, cols, ringed, scal, total_ref, *refs):
    attention, refs = refs[0:4], refs[4:]
    pieces, sources, targets, norm_ref = refs[0:4], refs[4:16], refs[16:31], refs[31]
    held, copies = refs[32:44], refs[44:47]
    loads, stores = refs[47:50], refs[50:53]
    grads, grad_loads, attention_ref, vector_ref = refs[53:57], refs[57], refs[58], refs[59]
    norm, factor = clip_factor(total_ref)
    norm_ref[...] = jnp.broadcast_to(norm, norm_ref.shape)
    decays = (weight_decay, weight_decay, 0.0)

    def chunk(kind, i):
        if counts[kind] == 1:
            return (slice(None), slice(None))
        size = held[4 * kind].shape[1] // counts[kind]
        return (slice(None), pl.ds(pl.multiple_of(i * size, size), size))

    def load(kind, i, state):
        place = chunk(kind, i)
        number = 4 * kind + state
        return pltpu.make_async_copy(
            sources[number].at[place], held[number].at[place], loads[kind].at[i, state]
        )

    def store(kind, i, state):
        place = chunk(kind, i)
        source = held[4 * kind + state] if state < 4 else copies[kind]
        return pltpu.make_async_copy(
            source.at[place], targets[3 * state + kind].at[place], stores[kind].at[i, state]
        )

    def every(kind, action):
        def step(i, carry):
            action(kind, i)
            return carry

        lax.fori_loop(0, counts[kind], step, 0)

    def start(kind, i):
        for state in range(4):
            load(kind, i, state).start()

    def work(kind, i):
        for state in range(4):
            load(kind, i, state).wait()
        place = chunk(kind, i)
        if kind == 0:
            gradient = attention_ref[place].astype(F32)
        elif kind == 2:
            gradient = vector_sum(attention, cols, held[8].shape[0], ringed, vector_ref)
        else:
            size = held[4].shape[1] // counts[1]
            half = pl.ds(pl.multiple_of((i // GROUPS) * size, size), size)
            source = scal[0] ^ (i % GROUPS)
            gradient = grads[0][:, half]
            for k in range(1, GROUPS):
                gradient = jnp.where(source == k, grads[k][:, half], gradient)
            gradient = gradient.astype(F32)
        results = adam_update(
            *[held[4 * kind + state][place] for state in range(4)], gradient, factor, decays[kind]
        )
        for state, value in zip((0, 1, 2, 3), results):
            held[4 * kind + state][place] = value
        copies[kind][place] = results[0].astype(BF)
        for state in range(5):
            store(kind, i, state).start()

    def finish(kind, i):
        for state in range(5):
            store(kind, i, state).wait()

    moves = [
        pltpu.make_async_copy(piece, grad, grad_loads.at[i])
        for i, (piece, grad) in enumerate(zip(pieces, grads))
    ]
    for move in moves:
        move.start()
    for kind in (1, 0, 2):
        every(kind, start)
    width = attention_ref.shape[1] // 4
    for member in range(GROUPS):

        @pl.when(scal[0] == member)
        def _():
            for i in range(4):
                for k in range(GROUPS):
                    first = i * width + (member ^ k) * cols
                    attention_ref[:, first : first + cols] = attention[k][
                        : held[0].shape[0], i * cols : (i + 1) * cols
                    ]

    for move in moves:
        move.wait()
    for kind in (1, 0, 2):
        every(kind, work)
    for kind in (1, 0, 2):
        every(kind, finish)


def adam(scal, totals, attention_grads, forward_grads_by_member, states, cols, ringed):
    counts = (4, 2 * GROUPS, 1)
    kinds = [states[4 * kind].shape for kind in range(3)]
    out_shape = [pltpu.HBM(shape, F32) for _ in range(4) for shape in kinds]
    out_shape += [pltpu.HBM(shape, BF) for shape in kinds]
    out_shape += [shaped((8, 128), F32)]
    return pl.pallas_call(
        functools.partial(adam_kernel, counts, cols, ringed),
        out_shape=out_shape,
        in_specs=[smem()] + [vmem()] * 5 + [far_space()] * 16,
        out_specs=[far_space()] * 15 + [vmem()],
        scratch_shapes=[pltpu.VMEM(kinds[kind], F32) for kind in range(3) for _ in range(4)]
        + [pltpu.VMEM(shape, BF) for shape in kinds]
        + [pltpu.SemaphoreType.DMA((count, 4)) for count in counts]
        + [pltpu.SemaphoreType.DMA((count, 5)) for count in counts]
        + [pltpu.VMEM(item.shape, item.dtype) for item in forward_grads_by_member]
        + [pltpu.SemaphoreType.DMA((GROUPS,))]
        + [pltpu.VMEM(kinds[0], BF), pltpu.VMEM(kinds[2], F32)],
        compiler_params=params(32),
        cost_estimate=cost(9.0),
        name="adam",
    )(scal, totals, *attention_grads, *map(pin, forward_grads_by_member), *map(pin, states))


def adam_update(master, moment, second, teacher, gradient, factor, decay_rate):
    clipped = gradient * factor
    moment_new = beta_one * moment + (1.0 - beta_one) * clipped
    second_new = beta_two * second + (1.0 - beta_two) * clipped * clipped
    scale_one = 1.0 - beta_one**ADAM_STEP
    scale_two = 1.0 - beta_two**ADAM_STEP
    update = (moment_new * (1.0 / scale_one)) / (
        jnp.sqrt(second_new * (1.0 / scale_two)) + adam_epsilon
    )
    master_new = master * (1.0 - learn_rate * decay_rate) - learn_rate * update
    teacher_new = teacher_keep * teacher + (1.0 - teacher_keep) * master_new
    return (master_new, moment_new, second_new, teacher_new)


def swap(part, bit):
    return lax.ppermute(part, "head", [(i, i ^ bit) for i in range(4)])


def spread(part, *others):
    across = swap(part, 2)
    if others:
        return [
            part,
            swap(after(part, *others), 1),
            across,
            swap(after(across, *others), 1),
        ]
    return [part, swap(part, 1), across, swap(across, 1)]


RING = (0, 2, 4, 6, 7, 5, 3, 1)


def ring_owners(count):
    if count != len(RING):
        return np.zeros((count, 1), np.int32)
    table = []
    for device in range(count):
        place = RING.index(device)
        owners = [device]
        for hop in range(1, count // 2 + 1):
            owners.append(RING[(place - hop) % count])
            owners.append(RING[(place + hop) % count])
        table.append(owners)
    return np.asarray(table, np.int32)


def after(value, *others):
    return lax.optimization_barrier((value, *others))[0]


class Ring:
    def __init__(self, block, count, halved=False):
        self.count = count
        self.halved = halved
        self.ringed = count == len(RING)
        self.hops = count // 2 if self.ringed else 1
        self.front = self.rear = block
        self.pieces = [block]
        self.done = 0

    def send(self, array, distance):
        count = self.count
        pairs = [(RING[i], RING[(i + distance) % count]) for i in range(count)]
        return lax.ppermute(array, "dp", pairs)

    def hop(self, *others):
        self.done += 1
        if not self.ringed:
            self.pieces = [lax.all_gather(after(self.front, *others), "dp", axis=0, tiled=True)]
            return self
        if self.done > 1 or others:
            self.front, self.rear = lax.optimization_barrier((self.front, self.rear, *others))[:2]
        if self.done == self.hops and self.halved:
            half = self.front.shape[0] // 2
            self.front, self.rear = self.front[:half], self.rear[half:]
        self.front = self.send(self.front, 1)
        self.pieces.append(self.front)
        if self.done < self.hops or self.halved:
            self.rear = self.send(self.rear, -1)
            self.pieces.append(self.rear)
        return self

    def rest(self):
        while self.done < self.hops:
            self.hop()
        return self.pieces


def exchange_owned(grads, count):
    blocks = grads.reshape(count, -1, grads.shape[1])
    return lax.all_to_all(blocks, "dp", split_axis=0, concat_axis=0)


def local(
    tokens,
    cotangent,
    segments,
    attention_master,
    feedforward_master,
    vector_master,
    attention_moment,
    feedforward_moment,
    vector_moment,
    attention_second,
    feedforward_second,
    vector_second,
    attention_teacher,
    feedforward_teacher,
    vector_teacher,
):
    width = tokens.shape[1]
    owners = lax.axis_size("dp")
    groups = lax.axis_size("head")
    hidden = feedforward_master.shape[1] // 2
    per = HEADS // groups
    cols = per * HEAD_DIM
    part = hidden // groups

    owner_table = ring_owners(owners)
    table = np.concatenate(
        [
            np.tile(np.arange(groups, dtype=np.int32), owners)[:, None],
            np.repeat(owner_table, groups, axis=0),
        ],
        axis=1,
    )
    place = lax.axis_index("dp") * groups + lax.axis_index("head")
    scal = lax.dynamic_index_in_dim(jnp.asarray(table), place, 0, keepdims=False)
    first = Ring(pack_attention(scal, attention_master, vector_master, cols), owners)
    first.rest()
    ringed = owners == len(RING)
    early = first.pieces[-3:-1] if ringed else first.pieces
    token_across, grad_across = swap(tokens, 2), swap(cotangent, 2)
    token, token_across = lax.optimization_barrier((tokens, token_across, *early))[:2]
    x_all = place_blocks(scal, [token, swap(token, 1), token_across, swap(token_across, 1)])
    second = Ring(pack_forward(scal, feedforward_master, part), owners)
    second.hop(first.pieces[-1])

    queries, keys, values, w_qkv, w_o, vec, seg_col, normed, hat, ranges = project(
        scal, segments, x_all, first.pieces, cols
    )
    if ringed:
        second.hop(queries)
    half = x_all.shape[0] // 2
    w_across = swap(w_o, 2)
    mixed_low, *kept = attend(
        scal,
        ranges,
        after(queries, grad_across),
        keys,
        values,
        segments,
        seg_col,
        per,
        0,
        half,
        (w_qkv, vec, normed, hat),
    )
    far_q, far_k, far_v, far_col, far_weights, far_vec, *far_normed = kept
    low_across = swap(mixed_low, 2)
    w_across = after(w_across, mixed_low)
    mixed_high = attend(
        scal, ranges, after(queries, w_across), keys, values, segments, seg_col, per, half, half
    )
    if ringed:
        second.hop(mixed_high)
    high_across = swap(after(mixed_high, low_across), 2)
    w_across, low_across, w_o, mixed_low, grad, grad_across = lax.optimization_barrier(
        (w_across, low_across, w_o, mixed_low, cotangent, grad_across, high_across)
    )[:6]
    dy_all = place_blocks(scal, [grad, swap(grad, 1), grad_across, swap(grad_across, 1)])
    w_out = [w_o, swap(w_o, 1), w_across, swap(w_across, 1)]
    mixed = [
        (mixed_low, mixed_high),
        (swap(mixed_low, 1), swap(mixed_high, 1)),
        (low_across, high_across),
        (swap(low_across, 1), swap(high_across, 1)),
    ]
    (
        normed_two,
        active,
        grad_pre,
        keep,
        send,
        resid,
        w_ff,
        w_rows,
        sums_forward,
        mixed_all,
    ) = forward_back(scal, x_all, dy_all, mixed, w_out, second.rest(), vec, cols)
    grad_ff, far_active, *kept = forward_grads(
        scal,
        normed_two,
        active,
        grad_pre,
        dy_all,
        (resid, sums_forward, w_rows, w_ff, mixed_all),
    )
    far_resid, far_sums, far_rows, far_ff, far_mixed = kept
    got = swap(send, 1)
    grad_ff, got = lax.optimization_barrier((grad_ff, got))
    owned_ff = exchange_owned(grad_ff, owners)
    mine, send = merge(scal, keep, got)
    keep_branch, send_branch, cot_own = branch_part(
        scal, far_active, after(far_ff, send), cotangent
    )
    got = swap(send, 2)
    grad_resid, grad_low, sums_resid = resid_back(
        scal, after(mine, send_branch), got, resid, cot_own, vec
    )
    low_across = swap(grad_low, 2)
    mine, send = merge(
        scal, keep_branch, swap(after(send_branch, grad_low), 1), lazy=(1,)
    )
    table = vector_table(scal, far_sums, sums_resid)
    low_across = after(low_across, send, table)
    low_blocks = [grad_low, swap(grad_low, 1), low_across, swap(low_across, 1)]
    grad_mixed, grad_out = mixed_back(scal, low_blocks, far_mixed, far_rows)
    grad_qkv, far_dh, far_table, far_grad_out = attend_back(
        scal,
        ranges,
        far_q,
        far_k,
        far_v,
        grad_mixed,
        segments,
        far_col,
        per,
        (grad_resid, table, grad_out),
    )
    send_branch = send
    pack = query_grads(
        scal,
        far_normed[0],
        far_normed[1],
        far_grad_out,
        grad_qkv,
        far_weights,
        far_table,
        vector_master.shape[0],
        ringed,
    )
    owned_pack = exchange_owned(pack, owners)
    forward_parts = spread(owned_sum(scal, after(owned_ff, pack)))
    forward_squares, *forward_parts = squares_of(scal, forward_parts)
    keep, send = project_back(scal, grad_qkv, after(far_weights, pack))
    mine_input, send = merge(scal, keep, swap(send, 1))
    got_branch = swap(after(send_branch, pack), 2)
    block_output = output_sum(scal, mine, got_branch, far_resid, far_vec)
    got_input = swap(send, 2)
    owned_pack = after(owned_pack, forward_squares, got_input)
    input_gradient = input_back(scal, mine_input, got_input, tokens, far_dh, far_vec)
    attention_parts = spread(owned_vector(scal, owned_pack, cols, ringed))
    squares = join(
        scal, attention_parts, forward_squares, vector_master.shape, cols, owners, ringed
    )
    totals = lax.all_to_all(
        squares.reshape(owners, 8, 128), "dp", split_axis=0, concat_axis=0
    )
    *results, norm = adam(
        scal,
        totals,
        attention_parts,
        forward_parts,
        (
            attention_master,
            attention_moment,
            attention_second,
            attention_teacher,
            feedforward_master,
            feedforward_moment,
            feedforward_second,
            feedforward_teacher,
            vector_master,
            vector_moment,
            vector_second,
            vector_teacher,
        ),
        cols,
        ringed,
    )
    return (block_output, input_gradient, norm[0, 0], *results)


def solution(mesh):
    rows = P(("dp", "head"), None)
    shard = P("dp", None)
    vector = P(None, "dp")
    return jax.shard_map(
        local,
        mesh=mesh,
        in_specs=(rows, rows, shard) + (shard, shard, vector) * 4,
        out_specs=(rows, rows, P()) + (shard, shard, vector) * 5,
        check_vma=False,
    )
```

```python
import functools

import jax
import jax.numpy as jnp
import numpy as np
from jax import lax
from jax.experimental import pallas as pl
from jax.experimental.pallas import tpu as pltpu
from jax.sharding import PartitionSpec as P

HEADS = 12
HEAD_DIM = 64
ADAM_STEP = 3

norm_epsilon = 1e-06
beta_one = 0.5
beta_two = 0.5
adam_epsilon = 1e-08
learn_rate = 0.05
weight_decay = 0.05
teacher_keep = 0.8
clip_limit = 1.0
masked_score = -1e30

BF = jnp.bfloat16
F32 = jnp.float32


def dot_rows(left, right):
    return lax.dot_general(left, right, (((0,), (0,)), ((), ())), preferred_element_type=F32)


def dot_cols(left, right):
    return lax.dot_general(left, right, (((1,), (1,)), ((), ())), preferred_element_type=F32)


def dot(left, right):
    return jnp.dot(left, right, preferred_element_type=F32)


def normalize(values):
    center = jnp.mean(values, axis=-1, keepdims=True)
    deviate = values - center
    spread = jnp.mean(deviate * deviate, axis=-1, keepdims=True)
    inverse = lax.rsqrt(spread + norm_epsilon)
    return deviate * inverse, inverse


def norm_back(hat, inverse, gain, grad):
    scaled = grad * gain
    mean_one = jnp.mean(scaled, axis=-1, keepdims=True)
    mean_two = jnp.mean(scaled * hat, axis=-1, keepdims=True)
    return inverse * (scaled - mean_one - hat * mean_two)


def head_lanes(index, shape):
    lane = lax.broadcasted_iota(jnp.int32, shape, 1)
    return (lane >= index * HEAD_DIM) & (lane < (index + 1) * HEAD_DIM)


def unit_rows(rows, columns):
    row = lax.broadcasted_iota(jnp.int32, (rows, columns), 0)
    column = lax.broadcasted_iota(jnp.int32, (rows, columns), 1)
    return jnp.where(row == column, 1.0, 0.0).astype(BF)


def smem():
    return pl.BlockSpec(memory_space=pltpu.SMEM)


def vmem():
    return pl.BlockSpec(memory_space=pltpu.VMEM)


def whole(*shape):
    return pl.BlockSpec(shape, lambda *index: (0,) * len(shape))


def shaped(shape, kind):
    return jax.ShapeDtypeStruct(shape, kind)


def params(mebibytes):
    return pltpu.CompilerParams(vmem_limit_bytes=mebibytes * 2**20)


COST_SCALE = 1.0


def cost(microseconds):
    return pl.CostEstimate(
        flops=0, transcendentals=0, bytes_accessed=int(microseconds * COST_SCALE * 3.6e6)
    )


def pin(array):
    return pltpu.with_memory_space_constraint(array, pltpu.HBM)


def far_space():
    return pl.BlockSpec(memory_space=pltpu.HBM)


def run(
    kernel,
    name,
    outputs,
    inputs,
    microseconds,
    scratch=(),
    mebibytes=16,
    lazy=(),
    save=(),
    far=(),
    late=(),
    scalars=1,
    scalar_outputs=(),
):
    single = not isinstance(outputs, tuple)
    outputs = [outputs] if single else list(outputs)
    lazy, save, far = list(lazy), list(save), list(far)
    count, produced, own = len(inputs), len(outputs), len(scratch)
    buffers = [pltpu.VMEM(inputs[i].shape, inputs[i].dtype) for i in lazy]
    buffers += [pltpu.VMEM(outputs[i].shape, outputs[i].dtype) for i in far]
    moves = len(lazy) + len(save) + len(far)
    if moves:
        buffers.append(pltpu.SemaphoreType.DMA((moves,)))

    def body(*refs):
        items = list(refs[: count + produced])
        saved = refs[count + produced : count + produced + len(save)]
        rest = refs[count + produced + len(save) :]
        inner, extra = rest[:own], rest[own:]
        copies, number = [], 0
        for j, i in enumerate(lazy):
            copies.append(pltpu.make_async_copy(refs[i], extra[j], extra[-1].at[number]))
            items[i] = extra[j]
            number += 1
        stores = []
        for j, i in enumerate(save):
            stores.append(pltpu.make_async_copy(refs[i], saved[j], extra[-1].at[number]))
            number += 1
        last = []
        for j, i in enumerate(far):
            buffer = extra[len(lazy) + j]
            last.append(pltpu.make_async_copy(buffer, refs[count + i], extra[-1].at[number]))
            items[count + i] = buffer
            number += 1
        for copy in copies + stores:
            copy.start()
        for i, copy in zip(lazy, copies):
            if i not in late:
                copy.wait()
        if late:
            kernel(*items, *inner, ready=lambda i: copies[lazy.index(i)].wait())
        else:
            kernel(*items, *inner)
        for copy in last:
            copy.start()
        for copy in stores + last:
            copy.wait()

    shapes = [pltpu.HBM(item.shape, item.dtype) if i in far else item for i, item in enumerate(outputs)]
    results = pl.pallas_call(
        body,
        out_shape=shapes + [pltpu.HBM(inputs[i].shape, inputs[i].dtype) for i in save],
        in_specs=[smem()] * scalars
        + [far_space() if i in lazy else vmem() for i in range(scalars, count)],
        out_specs=[
            far_space() if i in far else smem() if i in scalar_outputs else vmem()
            for i in range(produced)
        ]
        + [far_space()] * len(save),
        scratch_shapes=list(scratch) + buffers,
        compiler_params=params(mebibytes),
        cost_estimate=cost(microseconds),
        name=name,
    )(*[pin(item) if i in lazy else item for i, item in enumerate(inputs)])
    return results[0] if single and not save else tuple(results)


GROUPS = 4


def pack_kernel(cols, scal, *refs):
    vector_ref, out_ref = refs[4:6]
    for side in range(2):

        @pl.when(scal[0] % 2 == side)
        def _():
            for i in range(4):
                out_ref[:, i * cols : (i + 1) * cols] = refs[i][
                    :, side * cols : (side + 1) * cols
                ].astype(BF)

    vector = vector_ref[...].astype(BF)
    out_ref[:, 4 * cols :] = dot_rows(vector, unit_rows(vector.shape[0], 128)).astype(BF)


def pack_attention(scal, attention, vector, cols):
    rows = attention.shape[0]

    def pair(i):
        return pl.BlockSpec((rows, 2 * cols), lambda step, scal: (0, 2 * i + scal[0] // 2))

    return pl.pallas_call(
        functools.partial(pack_kernel, cols),
        out_shape=shaped((rows, 4 * cols + 128), BF),
        grid_spec=pltpu.PrefetchScalarGridSpec(
            num_scalar_prefetch=1,
            grid=(1,),
            in_specs=[pair(i) for i in range(4)] + [whole(*vector.shape)],
            out_specs=whole(rows, 4 * cols + 128),
        ),
        compiler_params=params(8),
        cost_estimate=cost(1.5),
        name="pack_attention",
    )(scal, *[pin(attention)] * 4, pin(vector))


def cast_kernel(scal, in_ref, out_ref):
    out_ref[...] = in_ref[...].astype(BF)


def pack_forward(scal, forward, part):
    rows = forward.shape[0]
    return pl.pallas_call(
        cast_kernel,
        out_shape=shaped((rows, 2 * part), BF),
        grid_spec=pltpu.PrefetchScalarGridSpec(
            num_scalar_prefetch=1,
            grid=(2,),
            in_specs=[pl.BlockSpec((rows, part), lambda i, scal: (0, GROUPS * i + scal[0]))],
            out_specs=pl.BlockSpec((rows, part), lambda i, scal: (0, i)),
        ),
        compiler_params=params(8),
        cost_estimate=cost(1.5),
        name="pack_forward",
    )(scal, forward)


def place_rows(scal, pieces, target):
    rows = pieces[0].shape[0]
    if len(pieces) == 1:
        target[...] = pieces[0][...]
        return
    for i, piece in enumerate(pieces):
        size = piece.shape[0]
        first = rows - size if i == len(RING) else 0
        start = pl.multiple_of(scal[1 + i] * rows + first, size)
        target[pl.ds(start, size), :] = piece[...]


def place_members(scal, pieces, target):
    rows = pieces[0].shape[0]
    for i, piece in enumerate(pieces):
        start = pl.multiple_of((scal[0] ^ i) * rows, rows)
        target[pl.ds(start, rows), :] = piece[...]


def place_kernel(scal, *refs):
    place_members(scal, refs[0:4], refs[4])


def place_blocks(scal, blocks):
    rows, width = blocks[0].shape
    wide = shaped((GROUPS * rows, width), BF)
    return run(place_kernel, "place_blocks", wide, (scal, *blocks), 0.5, mebibytes=2)


def fold(value):
    rows, columns = value.shape
    count = 128 // (columns - 128)
    share = rows // count
    rest = [value[i * share : (i + 1) * share, 128:] for i in range(count)]
    return value[:, :128], jnp.concatenate(rest, axis=1)


def folded_rows(rows, columns):
    return rows + rows * (columns - 128) // 128


def segments_kernel(scal, seg_ref, col_ref, ranges_ref):
    numbers = seg_ref[...]
    key_ranges(numbers, ranges_ref)
    lines = jnp.broadcast_to(numbers.astype(F32), (8, numbers.shape[1])).astype(BF)
    col_ref[...] = dot_rows(lines, unit_rows(8, 128))[:, 0:1].astype(jnp.int32)


def read_segments(scal, segments):
    outputs = (shaped((segments.shape[1], 1), jnp.int32), shaped((16,), jnp.int32))
    inputs = (scal, segments)
    return run(
        segments_kernel, "read_segments", outputs, inputs, 1.0, mebibytes=4, scalar_outputs=(1,)
    )


def project_kernel(count, cols, scal, x_ref, *refs):
    pieces = refs[:count]
    q_ref, k_ref, v_ref, w_ref, wo_ref, vec_ref, a_ref, hat_ref = refs[count : 8 + count]
    weights, wq_ref, wk_ref, wv_ref = refs[8 + count : 12 + count]
    place_rows(scal, pieces, weights)
    for i, ref in enumerate((wq_ref, wk_ref, wv_ref)):
        ref[...] = weights[:, i * cols : (i + 1) * cols]
    w_ref[...] = weights[:, : 3 * cols]
    top, rest = fold(weights[:, 3 * cols : 4 * cols])
    wo_ref[: top.shape[0], :] = top
    wo_ref[top.shape[0] :, :] = rest
    unit = unit_rows(16, 128)
    vec_ref[...] = dot_cols(unit, weights[:, 4 * cols :])
    start = pl.multiple_of(scal[0] * cols, cols)
    own = dot_cols(unit, weights[pl.ds(start, cols), 4 * cols :])
    query_bias, value_bias = own[2:3, :], own[3:4, :]
    gain, shift = vec_ref[0:1, :], vec_ref[1:2, :]
    block = 256

    def step(i, carry):
        rows = pl.ds(pl.multiple_of(i * block, block), block)
        hat, _ = normalize(x_ref[rows, :].astype(F32))
        normed = (hat * gain + shift).astype(BF)
        a_ref[rows, :] = normed
        hat_ref[rows, :] = hat.astype(BF)
        q_ref[rows, :] = (dot(normed, wq_ref[...]) + query_bias).astype(BF)
        k_ref[rows, :] = dot(normed, wk_ref[...]).astype(BF)
        v_ref[rows, :] = (dot(normed, wv_ref[...]) + value_bias).astype(BF)
        return carry

    lax.fori_loop(0, x_ref.shape[0] // block, step, 0)


def project(scal, x_all, pieces, cols):
    length, width = x_all.shape
    outputs = (
        (shaped((length, cols), BF),) * 3
        + (shaped((width, 3 * cols), BF),)
        + (shaped((folded_rows(width, cols), 128), BF),)
        + (shaped((16, width), F32),)
        + (shaped((length, width), BF),) * 2
    )
    return run(
        functools.partial(project_kernel, len(pieces), cols),
        "project",
        outputs,
        (scal, x_all, *pieces),
        4.5,
        scratch=[pltpu.VMEM((width, 4 * cols + 128), BF)] + [pltpu.VMEM((width, cols), BF)] * 3,
    )


QUERIES = 256
WINDOWS = (512, 576)


def key_ranges(numbers, ranges_ref):
    length = numbers.shape[1]
    images = jnp.where(numbers < 0, length, numbers)
    place = lax.broadcasted_iota(jnp.int32, numbers.shape, 1)
    for block in range(length // QUERIES):
        first = jnp.max(jnp.where(place == block * QUERIES, images, 0))
        last = jnp.max(jnp.where(place == (block + 1) * QUERIES - 1, images, 0))
        ranges_ref[2 * block] = jnp.sum((images < first).astype(jnp.int32))
        ranges_ref[2 * block + 1] = jnp.sum((images <= last).astype(jnp.int32))


def each_window(ranges, block, length, body):
    low, high = ranges[2 * block], ranges[2 * block + 1]
    taken = jnp.bool_(False)
    for size in [size for size in WINDOWS if size < length] + [length]:
        start = (jnp.minimum(low, length - size) // 16) * 16
        fits = high - start <= size

        @pl.when(fits & jnp.logical_not(taken))
        def _():
            body(pl.multiple_of(start, 16), size)

        taken = taken | fits


def each_head(per, size, body, carry):
    if size > WINDOWS[0]:
        return lax.fori_loop(0, per, body, carry)
    for head in range(per):
        carry = body(head, carry)
    return carry


def attend_kernel(per, first, scal, ranges, q_ref, k_ref, v_ref, seg_row_ref, seg_col_ref, *refs):
    out_ref, held = refs[-2:]
    block = QUERIES
    length = k_ref.shape[0]

    def step(i, carry):
        start = pl.multiple_of(first + i * block, block)
        near = pl.ds(pl.multiple_of(i * block, block), block)

        def body(key_start, size):
            window = pl.ds(key_start, size)
            keys, values = k_ref[window, :], v_ref[window, :]
            numbers = seg_row_ref[...]
            if size < length:
                span = size - size % 128 + 256
                base = jnp.minimum(key_start // 128, (length - span) // 128) * 128
                numbers = seg_row_ref[:, pl.ds(pl.multiple_of(base, 128), span)]
                numbers = jnp.broadcast_to(numbers, (8, span))
                numbers = pltpu.roll(numbers, span - (key_start - base), 1)[0:1, :size]
            same = seg_col_ref[pl.ds(start, block), :] == numbers
            queries = q_ref[pl.ds(start, block), :] * jnp.asarray(HEAD_DIM**-0.5, BF)

            def one(head, result):
                lanes = head_lanes(head, queries.shape)
                score = dot_cols(jnp.where(lanes, queries, jnp.zeros_like(queries)), keys)
                score = jnp.where(same, score, masked_score)
                largest = jnp.max(score, axis=1, keepdims=True)
                power = jnp.exp(score - largest)
                total = jnp.sum(power, axis=1, keepdims=True)
                chance = (power * (1.0 / total)).astype(BF)
                return jnp.where(lanes, dot(chance, values), result)

            result = each_head(per, size, one, jnp.zeros(queries.shape, F32))
            held[near, :] = result.astype(BF)

        each_window(ranges, first // block + i, length, body)
        return carry

    lax.fori_loop(0, held.shape[0] // block, step, 0)
    top, rest = fold(held[...])
    out_ref[: top.shape[0], :] = top
    out_ref[top.shape[0] :, :] = rest


def attend(scal, ranges, queries, keys, values, seg_row, seg_col, per, first, count, kept=()):
    inputs = (scal, ranges, queries, keys, values, seg_row, seg_col, *kept)
    return run(
        functools.partial(attend_kernel, per, first),
        "attend",
        shaped((folded_rows(count, queries.shape[1]), 128), BF),
        inputs,
        7.0 * count / queries.shape[0],
        [pltpu.VMEM((count, queries.shape[1]), BF)],
        save=(2, 3, 4, 6, *range(7, len(inputs))) if kept else (),
        scalars=2,
    )


def forward_kernel(count, cols, parts, scal, x_ref, dy_ref, *refs):
    mixed, w_out = [refs[k * parts : (k + 1) * parts] for k in range(4)], refs[4 * parts :][:4]
    refs = refs[4 * parts + 4 :]
    pieces = refs[:count]
    vec_ref = refs[count]
    c_ref, u_ref, df_ref, keep_ref, send_ref, h_ref, w_ref, rows_ref, sums_ref, o_ref = refs[
        1 + count : 11 + count
    ]
    out_weight = refs[11 + count]
    member = scal[0]
    length, width = x_ref.shape
    part = w_ref.shape[1] // 2
    block = length // GROUPS
    narrow = cols - 128
    place_rows(scal, pieces, w_ref)

    def unfold(target, first, column, item):
        rows = item.shape[0] * 128 // cols
        share = rows * narrow // 128
        target[first : first + rows, column : column + 128] = item[:rows, :]
        for i in range(rows // share):
            start = first + i * share
            target[start : start + share, column + 128 : column + cols] = item[
                rows:, i * narrow : (i + 1) * narrow
            ]

    for index in range(GROUPS):

        @pl.when(member == index)
        def _():
            for k in range(GROUPS):
                column = (index ^ k) * cols
                unfold(out_weight, 0, column, w_out[k])
                for half in range(parts):
                    unfold(o_ref, half * (length // parts), column, mixed[k][half])

    rows_ref[...] = out_weight[pl.ds(pl.multiple_of(member * cols, cols), cols), :]
    zero = jnp.zeros((1, width), F32)
    up_bias = vec_ref[pl.ds(8 + member, 1), :]

    def run_block(step, carry):
        rows = pl.ds(pl.multiple_of(step * block, block), block)
        resid = x_ref[rows, :].astype(F32) + vec_ref[4:5, :] + dot(o_ref[rows, :], out_weight[...])

        @pl.when(step == member)
        def _():
            h_ref[...] = resid

        hat, _ = normalize(resid)
        normed = (hat * vec_ref[5:6, :] + vec_ref[6:7, :]).astype(BF)
        c_ref[rows, :] = normed
        pre = dot(normed, w_ref[:, :part]) + up_bias
        phi = 0.5 * (1.0 + lax.erf(pre * 0.7071067811865476))
        u_ref[rows, :] = (pre * phi).astype(BF)
        slope = phi + pre * (jnp.exp(-0.5 * pre * pre) * 0.3989422804014327)
        grad_pre = (dot(dy_ref[rows, :], w_ref[:, part:]) * slope).astype(BF)
        df_ref[rows, :] = grad_pre
        grad_normed = dot_cols(grad_pre, w_ref[:, :part])
        split_store(member, step, grad_normed, keep_ref, send_ref)
        return (
            carry[0] + jnp.sum(grad_normed * hat, axis=0, keepdims=True),
            carry[1] + jnp.sum(grad_normed, axis=0, keepdims=True),
            carry[2] + jnp.sum(grad_pre.astype(F32), axis=0, keepdims=True),
        )

    carry = lax.fori_loop(0, GROUPS, run_block, (zero, zero, zero))
    sums_ref[...] = jnp.zeros_like(sums_ref)
    for i in range(3):
        sums_ref[i : i + 1, :] = carry[i]


def split_store(member, index, value, keep_ref, send_ref):
    mine = (index % 2) == (member % 2)
    rows = value.shape[0]
    place = pl.ds(pl.multiple_of((index // 2) * rows, rows), rows)

    @pl.when(mine)
    def _():
        keep_ref[place, :] = value

    @pl.when(jnp.logical_not(mine))
    def _():
        send_ref[place, :] = value.astype(BF)


def forward_back(scal, x_all, dy_all, mixed, w_out, pieces, vec, cols):
    length, width = x_all.shape
    part = pieces[0].shape[1] // 2
    rows = length // GROUPS
    outputs = (
        shaped((length, width), BF),
        shaped((length, part), BF),
        shaped((length, part), BF),
        shaped((2 * rows, width), F32),
        shaped((2 * rows, width), BF),
        shaped((rows, width), F32),
        shaped((width, 2 * part), BF),
        shaped((cols, width), BF),
        shaped((8, width), F32),
        shaped((length, width), BF),
    )
    flat = [item for items in mixed for item in items]
    return run(
        functools.partial(forward_kernel, len(pieces), cols, len(mixed[0])),
        "forward_back",
        outputs,
        (scal, x_all, dy_all, *flat, *w_out, *pieces, vec),
        13.0,
        [pltpu.VMEM((width, width), BF)],
    )


def forward_grads_kernel(scal, c_ref, u_ref, df_ref, dy_ref, *refs):
    g_ref = refs[-1]
    part = u_ref.shape[1]
    third = c_ref.shape[1] // 3

    def weight(i, carry):
        lanes = pl.ds(pl.multiple_of(i * third, third), third)
        g_ref[lanes, :part] = dot_rows(c_ref[:, lanes], df_ref[...]).astype(BF)
        g_ref[lanes, part:] = dot_rows(dy_ref[:, lanes], u_ref[...]).astype(BF)
        return carry

    lax.fori_loop(0, 3, weight, 0)


def forward_grads(scal, normed, active, grad_pre, dy_all, kept):
    width = normed.shape[1]
    part = active.shape[1]
    outputs = shaped((width, 2 * part), BF)
    inputs = (scal, normed, active, grad_pre, dy_all, *kept)
    return run(
        forward_grads_kernel,
        "forward_grads",
        outputs,
        inputs,
        4.0,
        save=(2, *range(5, len(inputs))),
    )


def branch_kernel(scal, u_ref, w_ref, dy_ref, keep_ref, send_ref, own_ref):
    own_ref[...] = dy_ref[...]
    part = u_ref.shape[1]
    block = u_ref.shape[0] // GROUPS

    def branch(i, carry):
        rows = pl.ds(pl.multiple_of(i * block, block), block)
        split_store(scal[0], i, dot_cols(u_ref[rows, :], w_ref[:, part:]), keep_ref, send_ref)
        return carry

    lax.fori_loop(0, GROUPS, branch, 0)


def branch_part(scal, active, weights, cotangent):
    rows = active.shape[0] // GROUPS
    width = weights.shape[0]
    return run(
        branch_kernel,
        "branch_part",
        (
            shaped((2 * rows, width), F32),
            shaped((2 * rows, width), BF),
            shaped(cotangent.shape, BF),
        ),
        (scal, active, weights, cotangent),
        3.0,
        lazy=(1, 2, 3),
        far=(0,),
    )


def merge_kernel(scal, keep_ref, got_ref, mine_ref, send_ref):
    rows = mine_ref.shape[0]
    mine = pl.ds(pl.multiple_of((scal[0] // 2) * rows, rows), rows)
    other = pl.ds(pl.multiple_of((1 - scal[0] // 2) * rows, rows), rows)
    mine_ref[...] = keep_ref[mine, :] + got_ref[mine, :].astype(F32)
    send_ref[...] = (keep_ref[other, :] + got_ref[other, :].astype(F32)).astype(BF)


def merge(scal, keep, got, lazy=()):
    rows, width = keep.shape
    outputs = (shaped((rows // 2, width), F32), shaped((rows // 2, width), BF))
    return run(merge_kernel, "merge", outputs, (scal, keep, got), 0.7, mebibytes=8, lazy=lazy)


def resid_kernel(scal, mine_ref, got_ref, h_ref, dy_ref, vec_ref, dh_ref, dp_ref, sums_ref):
    grad = mine_ref[...] + got_ref[...].astype(F32)
    hat, inverse = normalize(h_ref[...])
    dy = dy_ref[...].astype(F32)
    grad_resid = dy + norm_back(hat, inverse, vec_ref[5:6, :], grad)
    dh_ref[...] = grad_resid
    low = grad_resid.astype(BF)
    dp_ref[...] = low
    sums_ref[...] = jnp.zeros_like(sums_ref)
    sums_ref[0:1, :] = jnp.sum(low.astype(F32), axis=0, keepdims=True)
    sums_ref[1:2, :] = jnp.sum(dy, axis=0, keepdims=True)


def resid_back(scal, mine, got, resid, cotangent, vec):
    rows, width = mine.shape
    outputs = (shaped((rows, width), F32), shaped((rows, width), BF), shaped((8, width), F32))
    return run(resid_kernel, "resid_back", outputs, (scal, mine, got, resid, cotangent, vec), 0.8)


def mixed_kernel(cols, scal, *refs, ready):
    grads, (o_ref, rows_ref, do_ref, g_ref, all_ref, own_ref) = refs[0:4], refs[4:10]
    place_members(scal, grads, all_ref)
    do_ref[...] = dot_cols(all_ref[...], rows_ref[...]).astype(BF)
    for index in range(GROUPS):

        @pl.when(scal[0] == index)
        def _():
            own_ref[...] = all_ref[:, index * cols : (index + 1) * cols]

    ready(5)
    g_ref[...] = dot_rows(o_ref[...], own_ref[...]).astype(BF)


def mixed_back(scal, grads, mixed, w_rows):
    cols, width = w_rows.shape
    length = mixed.shape[0]
    return run(
        functools.partial(mixed_kernel, cols),
        "mixed_back",
        (shaped((length, cols), BF), shaped((width, cols), BF)),
        (scal, *grads, mixed, w_rows),
        2.5,
        [pltpu.VMEM((length, width), BF), pltpu.VMEM((length, cols), BF)],
        lazy=(5, 6),
        late=(5,),
    )


def attend_back_kernel(
    per, scal, ranges, q_ref, k_ref, v_ref, do_ref, seg_row_ref, seg_col_ref, *refs, ready
):
    out_ref, k_acc, v_acc = refs[-3:]
    cols = q_ref.shape[1]
    block = 256
    length = k_ref.shape[0]
    k_acc[...] = jnp.zeros_like(k_acc)
    v_acc[...] = jnp.zeros_like(v_acc)
    for position in (2, 3, 4, 7):
        ready(position)

    def step(i, carry):
        start = pl.multiple_of(i * block, block)
        rows = pl.ds(start, block)

        def body(key_start, size):
            window = pl.ds(key_start, size)
            keys, values = k_ref[window, :], v_ref[window, :]
            same = seg_col_ref[window, :] == seg_row_ref[:, rows]
            queries = q_ref[rows, :] * jnp.asarray(HEAD_DIM**-0.5, BF)
            grads = do_ref[rows, :]

            def one(head, carry):
                grad_query, grad_key, grad_value = carry
                lanes = head_lanes(head, queries.shape)
                query = jnp.where(lanes, queries, jnp.zeros_like(queries))
                grad = jnp.where(lanes, grads, jnp.zeros_like(grads))
                score = jnp.where(same, dot_cols(keys, query), masked_score)
                largest = jnp.max(score, axis=0, keepdims=True)
                power = jnp.exp(score - largest)
                total = jnp.sum(power, axis=0, keepdims=True)
                chance = power * (1.0 / total)
                grad_chance = dot_cols(values, grad)
                inner = jnp.sum(chance * grad_chance, axis=0, keepdims=True)
                grad_score = (chance * (grad_chance - inner)).astype(BF)
                return (
                    jnp.where(lanes, dot_rows(grad_score, keys), grad_query),
                    grad_key + dot(grad_score, query),
                    grad_value + dot(chance.astype(BF), grad),
                )

            zeros = jnp.zeros(keys.shape, F32)
            grad_query, grad_key, grad_value = each_head(
                per, size, one, (jnp.zeros(queries.shape, F32), zeros, zeros)
            )
            k_acc[window, :] += grad_key
            v_acc[window, :] += grad_value
            out_ref[rows, :cols] = (grad_query * HEAD_DIM**-0.5).astype(BF)

        each_window(ranges, i, length, body)
        return carry

    lax.fori_loop(0, q_ref.shape[0] // block, step, 0)
    out_ref[:, cols : 2 * cols] = k_acc[...].astype(BF)
    out_ref[:, 2 * cols :] = v_acc[...].astype(BF)


def attend_back(scal, ranges, queries, keys, values, grad_out, seg_row, seg_col, per, kept):
    length, cols = queries.shape
    wide = pltpu.VMEM(queries.shape, F32)
    inputs = (scal, ranges, queries, keys, values, grad_out, seg_row, seg_col, *kept)
    return run(
        functools.partial(attend_back_kernel, per),
        "attend_back",
        shaped((length, 3 * cols), BF),
        inputs,
        16.0,
        [wide, wide],
        lazy=(2, 3, 4, 7),
        late=(2, 3, 4, 7),
        save=range(8, len(inputs)),
        scalars=2,
    )


def table_kernel(scal, forward_ref, resid_ref, table_ref, rows_ref):
    rows_ref[...] = jnp.zeros_like(rows_ref)
    rows_ref[4:5, :] = resid_ref[0:1, :]
    rows_ref[5:7, :] = forward_ref[0:2, :]
    rows_ref[7:8, :] = resid_ref[1:2, :]
    rows_ref[pl.ds(8 + scal[0], 1), :] = forward_ref[2:3, :]
    rest = rows_ref[...]
    unit = unit_rows(16, 128)
    table = jnp.zeros(table_ref.shape, F32)
    for _ in range(3):
        high = rest.astype(BF)
        rest = rest - high.astype(F32)
        table += dot_rows(high, unit)
    table_ref[...] = table


def vector_table(scal, sums_forward, sums_resid):
    width = sums_resid.shape[1]
    return run(
        table_kernel,
        "vector_table",
        shaped((width, 128), F32),
        (scal, sums_forward, sums_resid),
        1.0,
        [pltpu.VMEM((16, width), F32)],
        mebibytes=8,
        lazy=(1,),
    )


TERMS = 8


def vector_places(count, rows, width):
    each = width // rows
    return [(i // each, (i % each) * rows) for i in range(2 * count)]


def query_grads_kernel(cols, count, ringed, scal, *refs, ready):
    a_ref, hat_ref, out_ref, grad_ref, w_ref, table_ref, g_ref = refs
    width = a_ref.shape[1]
    owners = len(RING)
    rows = width // owners
    block = 4 * rows if ringed else 256
    ready(1)

    def place(first):
        if not ringed:
            return slice(first, first + block)
        owner = first // rows
        return slice(first + TERMS * owner, first + TERMS * owner + rows)

    for first in range(0, width, block):
        total = dot_rows(a_ref[:, first : first + block], grad_ref[...]).astype(BF)
        if not ringed:
            g_ref[place(first), : 3 * cols] = total
        else:
            for i in range(4):
                g_ref[place(first + i * rows), : 3 * cols] = total[i * rows : (i + 1) * rows, :]
    row = lax.broadcasted_iota(jnp.int32, (8, 3 * cols), 0)
    rest = dot_rows(jnp.ones((a_ref.shape[0], 8), BF), grad_ref[...])
    terms = jnp.zeros((8, 3 * cols), F32)
    for term in range(3):
        high = rest.astype(BF).astype(F32)
        terms = jnp.where(row == term, high, terms)
        rest = rest - high
    terms = terms.astype(BF)
    for position in (2, 3, 5, 6):
        ready(position)
    chunk = 256
    lane = lax.broadcasted_iota(jnp.int32, (chunk, 128), 1)

    def vectors(i, carry):
        lanes = pl.ds(pl.multiple_of(i * chunk, chunk), chunk)
        weight = w_ref[lanes, :]
        product = dot_rows(hat_ref[:, lanes], grad_ref[...]) * weight.astype(F32)
        gain = jnp.sum(product, axis=1, keepdims=True)
        shift = jnp.sum(dot_cols(weight, terms), axis=1, keepdims=True)
        table = jnp.where(lane == 0, gain, table_ref[lanes, :])
        table_ref[lanes, :] = jnp.where(lane == 1, shift, table)
        return carry

    lax.fori_loop(0, width // chunk, vectors, 0)
    own = pl.ds(pl.multiple_of(scal[0] * cols, cols), cols)
    bias = table_ref[own, :]
    near = lax.broadcasted_iota(jnp.int32, (cols, 128), 1)
    ones = jnp.ones((8, 8), BF)
    for i, column in ((0, 2), (2, 3)):
        part = dot_rows(terms[:, i * cols : (i + 1) * cols], ones)
        bias = jnp.where(near == column, part[:, 0:1], bias)
    table_ref[own, :] = bias
    total = table_ref[...]
    high = total.astype(BF)
    low = (total - high.astype(F32)).astype(BF)
    if not ringed:
        g_ref[:, 3 * cols : 4 * cols] = out_ref[...]
        g_ref[:, 4 * cols : 4 * cols + 16] = high[:, 0:16]
        g_ref[:, 4 * cols + 16 : 4 * cols + 32] = low[:, 0:16]
        g_ref[:, 4 * cols + 32 :] = jnp.zeros((width, 96), BF)
        return
    unit = unit_rows(16, 128)
    lines = (dot_cols(unit, high), dot_cols(unit, low))
    places = vector_places(count, rows, width)
    for owner in range(owners):
        first = owner * rows
        g_ref[place(first), 3 * cols :] = out_ref[first : first + rows, :]
        base = first + TERMS * owner + rows
        g_ref[base : base + TERMS, :] = jnp.zeros((TERMS, width), BF)
        for i, (line, start) in enumerate(places):
            piece = lines[i // count][i % count : i % count + 1, first : first + rows]
            g_ref[base + line : base + line + 1, start : start + rows] = piece.astype(BF)


def query_grads(scal, normed, hat, grad_out, grad, weights, table, count, ringed):
    width, cols = grad_out.shape
    shape = (width, 4 * cols + 128)
    if ringed:
        shape = (width + TERMS * len(RING), 4 * cols)
    return run(
        functools.partial(query_grads_kernel, cols, count, ringed),
        "query_grads",
        shaped(shape, BF),
        (scal, normed, hat, grad_out, grad, weights, table),
        4.0,
        lazy=(1, 2, 3, 5, 6),
        late=(1, 2, 3, 5, 6),
        far=(0,),
    )


def project_back_kernel(scal, grad_ref, w_ref, keep_ref, send_ref):
    block = grad_ref.shape[0] // GROUPS

    def step(i, carry):
        rows = pl.ds(pl.multiple_of(i * block, block), block)
        split_store(scal[0], i, dot_cols(grad_ref[rows, :], w_ref[...]), keep_ref, send_ref)
        return carry

    lax.fori_loop(0, GROUPS, step, 0)


def project_back(scal, grad, weights):
    rows, width = grad.shape[0] // 2, weights.shape[0]
    return run(
        project_back_kernel,
        "project_back",
        (shaped((rows, width), F32), shaped((rows, width), BF)),
        (scal, grad, weights),
        3.0,
        lazy=(2,),
    )


def input_kernel(scal, mine_ref, got_ref, x_ref, dh_ref, vec_ref, out_ref):
    grad = mine_ref[...] + got_ref[...].astype(F32)
    hat, inverse = normalize(x_ref[...].astype(F32))
    out_ref[...] = dh_ref[...] + norm_back(hat, inverse, vec_ref[0:1, :], grad)


def input_back(scal, mine, got, tokens, grad_resid, vec):
    inputs = (scal, mine, got, tokens, grad_resid, vec)
    return run(input_kernel, "input_back", shaped(mine.shape, F32), inputs, 1.0, lazy=(2, 3, 4, 5))


def output_kernel(scal, mine_ref, got_ref, h_ref, vec_ref, out_ref):
    branch = mine_ref[...] + got_ref[...].astype(F32) + vec_ref[7:8, :]
    out_ref[...] = (h_ref[...] + branch).astype(BF)


def output_sum(scal, mine, got, resid, vec):
    inputs = (scal, mine, got, resid, vec)
    return run(output_kernel, "output_sum", shaped(mine.shape, BF), inputs, 0.8, lazy=(2, 3, 4))


def owned_kernel(scal, in_ref, low_ref):
    total = in_ref[0].astype(F32)
    for i in range(1, in_ref.shape[0]):
        total += in_ref[i].astype(F32)
    low_ref[...] = total.astype(BF)


def owned_sum(scal, pieces):
    outputs = shaped(pieces.shape[1:], BF)
    return run(owned_kernel, "owned_sum", outputs, (scal, pieces), 1.5, lazy=(1,))


def squares_kernel(scal, *refs):
    sums = []
    for piece in refs[:4]:
        wide = piece[...].astype(F32)
        sums.append(jnp.sum(wide * wide))
    total = (sums[0] + sums[1]) + (sums[2] + sums[3])
    refs[4][...] = jnp.full(refs[4].shape, total, F32)


def squares_of(scal, pieces):
    outputs = shaped((8, 128), F32)
    return run(squares_kernel, "squares_of", outputs, (scal, *pieces), 1.0, save=range(1, 5))


def owned_vector_kernel(cols, ringed, scal, in_ref, low_ref):
    total = in_ref[0].astype(F32)
    for i in range(1, in_ref.shape[0]):
        total += in_ref[i].astype(F32)
    if ringed:
        rows = total.shape[0] - TERMS
        low_ref[:rows, :] = total[:rows, :].astype(BF)
        vector = total[rows:, :]
        high = vector.astype(BF).astype(F32)
        line = lax.broadcasted_iota(jnp.int32, vector.shape, 0)
        rest = pltpu.roll(vector - high, 3, 0)
        low_ref[rows:, :] = jnp.where(line < 3, high, rest).astype(BF)
        return
    low_ref[:, : 4 * cols] = total[:, : 4 * cols].astype(BF)
    vector = total[:, 4 * cols :]
    high = vector.astype(BF).astype(F32)
    lane = lax.broadcasted_iota(jnp.int32, vector.shape, 1)
    rest = pltpu.roll(vector - high, 32, 1)
    low_ref[:, 4 * cols :] = jnp.where(lane < 32, high, rest).astype(BF)


def owned_vector(scal, pieces, cols, ringed):
    return run(
        functools.partial(owned_vector_kernel, cols, ringed),
        "owned_vector",
        shaped(pieces.shape[1:], BF),
        (scal, pieces),
        1.5,
    )


def vector_sum(pieces, cols, count, ringed, held):
    if ringed:
        rows, width = pieces[0].shape
        rows -= TERMS
        parts = [piece[rows:, :].astype(F32) for piece in pieces]
        lines = (parts[0] + parts[1]) + (parts[2] + parts[3])
        lines = lines + pltpu.roll(lines, TERMS - 3, 0)
        places = vector_places(count, rows, width)
        for i in range(count):
            total = jnp.zeros((1, rows), F32)
            for line, start in (places[i], places[i + count]):
                total += lines[line : line + 1, start : start + rows]
            held[i : i + 1, :] = total
        return held[...]
    parts = [piece[:, 4 * cols :].astype(F32) for piece in pieces]
    table = (parts[0] + parts[1]) + (parts[2] + parts[3])
    rows = lax.broadcasted_iota(jnp.int32, (16, 128), 0)
    lanes = lax.broadcasted_iota(jnp.int32, (16, 128), 1)
    unit = jnp.where((lanes % 16 == rows) & (lanes < 64), 1.0, 0.0)
    return lax.dot_general(
        unit,
        table,
        (((1,), (1,)), ((), ())),
        preferred_element_type=F32,
        precision=lax.Precision.HIGHEST,
    )[:count]


def join_kernel(cols, count, ringed, scal, *refs):
    pieces, forward_ref, squares_ref, held = refs[0:4], refs[4], refs[5], refs[6]
    rows = held.shape[1]
    sums = []
    for piece in pieces:
        wide = piece[:rows, : 4 * cols].astype(F32)
        sums.append(wide * wide)
    vector = vector_sum(pieces, cols, count, ringed, held)
    total = jnp.sum((sums[0] + sums[1]) + (sums[2] + sums[3])) + jnp.sum(vector * vector)
    total = forward_ref[...] + total
    for i in range(squares_ref.shape[0] // 8):
        squares_ref[8 * i : 8 * i + 8, :] = total


def join(scal, pieces, squares, shape, cols, owners, ringed):
    return run(
        functools.partial(join_kernel, cols, shape[0], ringed),
        "join",
        shaped((8 * owners, 128), F32),
        (scal, *pieces, squares),
        1.5,
        [pltpu.VMEM(shape, F32)],
    )


def clip_factor(total_ref):
    total = total_ref[0]
    for i in range(1, total_ref.shape[0]):
        total += total_ref[i]
    norm = jnp.sqrt(total[0:1, 0:1])
    return norm, jnp.minimum(1.0, clip_limit / (norm + 1e-06))


def adam_kernel(counts, cols, ringed, scal, total_ref, *refs):
    attention, refs = refs[0:4], refs[4:]
    pieces, sources, targets, norm_ref = refs[0:4], refs[4:16], refs[16:31], refs[31]
    held, copies = refs[32:44], refs[44:47]
    loads, stores = refs[47:50], refs[50:53]
    grads, grad_loads, attention_ref, vector_ref = refs[53:57], refs[57], refs[58], refs[59]
    norm, factor = clip_factor(total_ref)
    norm_ref[...] = jnp.broadcast_to(norm, norm_ref.shape)
    decays = (weight_decay, weight_decay, 0.0)

    def chunk(kind, i):
        if counts[kind] == 1:
            return (slice(None), slice(None))
        size = held[4 * kind].shape[1] // counts[kind]
        return (slice(None), pl.ds(pl.multiple_of(i * size, size), size))

    def load(kind, i, state):
        place = chunk(kind, i)
        number = 4 * kind + state
        return pltpu.make_async_copy(
            sources[number].at[place], held[number].at[place], loads[kind].at[i, state]
        )

    def store(kind, i, state):
        place = chunk(kind, i)
        source = held[4 * kind + state] if state < 4 else copies[kind]
        return pltpu.make_async_copy(
            source.at[place], targets[3 * state + kind].at[place], stores[kind].at[i, state]
        )

    def every(kind, action):
        def step(i, carry):
            action(kind, i)
            return carry

        lax.fori_loop(0, counts[kind], step, 0)

    def start(kind, i):
        for state in range(4):
            load(kind, i, state).start()

    def work(kind, i):
        for state in range(4):
            load(kind, i, state).wait()
        place = chunk(kind, i)
        if kind == 0:
            gradient = attention_ref[place].astype(F32)
        elif kind == 2:
            gradient = vector_sum(attention, cols, held[8].shape[0], ringed, vector_ref)
        else:
            size = held[4].shape[1] // counts[1]
            half = pl.ds(pl.multiple_of((i // GROUPS) * size, size), size)
            source = scal[0] ^ (i % GROUPS)
            gradient = grads[0][:, half]
            for k in range(1, GROUPS):
                gradient = jnp.where(source == k, grads[k][:, half], gradient)
            gradient = gradient.astype(F32)
        results = adam_update(
            *[held[4 * kind + state][place] for state in range(4)], gradient, factor, decays[kind]
        )
        for state, value in zip((0, 1, 2, 3), results):
            held[4 * kind + state][place] = value
        copies[kind][place] = results[0].astype(BF)
        for state in range(5):
            store(kind, i, state).start()

    def finish(kind, i):
        for state in range(5):
            store(kind, i, state).wait()

    moves = [
        pltpu.make_async_copy(piece, grad, grad_loads.at[i])
        for i, (piece, grad) in enumerate(zip(pieces, grads))
    ]
    for move in moves:
        move.start()
    for kind in (1, 0, 2):
        every(kind, start)
    width = attention_ref.shape[1] // 4
    for member in range(GROUPS):

        @pl.when(scal[0] == member)
        def _():
            for i in range(4):
                for k in range(GROUPS):
                    first = i * width + (member ^ k) * cols
                    attention_ref[:, first : first + cols] = attention[k][
                        : held[0].shape[0], i * cols : (i + 1) * cols
                    ]

    for move in moves:
        move.wait()
    for kind in (1, 0, 2):
        every(kind, work)
    for kind in (1, 0, 2):
        every(kind, finish)


def adam(scal, totals, attention_grads, forward_grads_by_member, states, cols, ringed):
    counts = (4, 2 * GROUPS, 1)
    kinds = [states[4 * kind].shape for kind in range(3)]
    out_shape = [pltpu.HBM(shape, F32) for _ in range(4) for shape in kinds]
    out_shape += [pltpu.HBM(shape, BF) for shape in kinds]
    out_shape += [shaped((8, 128), F32)]
    return pl.pallas_call(
        functools.partial(adam_kernel, counts, cols, ringed),
        out_shape=out_shape,
        in_specs=[smem()] + [vmem()] * 5 + [far_space()] * 16,
        out_specs=[far_space()] * 15 + [vmem()],
        scratch_shapes=[pltpu.VMEM(kinds[kind], F32) for kind in range(3) for _ in range(4)]
        + [pltpu.VMEM(shape, BF) for shape in kinds]
        + [pltpu.SemaphoreType.DMA((count, 4)) for count in counts]
        + [pltpu.SemaphoreType.DMA((count, 5)) for count in counts]
        + [pltpu.VMEM(item.shape, item.dtype) for item in forward_grads_by_member]
        + [pltpu.SemaphoreType.DMA((GROUPS,))]
        + [pltpu.VMEM(kinds[0], BF), pltpu.VMEM(kinds[2], F32)],
        compiler_params=params(32),
        cost_estimate=cost(9.0),
        name="adam",
    )(scal, totals, *attention_grads, *map(pin, forward_grads_by_member), *map(pin, states))


def adam_update(master, moment, second, teacher, gradient, factor, decay_rate):
    clipped = gradient * factor
    moment_new = beta_one * moment + (1.0 - beta_one) * clipped
    second_new = beta_two * second + (1.0 - beta_two) * clipped * clipped
    scale_one = 1.0 - beta_one**ADAM_STEP
    scale_two = 1.0 - beta_two**ADAM_STEP
    update = (moment_new * (1.0 / scale_one)) / (
        jnp.sqrt(second_new * (1.0 / scale_two)) + adam_epsilon
    )
    master_new = master * (1.0 - learn_rate * decay_rate) - learn_rate * update
    teacher_new = teacher_keep * teacher + (1.0 - teacher_keep) * master_new
    return (master_new, moment_new, second_new, teacher_new)


def swap(part, bit):
    return lax.ppermute(part, "head", [(i, i ^ bit) for i in range(4)])


def spread(part, *others):
    across = swap(part, 2)
    if others:
        return [
            part,
            swap(after(part, *others), 1),
            across,
            swap(after(across, *others), 1),
        ]
    return [part, swap(part, 1), across, swap(across, 1)]


RING = (0, 2, 4, 6, 7, 5, 3, 1)


def ring_owners(count):
    if count != len(RING):
        return np.zeros((count, 1), np.int32)
    table = []
    for device in range(count):
        place = RING.index(device)
        owners = [device]
        for hop in range(1, count // 2 + 1):
            owners.append(RING[(place - hop) % count])
            owners.append(RING[(place + hop) % count])
        table.append(owners)
    return np.asarray(table, np.int32)


def after(value, *others):
    return lax.optimization_barrier((value, *others))[0]


class Ring:
    def __init__(self, block, count, halved=False):
        self.count = count
        self.halved = halved
        self.ringed = count == len(RING)
        self.hops = count // 2 if self.ringed else 1
        self.front = self.rear = block
        self.pieces = [block]
        self.done = 0

    def send(self, array, distance):
        count = self.count
        pairs = [(RING[i], RING[(i + distance) % count]) for i in range(count)]
        return lax.ppermute(array, "dp", pairs)

    def hop(self, *others):
        self.done += 1
        if not self.ringed:
            self.pieces = [lax.all_gather(after(self.front, *others), "dp", axis=0, tiled=True)]
            return self
        if self.done > 1 or others:
            self.front, self.rear = lax.optimization_barrier((self.front, self.rear, *others))[:2]
        if self.done == self.hops and self.halved:
            half = self.front.shape[0] // 2
            self.front, self.rear = self.front[:half], self.rear[half:]
        self.front = self.send(self.front, 1)
        self.pieces.append(self.front)
        if self.done < self.hops or self.halved:
            self.rear = self.send(self.rear, -1)
            self.pieces.append(self.rear)
        return self

    def rest(self):
        while self.done < self.hops:
            self.hop()
        return self.pieces


def exchange_owned(grads, count):
    blocks = grads.reshape(count, -1, grads.shape[1])
    return lax.all_to_all(blocks, "dp", split_axis=0, concat_axis=0)


def local(
    tokens,
    cotangent,
    segments,
    attention_master,
    feedforward_master,
    vector_master,
    attention_moment,
    feedforward_moment,
    vector_moment,
    attention_second,
    feedforward_second,
    vector_second,
    attention_teacher,
    feedforward_teacher,
    vector_teacher,
):
    width = tokens.shape[1]
    owners = lax.axis_size("dp")
    groups = lax.axis_size("head")
    hidden = feedforward_master.shape[1] // 2
    per = HEADS // groups
    cols = per * HEAD_DIM
    part = hidden // groups

    owner_table = ring_owners(owners)
    table = np.concatenate(
        [
            np.tile(np.arange(groups, dtype=np.int32), owners)[:, None],
            np.repeat(owner_table, groups, axis=0),
        ],
        axis=1,
    )
    place = lax.axis_index("dp") * groups + lax.axis_index("head")
    scal = lax.dynamic_index_in_dim(jnp.asarray(table), place, 0, keepdims=False)
    first = Ring(pack_attention(scal, attention_master, vector_master, cols), owners)
    ringed = owners == len(RING)
    first.hop()
    if ringed:
        first.hop()
    seg_col, ranges = read_segments(scal, after(segments, *first.pieces[-2:]))
    if ringed:
        first.hop().hop(seg_col)
    early = first.pieces[-3:-1] if ringed else first.pieces
    token_across, grad_across = swap(tokens, 2), swap(cotangent, 2)
    token, token_across = lax.optimization_barrier((tokens, token_across, *early))[:2]
    x_all = place_blocks(scal, [token, swap(token, 1), token_across, swap(token_across, 1)])
    second = Ring(pack_forward(scal, feedforward_master, part), owners)
    second.hop(first.pieces[-1])

    queries, keys, values, w_qkv, w_o, vec, normed, hat = project(
        scal, x_all, first.pieces, cols
    )
    half = x_all.shape[0] // 2
    w_across = swap(w_o, 2)
    mixed_low, *kept = attend(
        scal,
        ranges,
        after(queries, grad_across),
        keys,
        values,
        segments,
        seg_col,
        per,
        0,
        half,
        (w_qkv, vec, normed, hat),
    )
    far_q, far_k, far_v, far_col, far_weights, far_vec, *far_normed = kept
    low_across = swap(mixed_low, 2)
    w_across = after(w_across, mixed_low)
    if ringed:
        second.hop(mixed_low)
    mixed_high = attend(
        scal, ranges, after(queries, w_across), keys, values, segments, seg_col, per, half, half
    )
    if ringed:
        second.hop(mixed_high)
    high_across = swap(mixed_high, 2)
    w_across, low_across, w_o, mixed_low, grad, grad_across = lax.optimization_barrier(
        (w_across, low_across, w_o, mixed_low, cotangent, grad_across, high_across)
    )[:6]
    dy_all = place_blocks(scal, [grad, swap(grad, 1), grad_across, swap(grad_across, 1)])
    w_out = [w_o, swap(w_o, 1), w_across, swap(w_across, 1)]
    mixed = [
        (mixed_low, mixed_high),
        (swap(mixed_low, 1), swap(mixed_high, 1)),
        (low_across, high_across),
        (swap(low_across, 1), swap(high_across, 1)),
    ]
    (
        normed_two,
        active,
        grad_pre,
        keep,
        send,
        resid,
        w_ff,
        w_rows,
        sums_forward,
        mixed_all,
    ) = forward_back(scal, x_all, dy_all, mixed, w_out, second.rest(), vec, cols)
    grad_ff, far_active, *kept = forward_grads(
        scal,
        normed_two,
        active,
        grad_pre,
        dy_all,
        (resid, sums_forward, w_rows, w_ff, mixed_all),
    )
    far_resid, far_sums, far_rows, far_ff, far_mixed = kept
    got = swap(send, 1)
    grad_ff, got = lax.optimization_barrier((grad_ff, got))
    owned_ff = exchange_owned(grad_ff, owners)
    mine, send = merge(scal, keep, got)
    keep_branch, send_branch, cot_own = branch_part(
        scal, far_active, after(far_ff, send), cotangent
    )
    got = swap(send, 2)
    grad_resid, grad_low, sums_resid = resid_back(
        scal, after(mine, send_branch), got, resid, cot_own, vec
    )
    low_across = swap(grad_low, 2)
    mine, send = merge(
        scal, keep_branch, swap(after(send_branch, grad_low), 1), lazy=(1,)
    )
    table = vector_table(scal, far_sums, sums_resid)
    low_across = after(low_across, send, table)
    low_blocks = [grad_low, swap(grad_low, 1), low_across, swap(low_across, 1)]
    grad_mixed, grad_out = mixed_back(scal, low_blocks, far_mixed, far_rows)
    grad_qkv, far_dh, far_table, far_grad_out = attend_back(
        scal,
        ranges,
        far_q,
        far_k,
        far_v,
        grad_mixed,
        segments,
        far_col,
        per,
        (grad_resid, table, grad_out),
    )
    got_branch = swap(after(send, grad_mixed), 2)
    pack = query_grads(
        scal,
        after(far_normed[0], got_branch),
        far_normed[1],
        far_grad_out,
        grad_qkv,
        far_weights,
        far_table,
        vector_master.shape[0],
        ringed,
    )
    owned_pack = exchange_owned(pack, owners)
    forward_parts = spread(owned_sum(scal, after(owned_ff, pack)))
    forward_squares, *forward_parts = squares_of(scal, forward_parts)
    keep, send = project_back(scal, grad_qkv, after(far_weights, pack))
    mine_input, send = merge(scal, keep, swap(send, 1))
    block_output = output_sum(scal, after(mine, pack), got_branch, far_resid, far_vec)
    got_input = swap(send, 2)
    owned_pack = after(owned_pack, forward_squares, got_input, block_output)
    input_gradient = input_back(scal, mine_input, got_input, tokens, far_dh, far_vec)
    attention_parts = spread(owned_vector(scal, owned_pack, cols, ringed))
    squares = join(
        scal, attention_parts, forward_squares, vector_master.shape, cols, owners, ringed
    )
    totals = lax.all_to_all(
        squares.reshape(owners, 8, 128), "dp", split_axis=0, concat_axis=0
    )
    *results, norm = adam(
        scal,
        totals,
        attention_parts,
        forward_parts,
        (
            attention_master,
            attention_moment,
            attention_second,
            attention_teacher,
            feedforward_master,
            feedforward_moment,
            feedforward_second,
            feedforward_teacher,
            vector_master,
            vector_moment,
            vector_second,
            vector_teacher,
        ),
        cols,
        ringed,
    )
    return (block_output, input_gradient, norm[0, 0], *results)


def solution(mesh):
    rows = P(("dp", "head"), None)
    shard = P("dp", None)
    vector = P(None, "dp")
    return jax.shard_map(
        local,
        mesh=mesh,
        in_specs=(rows, rows, shard) + (shard, shard, vector) * 4,
        out_specs=(rows, rows, P()) + (shard, shard, vector) * 5,
        check_vma=False,
    )
```

```python
import functools

import jax
import jax.numpy as jnp
import numpy as np
from jax import lax
from jax.experimental import pallas as pl
from jax.experimental.pallas import tpu as pltpu
from jax.sharding import PartitionSpec as P

HEADS = 12
HEAD_DIM = 64
ADAM_STEP = 3

norm_epsilon = 1e-06
beta_one = 0.5
beta_two = 0.5
adam_epsilon = 1e-08
learn_rate = 0.05
weight_decay = 0.05
teacher_keep = 0.8
clip_limit = 1.0
masked_score = -1e30

BF = jnp.bfloat16
F32 = jnp.float32


def dot_rows(left, right):
    return lax.dot_general(left, right, (((0,), (0,)), ((), ())), preferred_element_type=F32)


def dot_cols(left, right):
    return lax.dot_general(left, right, (((1,), (1,)), ((), ())), preferred_element_type=F32)


def dot(left, right):
    return jnp.dot(left, right, preferred_element_type=F32)


def normalize(values):
    center = jnp.mean(values, axis=-1, keepdims=True)
    deviate = values - center
    spread = jnp.mean(deviate * deviate, axis=-1, keepdims=True)
    inverse = lax.rsqrt(spread + norm_epsilon)
    return deviate * inverse, inverse


def norm_back(hat, inverse, gain, grad):
    scaled = grad * gain
    mean_one = jnp.mean(scaled, axis=-1, keepdims=True)
    mean_two = jnp.mean(scaled * hat, axis=-1, keepdims=True)
    return inverse * (scaled - mean_one - hat * mean_two)


def head_lanes(index, shape):
    lane = lax.broadcasted_iota(jnp.int32, shape, 1)
    return (lane >= index * HEAD_DIM) & (lane < (index + 1) * HEAD_DIM)


def unit_rows(rows, columns):
    row = lax.broadcasted_iota(jnp.int32, (rows, columns), 0)
    column = lax.broadcasted_iota(jnp.int32, (rows, columns), 1)
    return jnp.where(row == column, 1.0, 0.0).astype(BF)


def smem():
    return pl.BlockSpec(memory_space=pltpu.SMEM)


def vmem():
    return pl.BlockSpec(memory_space=pltpu.VMEM)


def whole(*shape):
    return pl.BlockSpec(shape, lambda *index: (0,) * len(shape))


def shaped(shape, kind):
    return jax.ShapeDtypeStruct(shape, kind)


def params(mebibytes):
    return pltpu.CompilerParams(vmem_limit_bytes=mebibytes * 2**20)


COST_SCALE = 1.0


def cost(microseconds):
    return pl.CostEstimate(
        flops=0, transcendentals=0, bytes_accessed=int(microseconds * COST_SCALE * 3.6e6)
    )


def pin(array):
    return pltpu.with_memory_space_constraint(array, pltpu.HBM)


def far_space():
    return pl.BlockSpec(memory_space=pltpu.HBM)


def run(
    kernel,
    name,
    outputs,
    inputs,
    microseconds,
    scratch=(),
    mebibytes=16,
    lazy=(),
    save=(),
    far=(),
    late=(),
    scalars=1,
    scalar_outputs=(),
):
    single = not isinstance(outputs, tuple)
    outputs = [outputs] if single else list(outputs)
    lazy, save, far = list(lazy), list(save), list(far)
    count, produced, own = len(inputs), len(outputs), len(scratch)
    buffers = [pltpu.VMEM(inputs[i].shape, inputs[i].dtype) for i in lazy]
    buffers += [pltpu.VMEM(outputs[i].shape, outputs[i].dtype) for i in far]
    moves = len(lazy) + len(save) + len(far)
    if moves:
        buffers.append(pltpu.SemaphoreType.DMA((moves,)))

    def body(*refs):
        items = list(refs[: count + produced])
        saved = refs[count + produced : count + produced + len(save)]
        rest = refs[count + produced + len(save) :]
        inner, extra = rest[:own], rest[own:]
        copies, number = [], 0
        for j, i in enumerate(lazy):
            copies.append(pltpu.make_async_copy(refs[i], extra[j], extra[-1].at[number]))
            items[i] = extra[j]
            number += 1
        stores = []
        for j, i in enumerate(save):
            stores.append(pltpu.make_async_copy(refs[i], saved[j], extra[-1].at[number]))
            number += 1
        last = []
        for j, i in enumerate(far):
            buffer = extra[len(lazy) + j]
            last.append(pltpu.make_async_copy(buffer, refs[count + i], extra[-1].at[number]))
            items[count + i] = buffer
            number += 1
        for copy in copies + stores:
            copy.start()
        for i, copy in zip(lazy, copies):
            if i not in late:
                copy.wait()
        if late:
            kernel(*items, *inner, ready=lambda i: copies[lazy.index(i)].wait())
        else:
            kernel(*items, *inner)
        for copy in last:
            copy.start()
        for copy in stores + last:
            copy.wait()

    shapes = [pltpu.HBM(item.shape, item.dtype) if i in far else item for i, item in enumerate(outputs)]
    results = pl.pallas_call(
        body,
        out_shape=shapes + [pltpu.HBM(inputs[i].shape, inputs[i].dtype) for i in save],
        in_specs=[smem()] * scalars
        + [far_space() if i in lazy else vmem() for i in range(scalars, count)],
        out_specs=[
            far_space() if i in far else smem() if i in scalar_outputs else vmem()
            for i in range(produced)
        ]
        + [far_space()] * len(save),
        scratch_shapes=list(scratch) + buffers,
        compiler_params=params(mebibytes),
        cost_estimate=cost(microseconds),
        name=name,
    )(*[pin(item) if i in lazy else item for i, item in enumerate(inputs)])
    return results[0] if single and not save else tuple(results)


GROUPS = 4


def pack_kernel(cols, scal, *refs):
    vector_ref, out_ref = refs[4:6]
    for side in range(2):

        @pl.when(scal[0] % 2 == side)
        def _():
            for i in range(4):
                out_ref[:, i * cols : (i + 1) * cols] = refs[i][
                    :, side * cols : (side + 1) * cols
                ].astype(BF)

    vector = vector_ref[...].astype(BF)
    out_ref[:, 4 * cols :] = dot_rows(vector, unit_rows(vector.shape[0], 128)).astype(BF)


def pack_attention(scal, attention, vector, cols):
    rows = attention.shape[0]

    def pair(i):
        return pl.BlockSpec((rows, 2 * cols), lambda step, scal: (0, 2 * i + scal[0] // 2))

    return pl.pallas_call(
        functools.partial(pack_kernel, cols),
        out_shape=shaped((rows, 4 * cols + 128), BF),
        grid_spec=pltpu.PrefetchScalarGridSpec(
            num_scalar_prefetch=1,
            grid=(1,),
            in_specs=[pair(i) for i in range(4)] + [whole(*vector.shape)],
            out_specs=whole(rows, 4 * cols + 128),
        ),
        compiler_params=params(8),
        cost_estimate=cost(1.5),
        name="pack_attention",
    )(scal, *[pin(attention)] * 4, pin(vector))


def cast_kernel(scal, in_ref, out_ref):
    out_ref[...] = in_ref[...].astype(BF)


def pack_forward(scal, forward, part):
    rows = forward.shape[0]
    return pl.pallas_call(
        cast_kernel,
        out_shape=shaped((rows, 2 * part), BF),
        grid_spec=pltpu.PrefetchScalarGridSpec(
            num_scalar_prefetch=1,
            grid=(2,),
            in_specs=[pl.BlockSpec((rows, part), lambda i, scal: (0, GROUPS * i + scal[0]))],
            out_specs=pl.BlockSpec((rows, part), lambda i, scal: (0, i)),
        ),
        compiler_params=params(8),
        cost_estimate=cost(1.5),
        name="pack_forward",
    )(scal, forward)


def place_rows(scal, pieces, target):
    rows = pieces[0].shape[0]
    if len(pieces) == 1:
        target[...] = pieces[0][...]
        return
    for i, piece in enumerate(pieces):
        size = piece.shape[0]
        first = rows - size if i == len(RING) else 0
        start = pl.multiple_of(scal[1 + i] * rows + first, size)
        target[pl.ds(start, size), :] = piece[...]


def place_members(scal, pieces, target):
    rows = pieces[0].shape[0]
    for i, piece in enumerate(pieces):
        start = pl.multiple_of((scal[0] ^ i) * rows, rows)
        target[pl.ds(start, rows), :] = piece[...]


def place_kernel(scal, *refs):
    place_members(scal, refs[0:4], refs[4])


def place_blocks(scal, blocks):
    rows, width = blocks[0].shape
    wide = shaped((GROUPS * rows, width), BF)
    return run(place_kernel, "place_blocks", wide, (scal, *blocks), 0.5, mebibytes=2)


def fold(value):
    rows, columns = value.shape
    count = 128 // (columns - 128)
    share = rows // count
    rest = [value[i * share : (i + 1) * share, 128:] for i in range(count)]
    return value[:, :128], jnp.concatenate(rest, axis=1)


def folded_rows(rows, columns):
    return rows + rows * (columns - 128) // 128


def segments_kernel(scal, seg_ref, col_ref, ranges_ref):
    numbers = seg_ref[...]
    key_ranges(numbers, ranges_ref)
    lines = jnp.broadcast_to(numbers.astype(F32), (8, numbers.shape[1])).astype(BF)
    col_ref[...] = dot_rows(lines, unit_rows(8, 128))[:, 0:1].astype(jnp.int32)


def read_segments(scal, segments):
    outputs = (shaped((segments.shape[1], 1), jnp.int32), shaped((16,), jnp.int32))
    inputs = (scal, segments)
    return run(
        segments_kernel, "read_segments", outputs, inputs, 1.0, mebibytes=4, scalar_outputs=(1,)
    )


def project_kernel(count, cols, scal, x_ref, *refs):
    pieces = refs[:count]
    q_ref, k_ref, v_ref, w_ref, wo_ref, vec_ref, a_ref, hat_ref = refs[count : 8 + count]
    weights, wq_ref, wk_ref, wv_ref = refs[8 + count : 12 + count]
    place_rows(scal, pieces, weights)
    for i, ref in enumerate((wq_ref, wk_ref, wv_ref)):
        ref[...] = weights[:, i * cols : (i + 1) * cols]
    w_ref[...] = weights[:, : 3 * cols]
    top, rest = fold(weights[:, 3 * cols : 4 * cols])
    wo_ref[: top.shape[0], :] = top
    wo_ref[top.shape[0] :, :] = rest
    unit = unit_rows(16, 128)
    vec_ref[...] = dot_cols(unit, weights[:, 4 * cols :])
    start = pl.multiple_of(scal[0] * cols, cols)
    own = dot_cols(unit, weights[pl.ds(start, cols), 4 * cols :])
    query_bias, value_bias = own[2:3, :], own[3:4, :]
    gain, shift = vec_ref[0:1, :], vec_ref[1:2, :]
    block = 256

    def step(i, carry):
        rows = pl.ds(pl.multiple_of(i * block, block), block)
        hat, _ = normalize(x_ref[rows, :].astype(F32))
        normed = (hat * gain + shift).astype(BF)
        a_ref[rows, :] = normed
        hat_ref[rows, :] = hat.astype(BF)
        q_ref[rows, :] = (dot(normed, wq_ref[...]) + query_bias).astype(BF)
        k_ref[rows, :] = dot(normed, wk_ref[...]).astype(BF)
        v_ref[rows, :] = (dot(normed, wv_ref[...]) + value_bias).astype(BF)
        return carry

    lax.fori_loop(0, x_ref.shape[0] // block, step, 0)


def project(scal, x_all, pieces, cols):
    length, width = x_all.shape
    outputs = (
        (shaped((length, cols), BF),) * 3
        + (shaped((width, 3 * cols), BF),)
        + (shaped((folded_rows(width, cols), 128), BF),)
        + (shaped((16, width), F32),)
        + (shaped((length, width), BF),) * 2
    )
    return run(
        functools.partial(project_kernel, len(pieces), cols),
        "project",
        outputs,
        (scal, x_all, *pieces),
        4.5,
        scratch=[pltpu.VMEM((width, 4 * cols + 128), BF)] + [pltpu.VMEM((width, cols), BF)] * 3,
    )


QUERIES = 256
WINDOWS = (512, 576)


def key_ranges(numbers, ranges_ref):
    length = numbers.shape[1]
    images = jnp.where(numbers < 0, length, numbers)
    place = lax.broadcasted_iota(jnp.int32, numbers.shape, 1)
    for block in range(length // QUERIES):
        first = jnp.max(jnp.where(place == block * QUERIES, images, 0))
        last = jnp.max(jnp.where(place == (block + 1) * QUERIES - 1, images, 0))
        ranges_ref[2 * block] = jnp.sum((images < first).astype(jnp.int32))
        ranges_ref[2 * block + 1] = jnp.sum((images <= last).astype(jnp.int32))


def each_window(ranges, block, length, body):
    low, high = ranges[2 * block], ranges[2 * block + 1]
    taken = jnp.bool_(False)
    for size in [size for size in WINDOWS if size < length] + [length]:
        start = (jnp.minimum(low, length - size) // 16) * 16
        fits = high - start <= size

        @pl.when(fits & jnp.logical_not(taken))
        def _():
            body(pl.multiple_of(start, 16), size)

        taken = taken | fits


def each_head(per, size, body, carry):
    if size > WINDOWS[0]:
        return lax.fori_loop(0, per, body, carry)
    for head in range(per):
        carry = body(head, carry)
    return carry


def attend_kernel(per, first, scal, ranges, q_ref, k_ref, v_ref, seg_row_ref, seg_col_ref, *refs):
    out_ref, held = refs[-2:]
    block = QUERIES
    length = k_ref.shape[0]

    def step(i, carry):
        start = pl.multiple_of(first + i * block, block)
        near = pl.ds(pl.multiple_of(i * block, block), block)

        def body(key_start, size):
            window = pl.ds(key_start, size)
            keys, values = k_ref[window, :], v_ref[window, :]
            numbers = seg_row_ref[...]
            if size < length:
                span = size - size % 128 + 256
                base = jnp.minimum(key_start // 128, (length - span) // 128) * 128
                numbers = seg_row_ref[:, pl.ds(pl.multiple_of(base, 128), span)]
                numbers = jnp.broadcast_to(numbers, (8, span))
                numbers = pltpu.roll(numbers, span - (key_start - base), 1)[0:1, :size]
            same = seg_col_ref[pl.ds(start, block), :] == numbers
            queries = q_ref[pl.ds(start, block), :] * jnp.asarray(HEAD_DIM**-0.5, BF)

            def one(head, result):
                lanes = head_lanes(head, queries.shape)
                score = dot_cols(jnp.where(lanes, queries, jnp.zeros_like(queries)), keys)
                score = jnp.where(same, score, masked_score)
                largest = jnp.max(score, axis=1, keepdims=True)
                power = jnp.exp(score - largest)
                total = jnp.sum(power, axis=1, keepdims=True)
                chance = (power * (1.0 / total)).astype(BF)
                return jnp.where(lanes, dot(chance, values), result)

            result = each_head(per, size, one, jnp.zeros(queries.shape, F32))
            held[near, :] = result.astype(BF)

        each_window(ranges, first // block + i, length, body)
        return carry

    lax.fori_loop(0, held.shape[0] // block, step, 0)
    top, rest = fold(held[...])
    out_ref[: top.shape[0], :] = top
    out_ref[top.shape[0] :, :] = rest


def attend(scal, ranges, queries, keys, values, seg_row, seg_col, per, first, count, kept=()):
    inputs = (scal, ranges, queries, keys, values, seg_row, seg_col, *kept)
    return run(
        functools.partial(attend_kernel, per, first),
        "attend",
        shaped((folded_rows(count, queries.shape[1]), 128), BF),
        inputs,
        7.0 * count / queries.shape[0],
        [pltpu.VMEM((count, queries.shape[1]), BF)],
        save=(2, 3, 4, 6, *range(7, len(inputs))) if kept else (),
        scalars=2,
    )


def forward_kernel(count, cols, parts, scal, x_ref, dy_ref, *refs):
    mixed, w_out = [refs[k * parts : (k + 1) * parts] for k in range(4)], refs[4 * parts :][:4]
    refs = refs[4 * parts + 4 :]
    pieces = refs[:count]
    vec_ref = refs[count]
    c_ref, u_ref, df_ref, keep_ref, send_ref, h_ref, w_ref, rows_ref, sums_ref, o_ref = refs[
        1 + count : 11 + count
    ]
    out_weight = refs[11 + count]
    member = scal[0]
    length, width = x_ref.shape
    part = w_ref.shape[1] // 2
    block = length // GROUPS
    narrow = cols - 128
    place_rows(scal, pieces, w_ref)

    def unfold(target, first, column, item):
        rows = item.shape[0] * 128 // cols
        share = rows * narrow // 128
        target[first : first + rows, column : column + 128] = item[:rows, :]
        for i in range(rows // share):
            start = first + i * share
            target[start : start + share, column + 128 : column + cols] = item[
                rows:, i * narrow : (i + 1) * narrow
            ]

    for index in range(GROUPS):

        @pl.when(member == index)
        def _():
            for k in range(GROUPS):
                column = (index ^ k) * cols
                unfold(out_weight, 0, column, w_out[k])
                for half in range(parts):
                    unfold(o_ref, half * (length // parts), column, mixed[k][half])

    rows_ref[...] = out_weight[pl.ds(pl.multiple_of(member * cols, cols), cols), :]
    zero = jnp.zeros((1, width), F32)
    up_bias = vec_ref[pl.ds(8 + member, 1), :]

    def run_block(step, carry):
        rows = pl.ds(pl.multiple_of(step * block, block), block)
        resid = x_ref[rows, :].astype(F32) + vec_ref[4:5, :] + dot(o_ref[rows, :], out_weight[...])

        @pl.when(step == member)
        def _():
            h_ref[...] = resid

        hat, _ = normalize(resid)
        normed = (hat * vec_ref[5:6, :] + vec_ref[6:7, :]).astype(BF)
        c_ref[rows, :] = normed
        pre = dot(normed, w_ref[:, :part]) + up_bias
        phi = 0.5 * (1.0 + lax.erf(pre * 0.7071067811865476))
        u_ref[rows, :] = (pre * phi).astype(BF)
        slope = phi + pre * (jnp.exp(-0.5 * pre * pre) * 0.3989422804014327)
        grad_pre = (dot(dy_ref[rows, :], w_ref[:, part:]) * slope).astype(BF)
        df_ref[rows, :] = grad_pre
        grad_normed = dot_cols(grad_pre, w_ref[:, :part])
        split_store(member, step, grad_normed, keep_ref, send_ref)
        return (
            carry[0] + jnp.sum(grad_normed * hat, axis=0, keepdims=True),
            carry[1] + jnp.sum(grad_normed, axis=0, keepdims=True),
            carry[2] + jnp.sum(grad_pre.astype(F32), axis=0, keepdims=True),
        )

    carry = lax.fori_loop(0, GROUPS, run_block, (zero, zero, zero))
    sums_ref[...] = jnp.zeros_like(sums_ref)
    for i in range(3):
        sums_ref[i : i + 1, :] = carry[i]


def split_store(member, index, value, keep_ref, send_ref):
    mine = (index % 2) == (member % 2)
    rows = value.shape[0]
    place = pl.ds(pl.multiple_of((index // 2) * rows, rows), rows)

    @pl.when(mine)
    def _():
        keep_ref[place, :] = value

    @pl.when(jnp.logical_not(mine))
    def _():
        send_ref[place, :] = value.astype(BF)


def forward_back(scal, x_all, dy_all, mixed, w_out, pieces, vec, cols):
    length, width = x_all.shape
    part = pieces[0].shape[1] // 2
    rows = length // GROUPS
    outputs = (
        shaped((length, width), BF),
        shaped((length, part), BF),
        shaped((length, part), BF),
        shaped((2 * rows, width), F32),
        shaped((2 * rows, width), BF),
        shaped((rows, width), F32),
        shaped((width, 2 * part), BF),
        shaped((cols, width), BF),
        shaped((8, width), F32),
        shaped((length, width), BF),
    )
    flat = [item for items in mixed for item in items]
    return run(
        functools.partial(forward_kernel, len(pieces), cols, len(mixed[0])),
        "forward_back",
        outputs,
        (scal, x_all, dy_all, *flat, *w_out, *pieces, vec),
        13.0,
        [pltpu.VMEM((width, width), BF)],
    )


def forward_grads_kernel(scal, c_ref, u_ref, df_ref, dy_ref, *refs):
    g_ref = refs[-1]
    part = u_ref.shape[1]
    third = c_ref.shape[1] // 3

    def weight(i, carry):
        lanes = pl.ds(pl.multiple_of(i * third, third), third)
        g_ref[lanes, :part] = dot_rows(c_ref[:, lanes], df_ref[...]).astype(BF)
        g_ref[lanes, part:] = dot_rows(dy_ref[:, lanes], u_ref[...]).astype(BF)
        return carry

    lax.fori_loop(0, 3, weight, 0)


def forward_grads(scal, normed, active, grad_pre, dy_all, kept):
    width = normed.shape[1]
    part = active.shape[1]
    outputs = shaped((width, 2 * part), BF)
    inputs = (scal, normed, active, grad_pre, dy_all, *kept)
    return run(
        forward_grads_kernel,
        "forward_grads",
        outputs,
        inputs,
        4.0,
        save=(2, *range(5, len(inputs))),
    )


def branch_kernel(scal, u_ref, w_ref, dy_ref, keep_ref, send_ref, own_ref):
    own_ref[...] = dy_ref[...]
    part = u_ref.shape[1]
    block = u_ref.shape[0] // GROUPS

    def branch(i, carry):
        rows = pl.ds(pl.multiple_of(i * block, block), block)
        split_store(scal[0], i, dot_cols(u_ref[rows, :], w_ref[:, part:]), keep_ref, send_ref)
        return carry

    lax.fori_loop(0, GROUPS, branch, 0)


def branch_part(scal, active, weights, cotangent):
    rows = active.shape[0] // GROUPS
    width = weights.shape[0]
    return run(
        branch_kernel,
        "branch_part",
        (
            shaped((2 * rows, width), F32),
            shaped((2 * rows, width), BF),
            shaped(cotangent.shape, BF),
        ),
        (scal, active, weights, cotangent),
        3.0,
        lazy=(1, 2, 3),
        far=(0,),
    )


def merge_kernel(scal, keep_ref, got_ref, mine_ref, send_ref):
    rows = mine_ref.shape[0]
    mine = pl.ds(pl.multiple_of((scal[0] // 2) * rows, rows), rows)
    other = pl.ds(pl.multiple_of((1 - scal[0] // 2) * rows, rows), rows)
    mine_ref[...] = keep_ref[mine, :] + got_ref[mine, :].astype(F32)
    send_ref[...] = (keep_ref[other, :] + got_ref[other, :].astype(F32)).astype(BF)


def merge(scal, keep, got, lazy=()):
    rows, width = keep.shape
    outputs = (shaped((rows // 2, width), F32), shaped((rows // 2, width), BF))
    return run(merge_kernel, "merge", outputs, (scal, keep, got), 0.7, mebibytes=8, lazy=lazy)


def resid_kernel(scal, mine_ref, got_ref, h_ref, dy_ref, vec_ref, dh_ref, dp_ref, sums_ref):
    grad = mine_ref[...] + got_ref[...].astype(F32)
    hat, inverse = normalize(h_ref[...])
    dy = dy_ref[...].astype(F32)
    grad_resid = dy + norm_back(hat, inverse, vec_ref[5:6, :], grad)
    dh_ref[...] = grad_resid
    low = grad_resid.astype(BF)
    dp_ref[...] = low
    sums_ref[...] = jnp.zeros_like(sums_ref)
    sums_ref[0:1, :] = jnp.sum(low.astype(F32), axis=0, keepdims=True)
    sums_ref[1:2, :] = jnp.sum(dy, axis=0, keepdims=True)


def resid_back(scal, mine, got, resid, cotangent, vec):
    rows, width = mine.shape
    outputs = (shaped((rows, width), F32), shaped((rows, width), BF), shaped((8, width), F32))
    return run(resid_kernel, "resid_back", outputs, (scal, mine, got, resid, cotangent, vec), 0.8)


def mixed_kernel(cols, scal, *refs, ready):
    grads, (o_ref, rows_ref, do_ref, g_ref, all_ref, own_ref) = refs[0:4], refs[4:10]
    place_members(scal, grads, all_ref)
    do_ref[...] = dot_cols(all_ref[...], rows_ref[...]).astype(BF)
    for index in range(GROUPS):

        @pl.when(scal[0] == index)
        def _():
            own_ref[...] = all_ref[:, index * cols : (index + 1) * cols]

    ready(5)
    g_ref[...] = dot_rows(o_ref[...], own_ref[...]).astype(BF)


def mixed_back(scal, grads, mixed, w_rows):
    cols, width = w_rows.shape
    length = mixed.shape[0]
    return run(
        functools.partial(mixed_kernel, cols),
        "mixed_back",
        (shaped((length, cols), BF), shaped((width, cols), BF)),
        (scal, *grads, mixed, w_rows),
        2.5,
        [pltpu.VMEM((length, width), BF), pltpu.VMEM((length, cols), BF)],
        lazy=(5, 6),
        late=(5,),
    )


def attend_back_kernel(
    per, scal, ranges, q_ref, k_ref, v_ref, do_ref, seg_row_ref, seg_col_ref, *refs, ready
):
    out_ref, k_acc, v_acc = refs[-3:]
    cols = q_ref.shape[1]
    block = 256
    length = k_ref.shape[0]
    k_acc[...] = jnp.zeros_like(k_acc)
    v_acc[...] = jnp.zeros_like(v_acc)
    for position in (2, 3, 4, 7):
        ready(position)

    def step(i, carry):
        start = pl.multiple_of(i * block, block)
        rows = pl.ds(start, block)

        def body(key_start, size):
            window = pl.ds(key_start, size)
            keys, values = k_ref[window, :], v_ref[window, :]
            same = seg_col_ref[window, :] == seg_row_ref[:, rows]
            queries = q_ref[rows, :] * jnp.asarray(HEAD_DIM**-0.5, BF)
            grads = do_ref[rows, :]

            def one(head, carry):
                grad_query, grad_key, grad_value = carry
                lanes = head_lanes(head, queries.shape)
                query = jnp.where(lanes, queries, jnp.zeros_like(queries))
                grad = jnp.where(lanes, grads, jnp.zeros_like(grads))
                score = jnp.where(same, dot_cols(keys, query), masked_score)
                largest = jnp.max(score, axis=0, keepdims=True)
                power = jnp.exp(score - largest)
                total = jnp.sum(power, axis=0, keepdims=True)
                chance = power * (1.0 / total)
                grad_chance = dot_cols(values, grad)
                inner = jnp.sum(chance * grad_chance, axis=0, keepdims=True)
                grad_score = (chance * (grad_chance - inner)).astype(BF)
                return (
                    jnp.where(lanes, dot_rows(grad_score, keys), grad_query),
                    grad_key + dot(grad_score, query),
                    grad_value + dot(chance.astype(BF), grad),
                )

            zeros = jnp.zeros(keys.shape, F32)
            grad_query, grad_key, grad_value = each_head(
                per, size, one, (jnp.zeros(queries.shape, F32), zeros, zeros)
            )
            k_acc[window, :] += grad_key
            v_acc[window, :] += grad_value
            out_ref[rows, :cols] = (grad_query * HEAD_DIM**-0.5).astype(BF)

        each_window(ranges, i, length, body)
        return carry

    lax.fori_loop(0, q_ref.shape[0] // block, step, 0)
    out_ref[:, cols : 2 * cols] = k_acc[...].astype(BF)
    out_ref[:, 2 * cols :] = v_acc[...].astype(BF)


def attend_back(scal, ranges, queries, keys, values, grad_out, seg_row, seg_col, per, kept):
    length, cols = queries.shape
    wide = pltpu.VMEM(queries.shape, F32)
    inputs = (scal, ranges, queries, keys, values, grad_out, seg_row, seg_col, *kept)
    return run(
        functools.partial(attend_back_kernel, per),
        "attend_back",
        shaped((length, 3 * cols), BF),
        inputs,
        16.0,
        [wide, wide],
        lazy=(2, 3, 4, 7),
        late=(2, 3, 4, 7),
        save=range(8, len(inputs)),
        scalars=2,
    )


def table_kernel(scal, forward_ref, resid_ref, table_ref, rows_ref):
    rows_ref[...] = jnp.zeros_like(rows_ref)
    rows_ref[4:5, :] = resid_ref[0:1, :]
    rows_ref[5:7, :] = forward_ref[0:2, :]
    rows_ref[7:8, :] = resid_ref[1:2, :]
    rows_ref[pl.ds(8 + scal[0], 1), :] = forward_ref[2:3, :]
    rest = rows_ref[...]
    unit = unit_rows(16, 128)
    table = jnp.zeros(table_ref.shape, F32)
    for _ in range(3):
        high = rest.astype(BF)
        rest = rest - high.astype(F32)
        table += dot_rows(high, unit)
    table_ref[...] = table


def vector_table(scal, sums_forward, sums_resid):
    width = sums_resid.shape[1]
    return run(
        table_kernel,
        "vector_table",
        shaped((width, 128), F32),
        (scal, sums_forward, sums_resid),
        1.0,
        [pltpu.VMEM((16, width), F32)],
        mebibytes=8,
        lazy=(1,),
    )


TERMS = 8


def vector_places(count, rows, width):
    each = width // rows
    return [(i // each, (i % each) * rows) for i in range(2 * count)]


def query_grads_kernel(cols, count, ringed, scal, *refs, ready):
    a_ref, hat_ref, out_ref, grad_ref, w_ref, table_ref, g_ref = refs
    width = a_ref.shape[1]
    owners = len(RING)
    rows = width // owners
    block = 4 * rows if ringed else 256
    ready(1)

    def place(first):
        if not ringed:
            return slice(first, first + block)
        owner = first // rows
        return slice(first + TERMS * owner, first + TERMS * owner + rows)

    for first in range(0, width, block):
        total = dot_rows(a_ref[:, first : first + block], grad_ref[...]).astype(BF)
        if not ringed:
            g_ref[place(first), : 3 * cols] = total
        else:
            for i in range(4):
                g_ref[place(first + i * rows), : 3 * cols] = total[i * rows : (i + 1) * rows, :]
    row = lax.broadcasted_iota(jnp.int32, (8, 3 * cols), 0)
    rest = dot_rows(jnp.ones((a_ref.shape[0], 8), BF), grad_ref[...])
    terms = jnp.zeros((8, 3 * cols), F32)
    for term in range(3):
        high = rest.astype(BF).astype(F32)
        terms = jnp.where(row == term, high, terms)
        rest = rest - high
    terms = terms.astype(BF)
    for position in (2, 3, 5, 6):
        ready(position)
    chunk = 256
    lane = lax.broadcasted_iota(jnp.int32, (chunk, 128), 1)

    def vectors(i, carry):
        lanes = pl.ds(pl.multiple_of(i * chunk, chunk), chunk)
        weight = w_ref[lanes, :]
        product = dot_rows(hat_ref[:, lanes], grad_ref[...]) * weight.astype(F32)
        gain = jnp.sum(product, axis=1, keepdims=True)
        shift = jnp.sum(dot_cols(weight, terms), axis=1, keepdims=True)
        table = jnp.where(lane == 0, gain, table_ref[lanes, :])
        table_ref[lanes, :] = jnp.where(lane == 1, shift, table)
        return carry

    lax.fori_loop(0, width // chunk, vectors, 0)
    own = pl.ds(pl.multiple_of(scal[0] * cols, cols), cols)
    bias = table_ref[own, :]
    near = lax.broadcasted_iota(jnp.int32, (cols, 128), 1)
    ones = jnp.ones((8, 8), BF)
    for i, column in ((0, 2), (2, 3)):
        part = dot_rows(terms[:, i * cols : (i + 1) * cols], ones)
        bias = jnp.where(near == column, part[:, 0:1], bias)
    table_ref[own, :] = bias
    total = table_ref[...]
    high = total.astype(BF)
    low = (total - high.astype(F32)).astype(BF)
    if not ringed:
        g_ref[:, 3 * cols : 4 * cols] = out_ref[...]
        g_ref[:, 4 * cols : 4 * cols + 16] = high[:, 0:16]
        g_ref[:, 4 * cols + 16 : 4 * cols + 32] = low[:, 0:16]
        g_ref[:, 4 * cols + 32 :] = jnp.zeros((width, 96), BF)
        return
    unit = unit_rows(16, 128)
    lines = (dot_cols(unit, high), dot_cols(unit, low))
    places = vector_places(count, rows, width)
    for owner in range(owners):
        first = owner * rows
        g_ref[place(first), 3 * cols :] = out_ref[first : first + rows, :]
        base = first + TERMS * owner + rows
        g_ref[base : base + TERMS, :] = jnp.zeros((TERMS, width), BF)
        for i, (line, start) in enumerate(places):
            piece = lines[i // count][i % count : i % count + 1, first : first + rows]
            g_ref[base + line : base + line + 1, start : start + rows] = piece.astype(BF)


def query_grads(scal, normed, hat, grad_out, grad, weights, table, count, ringed):
    width, cols = grad_out.shape
    shape = (width, 4 * cols + 128)
    if ringed:
        shape = (width + TERMS * len(RING), 4 * cols)
    return run(
        functools.partial(query_grads_kernel, cols, count, ringed),
        "query_grads",
        shaped(shape, BF),
        (scal, normed, hat, grad_out, grad, weights, table),
        4.0,
        lazy=(1, 2, 3, 5, 6),
        late=(1, 2, 3, 5, 6),
        far=(0,),
    )


def project_back_kernel(scal, grad_ref, w_ref, keep_ref, send_ref):
    block = grad_ref.shape[0] // GROUPS

    def step(i, carry):
        rows = pl.ds(pl.multiple_of(i * block, block), block)
        split_store(scal[0], i, dot_cols(grad_ref[rows, :], w_ref[...]), keep_ref, send_ref)
        return carry

    lax.fori_loop(0, GROUPS, step, 0)


def project_back(scal, grad, weights):
    rows, width = grad.shape[0] // 2, weights.shape[0]
    return run(
        project_back_kernel,
        "project_back",
        (shaped((rows, width), F32), shaped((rows, width), BF)),
        (scal, grad, weights),
        3.0,
        lazy=(2,),
    )


def input_kernel(scal, mine_ref, got_ref, x_ref, dh_ref, vec_ref, out_ref):
    grad = mine_ref[...] + got_ref[...].astype(F32)
    hat, inverse = normalize(x_ref[...].astype(F32))
    out_ref[...] = dh_ref[...] + norm_back(hat, inverse, vec_ref[0:1, :], grad)


def input_back(scal, mine, got, tokens, grad_resid, vec):
    inputs = (scal, mine, got, tokens, grad_resid, vec)
    return run(input_kernel, "input_back", shaped(mine.shape, F32), inputs, 1.0, lazy=(2, 3, 4, 5))


def output_kernel(scal, mine_ref, got_ref, h_ref, vec_ref, out_ref):
    branch = mine_ref[...] + got_ref[...].astype(F32) + vec_ref[7:8, :]
    out_ref[...] = (h_ref[...] + branch).astype(BF)


def output_sum(scal, mine, got, resid, vec):
    inputs = (scal, mine, got, resid, vec)
    return run(output_kernel, "output_sum", shaped(mine.shape, BF), inputs, 0.8, lazy=(2, 3, 4))


def owned_kernel(scal, in_ref, low_ref):
    total = in_ref[0].astype(F32)
    for i in range(1, in_ref.shape[0]):
        total += in_ref[i].astype(F32)
    low_ref[...] = total.astype(BF)


def owned_sum(scal, pieces):
    outputs = shaped(pieces.shape[1:], BF)
    return run(owned_kernel, "owned_sum", outputs, (scal, pieces), 1.5, lazy=(1,))


def squares_kernel(scal, *refs):
    sums = []
    for piece in refs[:4]:
        wide = piece[...].astype(F32)
        sums.append(jnp.sum(wide * wide))
    total = (sums[0] + sums[1]) + (sums[2] + sums[3])
    refs[4][...] = jnp.full(refs[4].shape, total, F32)


def squares_of(scal, pieces):
    outputs = shaped((8, 128), F32)
    return run(squares_kernel, "squares_of", outputs, (scal, *pieces), 1.0, save=range(1, 5))


def owned_vector_kernel(cols, ringed, scal, in_ref, low_ref):
    total = in_ref[0].astype(F32)
    for i in range(1, in_ref.shape[0]):
        total += in_ref[i].astype(F32)
    if ringed:
        rows = total.shape[0] - TERMS
        low_ref[:rows, :] = total[:rows, :].astype(BF)
        vector = total[rows:, :]
        high = vector.astype(BF).astype(F32)
        line = lax.broadcasted_iota(jnp.int32, vector.shape, 0)
        rest = pltpu.roll(vector - high, 3, 0)
        low_ref[rows:, :] = jnp.where(line < 3, high, rest).astype(BF)
        return
    low_ref[:, : 4 * cols] = total[:, : 4 * cols].astype(BF)
    vector = total[:, 4 * cols :]
    high = vector.astype(BF).astype(F32)
    lane = lax.broadcasted_iota(jnp.int32, vector.shape, 1)
    rest = pltpu.roll(vector - high, 32, 1)
    low_ref[:, 4 * cols :] = jnp.where(lane < 32, high, rest).astype(BF)


def owned_vector(scal, pieces, cols, ringed):
    return run(
        functools.partial(owned_vector_kernel, cols, ringed),
        "owned_vector",
        shaped(pieces.shape[1:], BF),
        (scal, pieces),
        1.5,
    )


def vector_sum(pieces, cols, count, ringed, held):
    if ringed:
        rows, width = pieces[0].shape
        rows -= TERMS
        parts = [piece[rows:, :].astype(F32) for piece in pieces]
        lines = (parts[0] + parts[1]) + (parts[2] + parts[3])
        lines = lines + pltpu.roll(lines, TERMS - 3, 0)
        places = vector_places(count, rows, width)
        for i in range(count):
            total = jnp.zeros((1, rows), F32)
            for line, start in (places[i], places[i + count]):
                total += lines[line : line + 1, start : start + rows]
            held[i : i + 1, :] = total
        return held[...]
    parts = [piece[:, 4 * cols :].astype(F32) for piece in pieces]
    table = (parts[0] + parts[1]) + (parts[2] + parts[3])
    rows = lax.broadcasted_iota(jnp.int32, (16, 128), 0)
    lanes = lax.broadcasted_iota(jnp.int32, (16, 128), 1)
    unit = jnp.where((lanes % 16 == rows) & (lanes < 64), 1.0, 0.0)
    return lax.dot_general(
        unit,
        table,
        (((1,), (1,)), ((), ())),
        preferred_element_type=F32,
        precision=lax.Precision.HIGHEST,
    )[:count]


def join_kernel(cols, count, ringed, scal, *refs):
    pieces, forward_ref, squares_ref, held = refs[0:4], refs[4], refs[5], refs[6]
    rows = held.shape[1]
    sums = []
    for piece in pieces:
        wide = piece[:rows, : 4 * cols].astype(F32)
        sums.append(wide * wide)
    vector = vector_sum(pieces, cols, count, ringed, held)
    total = jnp.sum((sums[0] + sums[1]) + (sums[2] + sums[3])) + jnp.sum(vector * vector)
    total = forward_ref[...] + total
    for i in range(squares_ref.shape[0] // 8):
        squares_ref[8 * i : 8 * i + 8, :] = total


def join(scal, pieces, squares, shape, cols, owners, ringed):
    return run(
        functools.partial(join_kernel, cols, shape[0], ringed),
        "join",
        shaped((8 * owners, 128), F32),
        (scal, *pieces, squares),
        1.5,
        [pltpu.VMEM(shape, F32)],
    )


def clip_factor(total_ref):
    total = total_ref[0]
    for i in range(1, total_ref.shape[0]):
        total += total_ref[i]
    norm = jnp.sqrt(total[0:1, 0:1])
    return norm, jnp.minimum(1.0, clip_limit / (norm + 1e-06))


def adam_kernel(counts, cols, ringed, scal, total_ref, *refs):
    attention, refs = refs[0:4], refs[4:]
    pieces, sources, targets, norm_ref = refs[0:4], refs[4:16], refs[16:31], refs[31]
    held, copies = refs[32:44], refs[44:47]
    loads, stores = refs[47:50], refs[50:53]
    grads, grad_loads, attention_ref, vector_ref = refs[53:57], refs[57], refs[58], refs[59]
    norm, factor = clip_factor(total_ref)
    norm_ref[...] = jnp.broadcast_to(norm, norm_ref.shape)
    decays = (weight_decay, weight_decay, 0.0)

    def chunk(kind, i):
        if counts[kind] == 1:
            return (slice(None), slice(None))
        size = held[4 * kind].shape[1] // counts[kind]
        return (slice(None), pl.ds(pl.multiple_of(i * size, size), size))

    def load(kind, i, state):
        place = chunk(kind, i)
        number = 4 * kind + state
        return pltpu.make_async_copy(
            sources[number].at[place], held[number].at[place], loads[kind].at[i, state]
        )

    def store(kind, i, state):
        place = chunk(kind, i)
        source = held[4 * kind + state] if state < 4 else copies[kind]
        return pltpu.make_async_copy(
            source.at[place], targets[3 * state + kind].at[place], stores[kind].at[i, state]
        )

    def every(kind, action):
        def step(i, carry):
            action(kind, i)
            return carry

        lax.fori_loop(0, counts[kind], step, 0)

    def start(kind, i):
        for state in range(4):
            load(kind, i, state).start()

    def work(kind, i):
        for state in range(4):
            load(kind, i, state).wait()
        place = chunk(kind, i)
        if kind == 0:
            gradient = attention_ref[place].astype(F32)
        elif kind == 2:
            gradient = vector_sum(attention, cols, held[8].shape[0], ringed, vector_ref)
        else:
            size = held[4].shape[1] // counts[1]
            half = pl.ds(pl.multiple_of((i // GROUPS) * size, size), size)
            source = scal[0] ^ (i % GROUPS)
            gradient = grads[0][:, half]
            for k in range(1, GROUPS):
                gradient = jnp.where(source == k, grads[k][:, half], gradient)
            gradient = gradient.astype(F32)
        results = adam_update(
            *[held[4 * kind + state][place] for state in range(4)], gradient, factor, decays[kind]
        )
        for state, value in zip((0, 1, 2, 3), results):
            held[4 * kind + state][place] = value
        copies[kind][place] = results[0].astype(BF)
        for state in range(5):
            store(kind, i, state).start()

    def finish(kind, i):
        for state in range(5):
            store(kind, i, state).wait()

    moves = [
        pltpu.make_async_copy(piece, grad, grad_loads.at[i])
        for i, (piece, grad) in enumerate(zip(pieces, grads))
    ]
    for move in moves:
        move.start()
    for kind in (1, 0, 2):
        every(kind, start)
    width = attention_ref.shape[1] // 4
    for member in range(GROUPS):

        @pl.when(scal[0] == member)
        def _():
            for i in range(4):
                for k in range(GROUPS):
                    first = i * width + (member ^ k) * cols
                    attention_ref[:, first : first + cols] = attention[k][
                        : held[0].shape[0], i * cols : (i + 1) * cols
                    ]

    for move in moves:
        move.wait()
    for kind in (1, 0, 2):
        every(kind, work)
    for kind in (1, 0, 2):
        every(kind, finish)


def adam(scal, totals, attention_grads, forward_grads_by_member, states, cols, ringed):
    counts = (8, 2 * GROUPS, 1)
    kinds = [states[4 * kind].shape for kind in range(3)]
    out_shape = [pltpu.HBM(shape, F32) for _ in range(4) for shape in kinds]
    out_shape += [pltpu.HBM(shape, BF) for shape in kinds]
    out_shape += [shaped((8, 128), F32)]
    return pl.pallas_call(
        functools.partial(adam_kernel, counts, cols, ringed),
        out_shape=out_shape,
        in_specs=[smem()] + [vmem()] * 5 + [far_space()] * 16,
        out_specs=[far_space()] * 15 + [vmem()],
        scratch_shapes=[pltpu.VMEM(kinds[kind], F32) for kind in range(3) for _ in range(4)]
        + [pltpu.VMEM(shape, BF) for shape in kinds]
        + [pltpu.SemaphoreType.DMA((count, 4)) for count in counts]
        + [pltpu.SemaphoreType.DMA((count, 5)) for count in counts]
        + [pltpu.VMEM(item.shape, item.dtype) for item in forward_grads_by_member]
        + [pltpu.SemaphoreType.DMA((GROUPS,))]
        + [pltpu.VMEM(kinds[0], BF), pltpu.VMEM(kinds[2], F32)],
        compiler_params=params(32),
        cost_estimate=cost(9.0),
        name="adam",
    )(scal, totals, *attention_grads, *map(pin, forward_grads_by_member), *map(pin, states))


def adam_update(master, moment, second, teacher, gradient, factor, decay_rate):
    clipped = gradient * factor
    moment_new = beta_one * moment + (1.0 - beta_one) * clipped
    second_new = beta_two * second + (1.0 - beta_two) * clipped * clipped
    scale_one = 1.0 - beta_one**ADAM_STEP
    scale_two = 1.0 - beta_two**ADAM_STEP
    update = (moment_new * (1.0 / scale_one)) / (
        jnp.sqrt(second_new * (1.0 / scale_two)) + adam_epsilon
    )
    master_new = master * (1.0 - learn_rate * decay_rate) - learn_rate * update
    teacher_new = teacher_keep * teacher + (1.0 - teacher_keep) * master_new
    return (master_new, moment_new, second_new, teacher_new)


def swap(part, bit):
    return lax.ppermute(part, "head", [(i, i ^ bit) for i in range(4)])


def spread(part, *others):
    across = swap(part, 2)
    if others:
        return [
            part,
            swap(after(part, *others), 1),
            across,
            swap(after(across, *others), 1),
        ]
    return [part, swap(part, 1), across, swap(across, 1)]


RING = (0, 2, 4, 6, 7, 5, 3, 1)


def ring_owners(count):
    if count != len(RING):
        return np.zeros((count, 1), np.int32)
    table = []
    for device in range(count):
        place = RING.index(device)
        owners = [device]
        for hop in range(1, count // 2 + 1):
            owners.append(RING[(place - hop) % count])
            owners.append(RING[(place + hop) % count])
        table.append(owners)
    return np.asarray(table, np.int32)


def after(value, *others):
    return lax.optimization_barrier((value, *others))[0]


class Ring:
    def __init__(self, block, count, halved=False):
        self.count = count
        self.halved = halved
        self.ringed = count == len(RING)
        self.hops = count // 2 if self.ringed else 1
        self.front = self.rear = block
        self.pieces = [block]
        self.done = 0

    def send(self, array, distance):
        count = self.count
        pairs = [(RING[i], RING[(i + distance) % count]) for i in range(count)]
        return lax.ppermute(array, "dp", pairs)

    def hop(self, *others):
        self.done += 1
        if not self.ringed:
            self.pieces = [lax.all_gather(after(self.front, *others), "dp", axis=0, tiled=True)]
            return self
        if self.done > 1 or others:
            self.front, self.rear = lax.optimization_barrier((self.front, self.rear, *others))[:2]
        if self.done == self.hops and self.halved:
            half = self.front.shape[0] // 2
            self.front, self.rear = self.front[:half], self.rear[half:]
        self.front = self.send(self.front, 1)
        self.pieces.append(self.front)
        if self.done < self.hops or self.halved:
            self.rear = self.send(self.rear, -1)
            self.pieces.append(self.rear)
        return self

    def rest(self):
        while self.done < self.hops:
            self.hop()
        return self.pieces


def exchange_owned(grads, count):
    blocks = grads.reshape(count, -1, grads.shape[1])
    return lax.all_to_all(blocks, "dp", split_axis=0, concat_axis=0)


def local(
    tokens,
    cotangent,
    segments,
    attention_master,
    feedforward_master,
    vector_master,
    attention_moment,
    feedforward_moment,
    vector_moment,
    attention_second,
    feedforward_second,
    vector_second,
    attention_teacher,
    feedforward_teacher,
    vector_teacher,
):
    width = tokens.shape[1]
    owners = lax.axis_size("dp")
    groups = lax.axis_size("head")
    hidden = feedforward_master.shape[1] // 2
    per = HEADS // groups
    cols = per * HEAD_DIM
    part = hidden // groups

    owner_table = ring_owners(owners)
    table = np.concatenate(
        [
            np.tile(np.arange(groups, dtype=np.int32), owners)[:, None],
            np.repeat(owner_table, groups, axis=0),
        ],
        axis=1,
    )
    place = lax.axis_index("dp") * groups + lax.axis_index("head")
    scal = lax.dynamic_index_in_dim(jnp.asarray(table), place, 0, keepdims=False)
    first = Ring(pack_attention(scal, attention_master, vector_master, cols), owners)
    ringed = owners == len(RING)
    first.hop()
    if ringed:
        first.hop()
    seg_col, ranges = read_segments(scal, after(segments, *first.pieces[-2:]))
    if ringed:
        first.hop().hop(seg_col)
    early = first.pieces[-3:-1] if ringed else first.pieces
    token_across, grad_across = swap(tokens, 2), swap(cotangent, 2)
    token, token_across = lax.optimization_barrier((tokens, token_across, *early))[:2]
    x_all = place_blocks(scal, [token, swap(token, 1), token_across, swap(token_across, 1)])
    second = Ring(pack_forward(scal, feedforward_master, part), owners)
    second.hop(first.pieces[-1])

    queries, keys, values, w_qkv, w_o, vec, normed, hat = project(
        scal, x_all, first.pieces, cols
    )
    half = x_all.shape[0] // 2
    w_across = swap(w_o, 2)
    mixed_low, *kept = attend(
        scal,
        ranges,
        after(queries, grad_across),
        keys,
        values,
        segments,
        seg_col,
        per,
        0,
        half,
        (w_qkv, vec, normed, hat),
    )
    far_q, far_k, far_v, far_col, far_weights, far_vec, *far_normed = kept
    low_across = swap(mixed_low, 2)
    w_across = after(w_across, mixed_low)
    if ringed:
        second.hop(mixed_low)
    mixed_high = attend(
        scal, ranges, after(queries, w_across), keys, values, segments, seg_col, per, half, half
    )
    if ringed:
        second.hop(mixed_high)
    high_across = swap(mixed_high, 2)
    w_across, low_across, w_o, mixed_low, grad, grad_across = lax.optimization_barrier(
        (w_across, low_across, w_o, mixed_low, cotangent, grad_across, high_across)
    )[:6]
    dy_all = place_blocks(scal, [grad, swap(grad, 1), grad_across, swap(grad_across, 1)])
    w_out = [w_o, swap(w_o, 1), w_across, swap(w_across, 1)]
    mixed = [
        (mixed_low, mixed_high),
        (swap(mixed_low, 1), swap(mixed_high, 1)),
        (low_across, high_across),
        (swap(low_across, 1), swap(high_across, 1)),
    ]
    (
        normed_two,
        active,
        grad_pre,
        keep,
        send,
        resid,
        w_ff,
        w_rows,
        sums_forward,
        mixed_all,
    ) = forward_back(scal, x_all, dy_all, mixed, w_out, second.rest(), vec, cols)
    grad_ff, far_active, *kept = forward_grads(
        scal,
        normed_two,
        active,
        grad_pre,
        dy_all,
        (resid, sums_forward, w_rows, w_ff, mixed_all),
    )
    far_resid, far_sums, far_rows, far_ff, far_mixed = kept
    got = swap(send, 1)
    grad_ff, got = lax.optimization_barrier((grad_ff, got))
    owned_ff = exchange_owned(grad_ff, owners)
    mine, send = merge(scal, keep, got)
    keep_branch, send_branch, cot_own = branch_part(
        scal, far_active, after(far_ff, send), cotangent
    )
    got = swap(send, 2)
    grad_resid, grad_low, sums_resid = resid_back(
        scal, after(mine, send_branch), got, resid, cot_own, vec
    )
    low_across = swap(grad_low, 2)
    mine, send = merge(
        scal, keep_branch, swap(after(send_branch, grad_low), 1), lazy=(1,)
    )
    table = vector_table(scal, far_sums, sums_resid)
    low_across = after(low_across, send, table)
    low_blocks = [grad_low, swap(grad_low, 1), low_across, swap(low_across, 1)]
    grad_mixed, grad_out = mixed_back(scal, low_blocks, far_mixed, far_rows)
    grad_qkv, far_dh, far_table, far_grad_out = attend_back(
        scal,
        ranges,
        far_q,
        far_k,
        far_v,
        grad_mixed,
        segments,
        far_col,
        per,
        (grad_resid, table, grad_out),
    )
    got_branch = swap(after(send, grad_mixed), 2)
    pack = query_grads(
        scal,
        after(far_normed[0], got_branch),
        far_normed[1],
        far_grad_out,
        grad_qkv,
        far_weights,
        far_table,
        vector_master.shape[0],
        ringed,
    )
    owned_pack = exchange_owned(pack, owners)
    forward_parts = spread(owned_sum(scal, after(owned_ff, pack)))
    forward_squares, *forward_parts = squares_of(scal, forward_parts)
    keep, send = project_back(scal, grad_qkv, after(far_weights, pack))
    mine_input, send = merge(scal, keep, swap(send, 1))
    block_output = output_sum(scal, after(mine, pack), got_branch, far_resid, far_vec)
    got_input = swap(send, 2)
    owned_pack = after(owned_pack, forward_squares, got_input, block_output)
    input_gradient = input_back(scal, mine_input, got_input, tokens, far_dh, far_vec)
    attention_parts = spread(owned_vector(scal, owned_pack, cols, ringed))
    squares = join(
        scal, attention_parts, forward_squares, vector_master.shape, cols, owners, ringed
    )
    totals = lax.all_to_all(
        squares.reshape(owners, 8, 128), "dp", split_axis=0, concat_axis=0
    )
    *results, norm = adam(
        scal,
        totals,
        attention_parts,
        forward_parts,
        (
            attention_master,
            attention_moment,
            attention_second,
            attention_teacher,
            feedforward_master,
            feedforward_moment,
            feedforward_second,
            feedforward_teacher,
            vector_master,
            vector_moment,
            vector_second,
            vector_teacher,
        ),
        cols,
        ringed,
    )
    return (block_output, input_gradient, norm[0, 0], *results)


def solution(mesh):
    rows = P(("dp", "head"), None)
    shard = P("dp", None)
    vector = P(None, "dp")
    return jax.shard_map(
        local,
        mesh=mesh,
        in_specs=(rows, rows, shard) + (shard, shard, vector) * 4,
        out_specs=(rows, rows, P()) + (shard, shard, vector) * 5,
        check_vma=False,
    )
```
